32 devices in a mesh: dp: 4 (over y, x), ctx: 8 (over z, core).
Axes of the slice: x: 2, y: 2, z: 4, core: 2. Of those that a mesh axis runs over, the one named last changes fastest.
Arguments:
- hidden_in: bfloat16 [4, 2048, 2048], P('dp', 'ctx'), may hold values from -12.5 to 12.5
- seq_lengths: int32 [4, 8], replicated, may hold values from 0 to 1024, as said below
- qkv_weight: bfloat16 [2048, 6144], P(('dp', 'ctx')), may hold values from -0.125 to 0.125
- out_weight: bfloat16 [2048, 2048], P(('dp', 'ctx')), may hold values from -0.125 to 0.125
- in_weight: bfloat16 [2048, 16384], P(('dp', 'ctx')), may hold values from -0.125 to 0.125
- down_weight: bfloat16 [8192, 2048], P(('dp', 'ctx')), may hold values from -0.0625 to 0.0625
- norm_gains: float32 [4, 2048], replicated, may hold values from 0.25 to 1.75
- upstream: bfloat16 [4, 2048, 2048], P('dp', 'ctx'), may hold values from -6 to 6
Outputs:
- output: bfloat16 [4, 2048, 2048], P('dp', 'ctx')
- input_grad: float32 [4, 2048, 2048], P('dp', 'ctx')
- grad_qkv: float32 [2048, 6144], P(('dp', 'ctx'))
- grad_out: float32 [2048, 2048], P(('dp', 'ctx'))
- grad_in: float32 [2048, 16384], P(('dp', 'ctx'))
- grad_down: float32 [8192, 2048], P(('dp', 'ctx'))
- grad_gains: float32 [4, 2048], replicated
- rms_values: float32 [3], replicated
The draws below stay inside these ranges and needn't reach their ends.
Inputs may be any that keep to these rules, and one draw needn't show every extreme that they name: `seq_lengths`: each row lists the lengths of its packed sequences in order, each from 256 to 1024, then zeros; a row's lengths add up to at most 2048 and the positions after them are padding. Every row holds at least one sequence, and some row of every draw holds one of exactly 1024.
All inputs are finite; a program needn't handle non-finite values.
Results may differ from the reference program's by a relative error of at most 0.015.
Values may be sent and summed in bfloat16 or wider, within the bound.
No kernel may reach another device: no remote copies, remote signals or barrier semaphores. Data moves between devices by JAX's collectives and lax.ppermute only.
A program may use at most 512 MiB of HBM per device.

```python
import jax
import jax.numpy as jnp
from jax import lax

D = 2048
HEADS = 16
HEAD_DIM = 128
FF = 8192
ROWS = 4
ROW = 2048
SEQ_MIN = 256
SEQ_MAX = 1024
SLOTS = 8


def draw_hidden_in(key, part):
    position = jnp.arange(ROW, dtype=jnp.float32) / max(ROW - 1, 1)
    row_place = jnp.arange(ROWS, dtype=jnp.float32) / max(ROWS - 1, 1)
    samples = jnp.clip(jax.random.normal(key, (ROWS, ROW, D), jnp.float32), -5.0, 5.0)
    ramp_scale = (0.5 + 1.5 * position)[None, :, None] * (0.75 + 0.5 * row_place)[:, None, None]
    return (samples * ramp_scale).astype(jnp.bfloat16)


def draw_seq_lengths(key, part):
    key_lengths = jax.random.fold_in(key, 11)
    key_choice = jax.random.fold_in(key, 13)
    seq_spans = jax.random.randint(key_lengths, (ROWS, SLOTS), SEQ_MIN, SEQ_MAX + 1, dtype=jnp.int32)
    chosen = jax.random.randint(key_choice, (), 0, ROWS, dtype=jnp.int32)
    forced = (jnp.arange(ROWS, dtype=jnp.int32) == chosen)[:, None] & (jnp.arange(SLOTS, dtype=jnp.int32) == 0)[None, :]
    seq_spans = jnp.where(forced, SEQ_MAX, seq_spans)
    finish = jnp.cumsum(seq_spans, axis=1)
    return jnp.where(finish <= ROW, seq_spans, 0).astype(jnp.int32)


def block_scale(rng, dims, split, low, high):
    def one(dim, shards_of):
        heights = jax.random.uniform(jax.random.fold_in(jax.random.fold_in(rng, 6), dim), (shards_of,), jnp.float32, low / len(split), high / len(split))
        return jnp.repeat(jnp.exp(heights), dims[dim] // shards_of).reshape((-1,) + (1,) * (len(dims) - dim - 1))

    level = one(*split[0])
    for cut in split[1:]:
        level = level * one(*cut)
    return level


def gaussian(stream_key, dims, deviation, bound, cuts=(), kind=jnp.bfloat16):
    values = deviation * jax.random.normal(stream_key, dims, jnp.float32)
    if cuts:
        values = values * block_scale(stream_key, dims, cuts, -0.22, 0.18)
    return jnp.clip(values, -bound, bound).astype(kind)


def setup_inputs(seed: int = 0) -> dict:
    splits = jax.random.split(jax.random.key(seed), 9)
    return {
        "hidden_in": draw_hidden_in(jax.random.fold_in(splits[8], 71), 0),
        "seq_lengths": draw_seq_lengths(jax.random.fold_in(splits[8], 71), 0),
        "qkv_weight": gaussian(splits[2], (D, 3 * D), D ** -0.5, 0.125, ((0, 32),)),
        "out_weight": gaussian(splits[3], (D, D), D ** -0.5, 0.125, ((0, 32),)),
        "in_weight": gaussian(splits[4], (D, 2 * FF), D ** -0.5, 0.125, ((0, 32),)),
        "down_weight": gaussian(splits[5], (FF, D), FF ** -0.5, 0.0625, ((0, 32),)),
        "norm_gains": jnp.clip(1.0 + 0.15 * jax.random.normal(splits[6], (4, D), jnp.float32), 0.25, 1.75),
        "upstream": gaussian(splits[7], (ROWS, ROW, D), 1.0, 6.0, ((0, 4), (1, 8))),
    }


norm_epsilon = 1e-06
rope_base = 500000.0
masked_score = -1e+30

@jax.custom_vjp
def low(v):
    return lax.optimization_barrier(v.astype(jnp.bfloat16)).astype(jnp.float32)

@jax.custom_vjp
def low_back(v):
    return v

def low_keep(v):
    return (low(v), None)

def low_pass(kept, grad):
    return (grad,)

def back_keep(v):
    return (v, None)

def back_low(kept, grad):
    return (low(grad),)
low.defvjp(low_keep, low_pass)
low_back.defvjp(back_keep, back_low)

def highest(left_side, right_side):
    return jnp.dot(left_side, right_side, precision=lax.Precision.HIGHEST, preferred_element_type=jnp.float32)

def rms_norm(values, gain_row):
    return values * lax.rsqrt(lax.optimization_barrier(jnp.mean(values * values, axis=-1, keepdims=True)) + norm_epsilon) * gain_row

def rotate(values, offsets):
    halfway = HEAD_DIM // 2
    inverse = rope_base ** (-2.0 * jnp.arange(halfway, dtype=jnp.float32) / HEAD_DIM)
    angles = offsets.astype(jnp.float32)[:, None] * inverse[None, :]
    cosine = jnp.cos(angles)[:, None, :]
    sine_part = jnp.sin(angles)[:, None, :]
    leading = values[..., :halfway]
    trailing = values[..., halfway:]
    return jnp.concatenate([leading * cosine - trailing * sine_part, trailing * cosine + leading * sine_part], axis=-1)

def arrange(lengths, positions):
    finish = jnp.cumsum(lengths).astype(jnp.int32)
    has_ended = finish[None, :] <= positions[:, None]
    segment = lax.optimization_barrier(jnp.sum(has_ended.astype(jnp.int32), axis=1)).astype(jnp.int32)
    starts = lax.optimization_barrier(jnp.sum(jnp.where(has_ended, lengths[None, :], 0), axis=1)).astype(jnp.int32)
    return (segment, positions - starts, positions < finish[-1])

def layer_row(row_in, qkv_weight, out_weight, in_weight, down_weight, gain_rows, segment, offsets, live_mask):
    length = row_in.shape[0]
    scale_factor = HEAD_DIM ** (-0.5)
    projected = low_back(highest(row_in, qkv_weight))
    queries = rotate(rms_norm(projected[:, :D], gain_rows[0]).reshape(length, HEADS, HEAD_DIM), offsets)
    key_rows = rotate(rms_norm(projected[:, D:2 * D], gain_rows[1]).reshape(length, HEADS, HEAD_DIM), offsets)
    queries = low(queries)
    key_rows = low(key_rows)
    values = low(projected[:, 2 * D:]).reshape(length, HEADS, HEAD_DIM)
    positions = jnp.arange(length, dtype=jnp.int32)
    block_rows = 512 if length % 512 == 0 else length

    def attend(block_start):
        query_block = lax.dynamic_slice_in_dim(queries, block_start, block_rows, 0)
        query_places = block_start + jnp.arange(block_rows, dtype=jnp.int32)
        query_segments = lax.dynamic_slice_in_dim(segment, block_start, block_rows, 0)
        scores = jnp.einsum('qhd,khd->hqk', query_block, key_rows, precision=lax.Precision.HIGHEST) * scale_factor
        scores = low_back(scores)
        allowed = (query_segments[:, None] == segment[None, :]) & (positions[None, :] <= query_places[:, None])
        scores = jnp.where(allowed[None], scores, masked_score)
        score_top = lax.optimization_barrier(jnp.max(scores, axis=-1, keepdims=True))
        expanded = jnp.exp(scores - score_top)
        weights = expanded / lax.optimization_barrier(jnp.sum(expanded, axis=-1, keepdims=True))
        return jnp.einsum('hqk,khd->qhd', low(weights), values, precision=lax.Precision.HIGHEST)
    block_starts = jnp.arange(length // block_rows, dtype=jnp.int32) * block_rows
    head_out = lax.map(jax.checkpoint(attend), block_starts).reshape(length, D)
    attended = low(low_back(head_out))
    branch = low_back(highest(attended, out_weight))
    residual = row_in + rms_norm(branch, gain_rows[2])
    gate_up = low_back(highest(low(residual), in_weight))
    hidden = low(jax.nn.silu(gate_up[:, :FF]) * gate_up[:, FF:])
    second = low_back(highest(hidden, down_weight))
    result = residual + rms_norm(second, gain_rows[3])
    counted = live_mask.astype(jnp.float32)[:, None]
    squares = jnp.stack([jnp.sum(result * result * counted), jnp.sum(branch * branch * counted), jnp.sum(second * second * counted)])
    return (result, squares)

def reference(hidden_in, seq_lengths, qkv_weight, out_weight, in_weight, down_weight, norm_gains, upstream):
    weights = (qkv_weight.astype(jnp.float32), out_weight.astype(jnp.float32), in_weight.astype(jnp.float32), down_weight.astype(jnp.float32))
    positions = jnp.arange(ROW, dtype=jnp.int32)

    def row_step(totals, row_data):
        row_in, lengths, row_grad = row_data
        segment, offsets, live_mask = arrange(lengths, positions)

        def forward(inputs, weight_set, gain_rows):
            return layer_row(inputs, weight_set[0], weight_set[1], weight_set[2], weight_set[3], gain_rows, segment, offsets, live_mask)
        result, pullback, squares = jax.vjp(forward, row_in.astype(jnp.float32), weights, norm_gains, has_aux=True)
        input_grad, weight_grads, gain_grads = pullback(row_grad.astype(jnp.float32))
        updated = (totals[0] + weight_grads[0], totals[1] + weight_grads[1], totals[2] + weight_grads[2], totals[3] + weight_grads[3], totals[4] + gain_grads, totals[5] + squares)
        return (updated, (result.astype(jnp.bfloat16), input_grad))
    zero_totals = tuple((jnp.zeros(matrix.shape, jnp.float32) for matrix in weights)) + (jnp.zeros((4, D), jnp.float32), jnp.zeros((3,), jnp.float32))
    totals, (output, input_grad) = lax.scan(row_step, zero_totals, (hidden_in, seq_lengths, upstream))
    live_count = jnp.sum(seq_lengths).astype(jnp.float32)
    rms_values = jnp.sqrt(totals[5] / (live_count * D))
    return (output, input_grad, totals[0], totals[1], totals[2], totals[3], totals[4], rms_values)
```

```python
import functools
import itertools

import jax
import jax.numpy as jnp
from jax import lax
from jax.experimental import pallas as pl
from jax.experimental.pallas import tpu as pltpu
from jax.sharding import Mesh
from jax.sharding import PartitionSpec as P

D = 2048
HEADS = 16
HEAD_DIM = 128
FF = 8192

norm_epsilon = 1e-06
rope_base = 500000.0
masked_score = -1e30
scale_factor = HEAD_DIM ** (-0.5)

AXES = ("dh", "dl", "zh", "zl", "c")
DATA = ("dh", "dl")
LINE = ("zh", "zl")
CTX = ("zh", "zl", "c")
MLP_CHIPS = ("zh", "zl")
MLP_DATA = tuple(a for a in AXES[:4] if a not in MLP_CHIPS)

BLOCK_Q = 512
BLOCK_K = 512

bf16 = jnp.bfloat16
f32 = jnp.float32


def sizes_of(axes):
    return tuple(lax.axis_size(a) for a in axes)


def offsets(axes):
    return list(itertools.product(*[range(n) for n in sizes_of(axes)]))


def linear(index, sizes):
    total = 0
    for i, n in zip(index, sizes):
        total = total * n + i
    return total


def shift(value, axes, steps):
    if not any(steps):
        return value
    sizes = sizes_of(axes)
    pairs = []
    for index in itertools.product(*[range(n) for n in sizes]):
        target = tuple((i + s) % n for i, s, n in zip(index, steps, sizes))
        pairs.append((linear(index, sizes), linear(target, sizes)))
    return lax.ppermute(value, axes, pairs)


def swap(value):
    return lax.ppermute(value, "c", [(0, 1), (1, 0)])


def place(axes, steps, sign=1):
    sizes = sizes_of(axes)
    here = [(lax.axis_index(a) + sign * s) % n for a, s, n in zip(axes, steps, sizes)]
    return linear(here, sizes)


def pick(value, index, axis=0):
    return lax.dynamic_index_in_dim(value, index, axis, keepdims=False)


def put(buffer, value, index):
    return lax.dynamic_update_slice_in_dim(buffer, value[None], index, 0)


def gather_groups(block, chips):
    same = [shift(block, chips, steps) for steps in offsets(chips)]
    return [(s, swap(s)) for s in same]


def scatter_sum(for_same, for_other):
    return for_same + swap(for_other.astype(bf16)).astype(f32)


def exchange(blocks, chips):
    core = lax.axis_index("c")
    got = swap(pick(blocks, 1 - core, 1))
    keep = pick(blocks, core, 1)
    first, second = jnp.where(core == 0, keep, got), jnp.where(core == 0, got, keep)
    pairs = jnp.stack([first, second], axis=1)
    result = jnp.zeros_like(pairs)
    for steps in offsets(chips):
        piece = shift(pick(pairs, place(chips, steps)), chips, steps)
        result = put(result, piece, place(chips, steps, -1))
    return result


def small_sum(value, axes):
    for axis in axes:
        if lax.axis_size(axis) == 2:
            value = value + lax.ppermute(value, axis, [(0, 1), (1, 0)])
        else:
            value = lax.psum(value, axis)
    return value


def product(left_side, right_side):
    return jnp.dot(left_side, right_side, preferred_element_type=f32)


def product_left(left_side, right_side):
    return lax.dot_general(
        left_side, right_side, (((0,), (0,)), ((), ())), preferred_element_type=f32
    )


def product_right(left_side, right_side):
    return lax.dot_general(
        left_side, right_side, (((1,), (1,)), ((), ())), preferred_element_type=f32
    )


def allowed_keys(shape, key_start, query_start, starts):
    key_place = key_start + lax.broadcasted_iota(jnp.int32, shape, 0)
    query_place = query_start + lax.broadcasted_iota(jnp.int32, shape, 1)
    return (key_place >= starts) & (key_place <= query_place)


def attend_kernel(low_ref, starts_ref, q_ref, k_ref, v_ref, out_ref, log_ref):
    block = pl.program_id(1)
    bq, bk = q_ref.shape[0], BLOCK_K
    queries, starts = q_ref[...], starts_ref[...]

    def step(j, carry):
        top, total, acc = carry
        rows = pl.ds(pl.multiple_of(j * bk, bk), bk)
        scores = product_right(k_ref[rows, :], queries) * scale_factor
        ok = allowed_keys(scores.shape, j * bk, block * bq, starts)
        scores = jnp.where(ok, scores, masked_score)
        new_top = jnp.maximum(top, jnp.max(scores, axis=0, keepdims=True))
        ratio = jnp.exp(top - new_top)
        expanded = jnp.exp(scores - new_top)
        total = total * ratio + jnp.sum(expanded, axis=0, keepdims=True)
        acc = acc * ratio + product_left(v_ref[rows, :], expanded.astype(bf16))
        return (new_top, total, acc)

    init = (
        jnp.full((1, bq), masked_score, f32),
        jnp.zeros((1, bq), f32),
        jnp.zeros((HEAD_DIM, bq), f32),
    )
    top, total, acc = lax.fori_loop(low_ref[block], (block * bq + bq) // bk, step, init)
    out_ref[...] = (acc / total).T
    log_ref[0] = top + jnp.log(total)


def attend(lows, starts, queries, keys, values):
    length, width = queries.shape
    heads, bq = width // HEAD_DIM, BLOCK_Q
    return pl.pallas_call(
        attend_kernel,
        grid_spec=pltpu.PrefetchScalarGridSpec(
            num_scalar_prefetch=1,
            grid=(heads, length // bq),
            in_specs=[
                pl.BlockSpec((1, bq), lambda h, i, low: (0, i)),
                pl.BlockSpec((bq, HEAD_DIM), lambda h, i, low: (i, h)),
                pl.BlockSpec((length, HEAD_DIM), lambda h, i, low: (0, h)),
                pl.BlockSpec((length, HEAD_DIM), lambda h, i, low: (0, h)),
            ],
            out_specs=[
                pl.BlockSpec((bq, HEAD_DIM), lambda h, i, low: (i, h)),
                pl.BlockSpec((1, 1, bq), lambda h, i, low: (h, 0, i)),
            ],
        ),
        out_shape=[
            jax.ShapeDtypeStruct((length, width), f32),
            jax.ShapeDtypeStruct((heads, 1, length), f32),
        ],
        compiler_params=pltpu.CompilerParams(vmem_limit_bytes=48 << 20),
        name="attend",
    )(lows, starts, queries, keys, values)


def attend_back_kernel(
    low_ref, starts_ref, q_ref, k_ref, v_ref, out_ref, log_ref, grad_ref, dq_ref, dk_ref, dv_ref
):
    length = q_ref.shape[0]
    bq, bk = BLOCK_Q, BLOCK_K
    dk_ref[...] = jnp.zeros_like(dk_ref)
    dv_ref[...] = jnp.zeros_like(dv_ref)

    def query_step(i, carry):
        queries_at = pl.ds(pl.multiple_of(i * bq, bq), bq)
        queries, grads = q_ref[queries_at, :], grad_ref[queries_at, :]
        starts = starts_ref[:, queries_at]
        log_total = log_ref[0, :, queries_at]
        inner = jnp.sum((grads.astype(f32) * out_ref[queries_at, :]).T, axis=0, keepdims=True)

        def step(j, acc):
            rows = pl.ds(pl.multiple_of(j * bk, bk), bk)
            keys = k_ref[rows, :]
            scores = product_right(keys, queries) * scale_factor
            ok = allowed_keys(scores.shape, j * bk, i * bq, starts)
            probs = jnp.where(ok, jnp.exp(scores - log_total), 0.0)
            dv_ref[rows, :] += product(probs.astype(bf16), grads)
            prob_grad = product_right(v_ref[rows, :], grads)
            score_grad = (probs * (prob_grad - inner)).astype(bf16)
            dk_ref[rows, :] += product(score_grad, queries) * scale_factor
            return acc + product_left(keys, score_grad)

        acc = lax.fori_loop(
            low_ref[i], (i * bq + bq) // bk, step, jnp.zeros((HEAD_DIM, bq), f32)
        )
        dq_ref[queries_at, :] = (acc * scale_factor).T
        return carry

    lax.fori_loop(0, length // bq, query_step, 0)


def attend_back(lows, starts, queries, keys, values, out, log_total, grads):
    length, width = queries.shape
    heads = width // HEAD_DIM
    column = pl.BlockSpec((length, HEAD_DIM), lambda h, low: (0, h))
    return pl.pallas_call(
        attend_back_kernel,
        grid_spec=pltpu.PrefetchScalarGridSpec(
            num_scalar_prefetch=1,
            grid=(heads,),
            in_specs=[
                pl.BlockSpec((1, length), lambda h, low: (0, 0)),
                column,
                column,
                column,
                column,
                pl.BlockSpec((1, 1, length), lambda h, low: (h, 0, 0)),
                column,
            ],
            out_specs=[column, column, column],
        ),
        out_shape=[jax.ShapeDtypeStruct((length, width), f32)] * 3,
        compiler_params=pltpu.CompilerParams(vmem_limit_bytes=56 << 20),
        name="attend_back",
    )(lows, starts, queries, keys, values, out, log_total, grads)


def norm_forward(values, gain_row):
    factor = lax.rsqrt(jnp.mean(values * values, axis=-1, keepdims=True) + norm_epsilon)
    return (values * factor * gain_row, factor)


def norm_backward(values, factor, gain_row, incoming):
    weighted = incoming * gain_row
    mixing = jnp.mean(weighted * values, axis=-1, keepdims=True)
    return (
        factor * (weighted - values * factor * factor * mixing),
        jnp.sum(incoming * values * factor, axis=0),
    )


def rotate(values, cosine, sine_part):
    count_rows, width = values.shape
    heads = values.reshape(count_rows, width // HEAD_DIM, HEAD_DIM)
    halfway = HEAD_DIM // 2
    turned = jnp.concatenate([heads[..., halfway:], heads[..., :halfway]], axis=-1)
    return (heads * cosine[:, None] + turned * sine_part[:, None]).reshape(count_rows, width)


def arrange(lengths, positions):
    finish = jnp.cumsum(lengths)
    has_ended = finish[None, :] <= positions[:, None]
    return jnp.sum(jnp.where(has_ended, lengths[None, :], 0), axis=1).astype(jnp.int32)


def to_natural(rows, chips, data):
    order = data + chips
    if order == AXES[:4]:
        return rows
    shaped = rows.reshape(sizes_of(order) + (-1,) + rows.shape[1:])
    back = tuple(order.index(a) for a in AXES[:4])
    return shaped.transpose(back + tuple(range(4, shaped.ndim))).reshape(rows.shape)


def from_natural(rows, chips, data):
    order = data + chips
    if order == AXES[:4]:
        return rows
    shaped = rows.reshape(sizes_of(AXES[:4]) + (-1,) + rows.shape[1:])
    perm = tuple(AXES.index(a) for a in order)
    return shaped.transpose(perm + tuple(range(4, shaped.ndim))).reshape(rows.shape)


def columns_out(weight):
    rows = weight.shape[0]
    shaped = weight.reshape((rows, 2) + sizes_of(AXES) + (-1,))
    where = {a: 2 + i for i, a in enumerate(AXES)}
    perm = [where[a] for a in MLP_CHIPS] + [where["c"], 0, 1] + [where[a] for a in MLP_DATA] + [7]
    chips = 1
    for a in MLP_CHIPS:
        chips *= lax.axis_size(a)
    return shaped.transpose(perm).reshape(chips, 2, rows, -1)


def columns_back(blocks):
    rows = blocks.shape[2]
    shape = sizes_of(MLP_CHIPS) + (2, rows, 2) + sizes_of(MLP_DATA) + (-1,)
    names = MLP_CHIPS + ("c", "rows", "half") + MLP_DATA + ("unit",)
    wanted = ("rows", "half") + AXES + ("unit",)
    perm = tuple(names.index(a) for a in wanted)
    return blocks.reshape(shape).transpose(perm).reshape(rows, -1)


def scatter_over(value, axes):
    return lax.psum_scatter(value.astype(bf16), axes, scatter_dimension=0, tiled=True)


def on_device(
    hidden_in, seq_lengths, qkv_weight, out_weight, in_weight, down_weight, norm_gains, upstream
):
    piece_len, model_width = hidden_in.shape[1:]
    line_sizes = sizes_of(LINE)
    line = line_sizes[0] * line_sizes[1]
    length = piece_len * line * 2
    width = D // (line * 2)
    core = lax.axis_index("c")
    ctx_place = linear([lax.axis_index(a) for a in CTX], sizes_of(CTX))
    data_place = linear([lax.axis_index(a) for a in DATA], sizes_of(DATA))
    line_place = linear([lax.axis_index(a) for a in LINE], line_sizes)
    lengths = lax.dynamic_index_in_dim(seq_lengths, data_place, 0, keepdims=False)
    places = jnp.arange(length, dtype=jnp.int32)
    starts = arrange(lengths, places)
    offset = (places - starts).astype(f32)
    lows = starts[::BLOCK_Q] // BLOCK_K
    starts_row = starts.reshape(1, length)
    inverse = rope_base ** (-2.0 * jnp.arange(HEAD_DIM // 2, dtype=f32) / HEAD_DIM)
    angles = offset[:, None] * inverse[None, :]
    cosine, sine_part = jnp.cos(angles), jnp.sin(angles)
    cosine = jnp.concatenate([cosine, cosine], axis=1)
    sine_part = jnp.concatenate([-sine_part, sine_part], axis=1)

    own_input = hidden_in.reshape(piece_len, model_width)

    row_count = qkv_weight.shape[0]
    qkv_blocks = qkv_weight.reshape(row_count, 3, line, 2, width).transpose(2, 3, 0, 1, 4)
    qkv_rows = exchange(qkv_blocks.reshape(line, 2, row_count, 3 * width), LINE)
    qkv_here = lax.all_gather(
        qkv_rows.reshape(-1, 3 * width), DATA, axis=0, tiled=True
    )

    full_input = jnp.zeros((line, 2, piece_len, model_width), bf16)
    for steps, (same, other) in zip(offsets(LINE), gather_groups(own_input, LINE)):
        at = place(LINE, steps, -1)
        full_input = lax.dynamic_update_slice(full_input, same[None, None], (at, core, 0, 0))
        full_input = lax.dynamic_update_slice(full_input, other[None, None], (at, 1 - core, 0, 0))
    full_input = full_input.reshape(length, model_width)

    out_line = jnp.zeros((line,) + out_weight.shape, bf16)
    for steps in offsets(LINE):
        out_line = put(out_line, shift(out_weight, LINE, steps), place(LINE, steps, -1))
    out_half = lax.all_gather(
        out_line.reshape(-1, D), DATA, axis=0, tiled=True
    ).reshape(-1, out_weight.shape[0], D)
    out_other = swap(out_half)
    out_full = jnp.stack(
        [jnp.where(core == 0, out_half, out_other), jnp.where(core == 0, out_other, out_half)],
        axis=1,
    ).reshape(D, D)

    in_rows = exchange(columns_out(in_weight), MLP_CHIPS)
    in_here = to_natural(
        lax.all_gather(in_rows.reshape(-1, in_rows.shape[-1]), MLP_DATA, axis=0, tiled=True),
        MLP_CHIPS,
        MLP_DATA,
    )
    down_here = lax.all_gather(down_weight, MLP_DATA, axis=0, tiled=True)
    units = down_here.shape[0]

    projected = product(full_input, qkv_here)
    q_raw, k_raw = projected[:, :width], projected[:, width : 2 * width]
    value_low = projected[:, 2 * width :].astype(bf16)
    squares = small_sum(
        jnp.stack([jnp.sum(q_raw * q_raw, axis=1), jnp.sum(k_raw * k_raw, axis=1)]), CTX
    )
    factors = lax.rsqrt(squares / D + norm_epsilon)
    q_factor, k_factor = factors[0][:, None], factors[1][:, None]
    gains_here = lax.dynamic_slice(norm_gains, (0, ctx_place * width), (2, width))
    query_low = rotate(q_raw * q_factor * gains_here[0], cosine, sine_part).astype(bf16)
    key_low = rotate(k_raw * k_factor * gains_here[1], cosine, sine_part).astype(bf16)
    head_out, log_total = attend(lows, starts_row, query_low, key_low, value_low)

    attended = exchange(head_out.astype(bf16).reshape(line, 2, piece_len, width), LINE)
    attended_low = attended.reshape(line * 2, piece_len, width).transpose(1, 0, 2)
    attended_low = attended_low.reshape(piece_len, D)
    branch = product(attended_low, out_full)
    branch_normed, branch_factor = norm_forward(branch, norm_gains[2])
    residual = own_input.astype(f32) + branch_normed
    residual_low = residual.astype(bf16)

    mlp_steps = offsets(MLP_CHIPS)
    residual_groups = [
        jnp.concatenate(pair, axis=0) for pair in gather_groups(residual_low, MLP_CHIPS)
    ]
    gate_ups, hidden_groups = [], []
    second = None
    for steps, rows in zip(mlp_steps, residual_groups):
        gate_up = product(rows, in_here)
        gate_part, up_part = gate_up[:, :units], gate_up[:, units:]
        hidden = (gate_part * jax.nn.sigmoid(gate_part) * up_part).astype(bf16)
        part = product(hidden, down_here)
        part = scatter_sum(part[:piece_len], part[piece_len:])
        if any(steps):
            back = tuple(-s for s in steps)
            part = shift(part.astype(bf16), MLP_CHIPS, back).astype(f32)
        second = part if second is None else second + part
        gate_ups.append(gate_up)
        hidden_groups.append(hidden)
    second_normed, second_factor = norm_forward(second, norm_gains[3])
    result = residual + second_normed
    live_places = ctx_place * piece_len + jnp.arange(piece_len, dtype=jnp.int32)
    live_rows = (live_places < jnp.sum(lengths)).astype(f32)[:, None]
    sums = jnp.stack(
        [
            jnp.sum(result * result * live_rows),
            jnp.sum(branch * branch * live_rows),
            jnp.sum(second * second * live_rows),
        ]
    )

    incoming = upstream.reshape(piece_len, model_width).astype(f32)
    second_grad, second_gain_grad = norm_backward(second, second_factor, norm_gains[3], incoming)
    second_grad_groups = [
        jnp.concatenate(pair, axis=0)
        for pair in gather_groups(second_grad.astype(bf16), MLP_CHIPS)
    ]
    gate_up_grads = []
    residual_grad = incoming
    for steps, rows, gate_up in zip(mlp_steps, second_grad_groups, gate_ups):
        hidden_grad = product_right(rows, down_here)
        gate_part, up_part = gate_up[:, :units], gate_up[:, units:]
        sigmoid_gate = jax.nn.sigmoid(gate_part)
        gate_grad = hidden_grad * up_part * sigmoid_gate * (1.0 + gate_part * (1.0 - sigmoid_gate))
        up_grad = hidden_grad * gate_part * sigmoid_gate
        gate_up_low = jnp.concatenate([gate_grad, up_grad], axis=1).astype(bf16)
        part = product_right(gate_up_low, in_here)
        part = scatter_sum(part[:piece_len], part[piece_len:])
        if any(steps):
            back = tuple(-s for s in steps)
            part = shift(part.astype(bf16), MLP_CHIPS, back).astype(f32)
        residual_grad = residual_grad + part
        gate_up_grads.append(gate_up_low)
    hidden_all = jnp.concatenate(hidden_groups, axis=0)
    second_grad_all = jnp.concatenate(second_grad_groups, axis=0)
    grad_down = scatter_over(product_left(hidden_all, second_grad_all), MLP_DATA).astype(f32)
    residual_all = jnp.concatenate(residual_groups, axis=0)
    gate_up_all = jnp.concatenate(gate_up_grads, axis=0)
    grad_in = from_natural(
        product_left(residual_all, gate_up_all).astype(bf16), MLP_CHIPS, MLP_DATA
    )
    grad_in = scatter_over(grad_in, MLP_DATA).reshape(in_rows.shape)
    grad_in = columns_back(exchange(grad_in, MLP_CHIPS)).astype(f32)

    branch_grad, branch_gain_grad = norm_backward(
        branch, branch_factor, norm_gains[2], residual_grad
    )
    branch_grad_low = branch_grad.astype(bf16)
    attended_grad = product_right(branch_grad_low, out_full).astype(bf16)
    attended_grad = attended_grad.reshape(piece_len, line, 2, width).transpose(1, 2, 0, 3)
    head_grad = exchange(attended_grad, LINE).reshape(length, width)

    out_grad = product_left(attended_low, branch_grad_low).reshape(-1, 2, out_weight.shape[0], D)
    out_grad = scatter_sum(pick(out_grad, core, 1), pick(out_grad, 1 - core, 1))
    out_grad = scatter_over(out_grad.reshape(D // 2, D), DATA).reshape((line,) + out_weight.shape)
    grad_out = None
    for steps in offsets(LINE):
        part = shift(pick(out_grad, place(LINE, steps)), LINE, steps).astype(f32)
        grad_out = part if grad_out is None else grad_out + part

    query_grad, key_grad, value_grad = attend_back(
        lows, starts_row, query_low, key_low, value_low, head_out, log_total, head_grad
    )
    query_turned = rotate(query_grad, cosine, -sine_part)
    key_turned = rotate(key_grad, cosine, -sine_part)
    query_weighted, key_weighted = query_turned * gains_here[0], key_turned * gains_here[1]
    mixing = small_sum(
        jnp.stack([jnp.sum(query_weighted * q_raw, axis=1), jnp.sum(key_weighted * k_raw, axis=1)]),
        CTX,
    )
    mixing = mixing / D
    query_mix, key_mix = mixing[0][:, None], mixing[1][:, None]
    query_raw_grad = q_factor * (query_weighted - q_raw * q_factor * q_factor * query_mix)
    key_raw_grad = k_factor * (key_weighted - k_raw * k_factor * k_factor * key_mix)
    query_gain_grad = jnp.sum(query_turned * q_raw * q_factor, axis=0)
    key_gain_grad = jnp.sum(key_turned * k_raw * k_factor, axis=0)
    projected_grad = jnp.concatenate([query_raw_grad, key_raw_grad, value_grad], axis=1)
    projected_grad = projected_grad.astype(bf16)

    grad_qkv = scatter_over(product_left(full_input, projected_grad), DATA)
    grad_qkv = exchange(grad_qkv.reshape(line, 2, row_count, 3 * width), LINE)
    grad_qkv = grad_qkv.reshape(line, 2, row_count, 3, width).transpose(2, 3, 0, 1, 4)
    grad_qkv = grad_qkv.reshape(row_count, 3 * D).astype(f32)

    input_grad = residual_grad
    grad_blocks = projected_grad.reshape(line, 2, piece_len, 3 * width)
    for steps in offsets(LINE)[::-1]:
        rows = pick(grad_blocks, place(LINE, steps))
        rows = jnp.concatenate([pick(rows, core), pick(rows, 1 - core)], axis=0)
        part = product_right(rows, qkv_here)
        part = scatter_sum(part[:piece_len], part[piece_len:])
        if any(steps):
            part = shift(part.astype(bf16), LINE, steps).astype(f32)
        input_grad = input_grad + part

    gain_rows = jnp.zeros((5, D), f32)
    gain_rows = lax.dynamic_update_slice(
        gain_rows, jnp.stack([query_gain_grad, key_gain_grad]), (0, ctx_place * width)
    )
    gain_rows = gain_rows.at[2].set(branch_gain_grad).at[3].set(second_gain_grad)
    gain_rows = gain_rows.at[4, :3].set(sums)
    gain_rows = small_sum(gain_rows, AXES)
    live_count = jnp.sum(seq_lengths).astype(f32)
    rms_values = jnp.sqrt(gain_rows[4, :3] / (live_count * model_width))
    return (
        result.astype(bf16)[None],
        input_grad[None],
        grad_qkv,
        grad_out,
        grad_in,
        grad_down,
        gain_rows[:4],
        rms_values,
    )


def solution(mesh):
    dp, ctx = mesh.shape["dp"], mesh.shape["ctx"]
    fine = Mesh(mesh.devices.reshape(2, dp // 2, 2, ctx // 4, 2), AXES)
    return jax.shard_map(
        on_device,
        mesh=fine,
        in_specs=(
            P(DATA, CTX, None),
            P(),
            P(AXES, None),
            P(AXES, None),
            P(AXES, None),
            P(AXES, None),
            P(),
            P(DATA, CTX, None),
        ),
        out_specs=(
            P(DATA, CTX, None),
            P(DATA, CTX, None),
            P(AXES, None),
            P(AXES, None),
            P(AXES, None),
            P(AXES, None),
            P(),
            P(),
        ),
        check_vma=False,
    )
```

```python
import itertools

import jax
import jax.numpy as jnp
import numpy as np
from jax import lax
from jax.experimental import pallas as pl
from jax.experimental.pallas import tpu as pltpu
from jax.sharding import Mesh
from jax.sharding import PartitionSpec as P

D = 2048
HEADS = 16
HEAD_DIM = 128
FF = 8192

norm_epsilon = 1e-06
rope_base = 500000.0
masked_score = -1e30
scale_factor = HEAD_DIM ** (-0.5)

AXES = ("dh", "dl", "zh", "zl", "c")
DATA = ("dh", "dl")
LINE = ("zh", "zl")
CTX = ("zh", "zl", "c")

BLOCK_Q = 512
BLOCK_K = 512

bf16 = jnp.bfloat16
f32 = jnp.float32


def sizes_of(axes):
    return tuple(lax.axis_size(a) for a in axes)


def offsets(axes):
    return list(itertools.product(*[range(n) for n in sizes_of(axes)]))


def linear(index, sizes):
    total = 0
    for i, n in zip(index, sizes):
        total = total * n + i
    return total


def shift(value, axes, steps):
    if not any(steps):
        return value
    sizes = sizes_of(axes)
    pairs = []
    for index in itertools.product(*[range(n) for n in sizes]):
        target = tuple((i + s) % n for i, s, n in zip(index, steps, sizes))
        pairs.append((linear(index, sizes), linear(target, sizes)))
    return lax.ppermute(value, axes, pairs)


def swap(value):
    return lax.ppermute(value, "c", [(0, 1), (1, 0)])


def place(axes, steps, sign=1):
    sizes = sizes_of(axes)
    here = [(lax.axis_index(a) + sign * s) % n for a, s, n in zip(axes, steps, sizes)]
    return linear(here, sizes)


def pick(value, index, axis=0):
    return lax.dynamic_index_in_dim(value, index, axis, keepdims=False)


def put(buffer, value, index):
    return lax.dynamic_update_slice_in_dim(buffer, value[None], index, 0)


def together(*values):
    return lax.optimization_barrier(values)


def line_order(count):
    return np.array(
        [sorted(range(count), key=lambda j: (abs(i - j), j != i ^ 1)) for i in range(count)],
        dtype=np.int32,
    )


class Line:
    def __init__(self, axes):
        self.axes = axes
        sizes = sizes_of(axes)
        self.count = sizes[0] * sizes[1]
        self.place = linear([lax.axis_index(a) for a in axes], sizes)
        self.order = line_order(self.count)

    def served(self, k):
        return jnp.asarray(self.order[:, k])[self.place]

    def hop(self, value, step, keep=lambda i: True):
        pairs = [
            (i, i + step) for i in range(self.count) if 0 <= i + step < self.count and keep(i)
        ]
        return lax.ppermute(value, self.axes, pairs)

    def choose(self, options, wanted):
        used = sorted({w for w in wanted if w is not None})
        value = options[used[0]]
        for w in used[1:]:
            mask = np.array([v == w for v in wanted])
            value = jnp.where(jnp.asarray(mask)[self.place], options[w], value)
        return value

    def gather(self, block, work, extra=None, plan=None):
        plan = plan or [[k] for k in range(self.count)]
        options, results, tied, arrived, swapped = {}, [], [], [], [None]
        for slot in range(self.count):
            if slot:
                wanted = []
                for i in range(self.count):
                    j = self.order[i, slot]
                    wanted.append((1, i - j) if j < i else (-1, j - i))
                arrived.append(self.choose(options, wanted))
            else:
                arrived.append(block)
            moved = ()
            if slot + 1 < self.count:
                moved = tuple(
                    self.hop(options[(step, slot)] if slot else block, step) for step in (1, -1)
                )
            other = swap(arrived[slot])
            done = [work(k, arrived[k], swapped[k]) for k in plan[slot]]
            more = extra(slot, tied) if extra else ()
            moved, other, done, more = together(moved, other, done, more)
            if moved:
                options[(1, slot + 1)], options[(-1, slot + 1)] = moved
            swapped.append(other)
            tied.append(more)
            results += done
        results.append(work(self.count, None, swapped[self.count]))
        return results, tied

    def scatter(self, parts, fill=None):
        count = self.count
        made = {count - 1: parts(count - 1)}
        last = {1: None, -1: None}
        tied = []
        for slot in range(1, count):
            far = count - slot
            moved = []
            for step in (1, -1):
                wanted = []
                for i in range(count):
                    j = i + step * far
                    wanted.append(int(np.argmax(self.order[i] == j)) if 0 <= j < count else None)
                value = self.choose(made, wanted)
                if last[step] is not None:
                    value = value + last[step].astype(f32)
                keep = lambda i: 0 <= i + step * far < count
                moved.append(self.hop(value.astype(bf16), step, keep))
            done = parts(far - 1)
            more = fill(slot, tied) if fill else ()
            moved, done, more = together(moved, done, more)
            tied.append(more)
            made[far - 1] = done
            last[1], last[-1] = moved
        return made[0] + last[1].astype(f32) + last[-1].astype(f32), tied


def scatter_sum(for_same, for_other):
    return for_same.astype(f32) + swap(for_other.astype(bf16)).astype(f32)


def exchange_cores(blocks):
    core = lax.axis_index("c")
    got = swap(pick(blocks, 1 - core, 1))
    return by_core(pick(blocks, core, 1), got)


def by_core(mine, other):
    shape = (mine.shape[0], 2) + mine.shape[1:]
    here = lax.broadcasted_iota(jnp.int32, shape, 1) == lax.axis_index("c")
    return jnp.where(here, mine[:, None], other[:, None])


def exchange_chips(pairs, chips):
    result = jnp.zeros_like(pairs)
    for steps in offsets(chips):
        piece = shift(pick(pairs, place(chips, steps)), chips, steps)
        result = put(result, piece, place(chips, steps, -1))
    return result


def exchange(blocks, chips):
    return exchange_chips(exchange_cores(blocks), chips)


def small_sum(value, axes):
    for axis in axes:
        if lax.axis_size(axis) == 2:
            value = value + lax.ppermute(value, axis, [(0, 1), (1, 0)])
        else:
            value = lax.psum(value, axis)
    return value


def product(left_side, right_side):
    return jnp.dot(left_side, right_side, preferred_element_type=f32)


def product_left(left_side, right_side):
    return lax.dot_general(
        left_side, right_side, (((0,), (0,)), ((), ())), preferred_element_type=f32
    )


def product_right(left_side, right_side):
    return lax.dot_general(
        left_side, right_side, (((1,), (1,)), ((), ())), preferred_element_type=f32
    )


def allowed_keys(shape, key_start, query_start, starts):
    key_place = key_start + lax.broadcasted_iota(jnp.int32, shape, 0)
    query_place = query_start + lax.broadcasted_iota(jnp.int32, shape, 1)
    return (key_place >= starts) & (key_place <= query_place)


def attend_kernel(low_ref, starts_ref, q_ref, k_ref, v_ref, out_ref, log_ref):
    block = pl.program_id(1)
    bq, bk = q_ref.shape[0], BLOCK_K
    queries, starts = q_ref[...], starts_ref[...]

    def step(j, carry):
        top, total, acc = carry
        rows = pl.ds(pl.multiple_of(j * bk, bk), bk)
        scores = product_right(k_ref[rows, :], queries) * scale_factor
        ok = allowed_keys(scores.shape, j * bk, block * bq, starts)
        scores = jnp.where(ok, scores, masked_score)
        new_top = jnp.maximum(top, jnp.max(scores, axis=0, keepdims=True))
        ratio = jnp.exp(top - new_top)
        expanded = jnp.exp(scores - new_top)
        total = total * ratio + jnp.sum(expanded, axis=0, keepdims=True)
        acc = acc * ratio + product_left(v_ref[rows, :], expanded.astype(bf16))
        return (new_top, total, acc)

    init = (
        jnp.full((1, bq), masked_score, f32),
        jnp.zeros((1, bq), f32),
        jnp.zeros((HEAD_DIM, bq), f32),
    )
    top, total, acc = lax.fori_loop(low_ref[block], (block * bq + bq) // bk, step, init)
    out_ref[...] = (acc / total).T
    log_ref[0] = top + jnp.log(total)


def attend(lows, starts, queries, keys, values):
    length, width = queries.shape
    heads, bq = width // HEAD_DIM, BLOCK_Q
    return pl.pallas_call(
        attend_kernel,
        grid_spec=pltpu.PrefetchScalarGridSpec(
            num_scalar_prefetch=1,
            grid=(heads, length // bq),
            in_specs=[
                pl.BlockSpec((1, bq), lambda h, i, low: (0, i)),
                pl.BlockSpec((bq, HEAD_DIM), lambda h, i, low: (i, h)),
                pl.BlockSpec((length, HEAD_DIM), lambda h, i, low: (0, h)),
                pl.BlockSpec((length, HEAD_DIM), lambda h, i, low: (0, h)),
            ],
            out_specs=[
                pl.BlockSpec((bq, HEAD_DIM), lambda h, i, low: (i, h)),
                pl.BlockSpec((1, 1, bq), lambda h, i, low: (h, 0, i)),
            ],
        ),
        out_shape=[
            jax.ShapeDtypeStruct((length, width), f32),
            jax.ShapeDtypeStruct((heads, 1, length), f32),
        ],
        compiler_params=pltpu.CompilerParams(vmem_limit_bytes=48 << 20),
        name="attend",
    )(lows, starts, queries, keys, values)


def attend_back_kernel(
    low_ref, starts_ref, q_ref, k_ref, v_ref, out_ref, log_ref, grad_ref, dq_ref, dk_ref, dv_ref
):
    length = q_ref.shape[0]
    bq, bk = BLOCK_Q, BLOCK_K
    dk_ref[...] = jnp.zeros_like(dk_ref)
    dv_ref[...] = jnp.zeros_like(dv_ref)

    def query_step(i, carry):
        queries_at = pl.ds(pl.multiple_of(i * bq, bq), bq)
        queries, grads = q_ref[queries_at, :], grad_ref[queries_at, :]
        starts = starts_ref[:, queries_at]
        log_total = log_ref[0, :, queries_at]
        inner = jnp.sum((grads.astype(f32) * out_ref[queries_at, :]).T, axis=0, keepdims=True)

        def step(j, acc):
            rows = pl.ds(pl.multiple_of(j * bk, bk), bk)
            keys = k_ref[rows, :]
            scores = product_right(keys, queries) * scale_factor
            ok = allowed_keys(scores.shape, j * bk, i * bq, starts)
            probs = jnp.where(ok, jnp.exp(scores - log_total), 0.0)
            dv_ref[rows, :] += product(probs.astype(bf16), grads)
            prob_grad = product_right(v_ref[rows, :], grads)
            score_grad = (probs * (prob_grad - inner)).astype(bf16)
            dk_ref[rows, :] += product(score_grad, queries) * scale_factor
            return acc + product_left(keys, score_grad)

        acc = lax.fori_loop(
            low_ref[i], (i * bq + bq) // bk, step, jnp.zeros((HEAD_DIM, bq), f32)
        )
        dq_ref[queries_at, :] = (acc * scale_factor).T
        return carry

    lax.fori_loop(0, length // bq, query_step, 0)


def attend_back(lows, starts, queries, keys, values, out, log_total, grads):
    length, width = queries.shape
    heads = width // HEAD_DIM
    column = pl.BlockSpec((length, HEAD_DIM), lambda h, low: (0, h))
    return pl.pallas_call(
        attend_back_kernel,
        grid_spec=pltpu.PrefetchScalarGridSpec(
            num_scalar_prefetch=1,
            grid=(heads,),
            in_specs=[
                pl.BlockSpec((1, length), lambda h, low: (0, 0)),
                column,
                column,
                column,
                column,
                pl.BlockSpec((1, 1, length), lambda h, low: (h, 0, 0)),
                column,
            ],
            out_specs=[column, column, column],
        ),
        out_shape=[jax.ShapeDtypeStruct((length, width), f32)] * 3,
        compiler_params=pltpu.CompilerParams(vmem_limit_bytes=56 << 20),
        name="attend_back",
    )(lows, starts, queries, keys, values, out, log_total, grads)


def spread_kernel(in_ref, out_ref):
    unit = out_ref.shape[2]
    for k in range(out_ref.shape[0]):
        out_ref[k] = in_ref[:, k * unit : (k + 1) * unit]


def spread(weight, groups, owners):
    rows, columns = weight.shape
    unit = columns // (groups * owners)
    if unit % 128:
        shaped = weight.reshape(rows, groups, owners, unit).transpose(2, 0, 1, 3)
        return shaped.reshape(owners, rows, groups * unit)
    return pl.pallas_call(
        spread_kernel,
        grid=(groups,),
        in_specs=[pl.BlockSpec((rows, owners * unit), lambda g: (0, g))],
        out_specs=pl.BlockSpec((owners, rows, unit), lambda g: (0, 0, g)),
        out_shape=jax.ShapeDtypeStruct((owners, rows, groups * unit), weight.dtype),
        name="spread",
    )(weight)


def collect_kernel(in_ref, out_ref):
    unit = in_ref.shape[2]
    for k in range(in_ref.shape[0]):
        out_ref[:, k * unit : (k + 1) * unit] = in_ref[k].astype(f32)


def collect(blocks, groups):
    owners, rows, columns = blocks.shape
    unit = columns // groups
    if unit % 128:
        shaped = blocks.reshape(owners, rows, groups, unit).transpose(1, 2, 0, 3)
        return shaped.reshape(rows, groups * owners * unit).astype(f32)
    return pl.pallas_call(
        collect_kernel,
        grid=(groups,),
        in_specs=[pl.BlockSpec((owners, rows, unit), lambda g: (0, 0, g))],
        out_specs=pl.BlockSpec((rows, owners * unit), lambda g: (0, g)),
        out_shape=jax.ShapeDtypeStruct((rows, groups * owners * unit), f32),
        name="collect",
    )(blocks)


def columns_of(row):
    return jnp.broadcast_to(row, (HEAD_DIM, row.shape[1])).T


def halves_swapped(values):
    return pltpu.roll(values, HEAD_DIM // 2, 1)


def project_kernel(in_ref, weight_ref, out_ref, square_ref):
    width = out_ref.shape[1] // 3
    out = product(in_ref[...], weight_ref[...])
    out_ref[...] = out
    for part in range(2):
        total = None
        for h in range(0, width, HEAD_DIM):
            raw = out[:, part * width + h : part * width + h + HEAD_DIM]
            total = raw * raw if total is None else total + raw * raw
        square_ref[part : part + 1, :] = jnp.sum(total.T, axis=0, keepdims=True)


def project(inputs, weight):
    length, depth = inputs.shape
    columns = weight.shape[1]
    return pl.pallas_call(
        project_kernel,
        grid=(length // 256,),
        in_specs=[row_block(depth, 256), whole_block(depth, columns)],
        out_specs=[row_block(columns, 256), lane_block(2, 256)],
        out_shape=[
            jax.ShapeDtypeStruct((length, columns), f32),
            jax.ShapeDtypeStruct((2, length), f32),
        ],
        compiler_params=pltpu.CompilerParams(vmem_limit_bytes=32 << 20),
        name="project",
    )(inputs, weight)


def turn_kernel(proj_ref, factor_ref, gain_ref, cos_ref, sin_ref, q_ref, k_ref, v_ref):
    width = q_ref.shape[1]
    cosine, sine_part = cos_ref[...], sin_ref[...]
    for part, out in enumerate((q_ref, k_ref)):
        factor = columns_of(factor_ref[part : part + 1, :])
        for h in range(0, width, HEAD_DIM):
            raw = proj_ref[:, part * width + h : part * width + h + HEAD_DIM]
            normed = raw * factor * gain_ref[part : part + 1, h : h + HEAD_DIM]
            turned = normed * cosine + halves_swapped(normed) * sine_part
            out[:, h : h + HEAD_DIM] = turned.astype(bf16)
    v_ref[...] = proj_ref[:, 2 * width :].astype(bf16)


def row_block(columns, rows=512):
    return pl.BlockSpec((rows, columns), lambda i: (i, 0))


def lane_block(lines, rows=512):
    return pl.BlockSpec((lines, rows), lambda i: (0, i))


def whole_block(*shape):
    return pl.BlockSpec(shape, lambda i: (0,) * len(shape))


def turn(projected, factors, gains, cosine, sine_part):
    length, columns = projected.shape
    width = columns // 3
    return pl.pallas_call(
        turn_kernel,
        grid=(length // 512,),
        in_specs=[
            row_block(columns),
            lane_block(2),
            whole_block(2, width),
            row_block(HEAD_DIM),
            row_block(HEAD_DIM),
        ],
        out_specs=[row_block(width)] * 3,
        out_shape=[jax.ShapeDtypeStruct((length, width), bf16)] * 3,
        name="turn",
    )(projected, factors, gains, cosine, sine_part)


def unturn_kernel(
    dq_ref, dk_ref, proj_ref, factor_ref, gain_ref, cos_ref, sin_ref, out_ref, mix_ref, sum_ref
):
    width = dq_ref.shape[1]
    cosine, sine_part = cos_ref[...], sin_ref[...]

    @pl.when(pl.program_id(0) == 0)
    def _():
        sum_ref[...] = jnp.zeros_like(sum_ref)

    for part, grad_ref in enumerate((dq_ref, dk_ref)):
        factor = columns_of(factor_ref[part : part + 1, :])
        mixed = None
        for h in range(0, width, HEAD_DIM):
            at = part * width + h
            grad = grad_ref[:, h : h + HEAD_DIM]
            turned = grad * cosine - halves_swapped(grad) * sine_part
            raw = proj_ref[:, at : at + HEAD_DIM]
            sums = jnp.sum(turned * raw * factor, axis=0, keepdims=True)
            sum_ref[part : part + 1, h : h + HEAD_DIM] += sums
            weighted = turned * gain_ref[part : part + 1, h : h + HEAD_DIM]
            out_ref[:, at : at + HEAD_DIM] = weighted
            mixed = weighted * raw if mixed is None else mixed + weighted * raw
        mix_ref[part : part + 1, :] = jnp.sum(mixed.T, axis=0, keepdims=True)


def unturn(query_grad, key_grad, projected, factors, gains, cosine, sine_part):
    length, width = query_grad.shape
    return pl.pallas_call(
        unturn_kernel,
        grid=(length // 512,),
        in_specs=[
            row_block(width),
            row_block(width),
            row_block(3 * width),
            lane_block(2),
            whole_block(2, width),
            row_block(HEAD_DIM),
            row_block(HEAD_DIM),
        ],
        out_specs=[row_block(2 * width), lane_block(2), whole_block(2, width)],
        out_shape=[
            jax.ShapeDtypeStruct((length, 2 * width), f32),
            jax.ShapeDtypeStruct((2, length), f32),
            jax.ShapeDtypeStruct((2, width), f32),
        ],
        name="unturn",
    )(query_grad, key_grad, projected, factors, gains, cosine, sine_part)


def finish_kernel(weighted_ref, proj_ref, factor_ref, mix_ref, dv_ref, out_ref):
    width = dv_ref.shape[1]
    for part in range(2):
        factor = columns_of(factor_ref[part : part + 1, :])
        mixing = columns_of(mix_ref[part : part + 1, :])
        for h in range(0, width, HEAD_DIM):
            at = pl.ds(part * width + h, HEAD_DIM)
            grad = weighted_ref[:, at] - proj_ref[:, at] * factor * factor * mixing
            out_ref[:, at] = (factor * grad).astype(bf16)
    out_ref[:, 2 * width :] = dv_ref[...].astype(bf16)


def finish(weighted, projected, factors, mixing, value_grad):
    length, width = value_grad.shape
    return pl.pallas_call(
        finish_kernel,
        grid=(length // 512,),
        in_specs=[
            row_block(2 * width),
            row_block(3 * width),
            lane_block(2),
            lane_block(2),
            row_block(width),
        ],
        out_specs=row_block(3 * width),
        out_shape=jax.ShapeDtypeStruct((length, 3 * width), bf16),
        name="finish",
    )(weighted, projected, factors, mixing, value_grad)


def norm_forward(values, gain_row):
    factor = lax.rsqrt(jnp.mean(values * values, axis=-1, keepdims=True) + norm_epsilon)
    return (values * factor * gain_row, factor)


def norm_backward(values, factor, gain_row, incoming):
    weighted = incoming * gain_row
    mixing = jnp.mean(weighted * values, axis=-1, keepdims=True)
    return (
        factor * (weighted - values * factor * factor * mixing),
        jnp.sum(incoming * values * factor, axis=0),
    )


def arrange(lengths, positions):
    finish = jnp.cumsum(lengths)
    has_ended = finish[None, :] <= positions[:, None]
    return jnp.sum(jnp.where(has_ended, lengths[None, :], 0), axis=1).astype(jnp.int32)


def scatter_over(value, axes):
    return lax.psum_scatter(value.astype(bf16), axes, scatter_dimension=0, tiled=True)


def on_device(
    hidden_in, seq_lengths, qkv_weight, out_weight, in_weight, down_weight, norm_gains, upstream
):
    piece_len, model_width = hidden_in.shape[1:]
    line_sizes = sizes_of(LINE)
    line = line_sizes[0] * line_sizes[1]
    length = piece_len * line * 2
    width = D // (line * 2)
    core = lax.axis_index("c")
    ctx_place = linear([lax.axis_index(a) for a in CTX], sizes_of(CTX))
    data_place = linear([lax.axis_index(a) for a in DATA], sizes_of(DATA))
    line_place = linear([lax.axis_index(a) for a in LINE], line_sizes)
    lengths = lax.dynamic_index_in_dim(seq_lengths, data_place, 0, keepdims=False)
    places = jnp.arange(length, dtype=jnp.int32)
    starts = arrange(lengths, places)
    offset = (places - starts).astype(f32)
    lows = starts[::BLOCK_Q] // BLOCK_K
    starts_row = starts.reshape(1, length)
    inverse = rope_base ** (-2.0 * jnp.arange(HEAD_DIM // 2, dtype=f32) / HEAD_DIM)
    angles = offset[:, None] * inverse[None, :]
    cosine, sine_part = jnp.cos(angles), jnp.sin(angles)
    cosine = jnp.concatenate([cosine, cosine], axis=1)
    sine_part = jnp.concatenate([-sine_part, sine_part], axis=1)

    own_input = hidden_in.reshape(piece_len, model_width)

    row = Line(LINE)

    row_count = qkv_weight.shape[0]
    owners = line * 2
    data_count = sizes_of(DATA)[0] * sizes_of(DATA)[1]
    buffer = [jnp.zeros((line, 2, piece_len, model_width), bf16)]

    def keep_input(k, same, other):
        for at_core, block, at in ((core, same, k), (1 - core, other, k - 1)):
            if block is not None:
                buffer[0] = lax.dynamic_update_slice(
                    buffer[0], block[None, None], (row.served(at), at_core, 0, 0)
                )
        return ()

    def weights_step(slot, tied):
        if slot == 0:
            blocks = spread(qkv_weight, 3, owners)
            return (exchange(blocks.reshape(line, 2, row_count, 3 * width), LINE),)
        if slot == 1:
            down = lax.all_gather(down_weight, DATA, axis=0, tiled=True)
            out_line = jnp.zeros((line,) + out_weight.shape, bf16)
            for steps in offsets(LINE):
                out_line = put(out_line, shift(out_weight, LINE, steps), place(LINE, steps, -1))
            return (down, out_line)
        if slot == 2:
            blocks = spread(in_weight, 2 * data_count, owners)
            return (exchange_cores(blocks.reshape((line, 2) + blocks.shape[1:])),)
        if slot == line - 1:
            return tied[2]
        return ()

    _, tied = row.gather(own_input, keep_input, weights_step)
    full_input = buffer[0].reshape(length, model_width)
    qkv_here = lax.all_gather(tied[0][0].reshape(-1, 3 * width), DATA, axis=0, tiled=True)
    down_here, out_line = tied[1]
    units = down_here.shape[0]
    out_half = lax.all_gather(out_line.reshape(-1, D), DATA, axis=0, tiled=True)
    in_rows = exchange_chips(tied[line - 1][0], LINE)

    projected, squares = project(full_input, qkv_here)
    factors = lax.rsqrt(small_sum(squares, CTX) / D + norm_epsilon)
    gains_here = lax.dynamic_slice(norm_gains, (0, ctx_place * width), (2, width))
    query_low, key_low, value_low = turn(projected, factors, gains_here, cosine, sine_part)
    head_out, log_total = attend(lows, starts_row, query_low, key_low, value_low)
    head_out, in_rows = together(head_out, in_rows)
    in_here = lax.all_gather(in_rows.reshape(-1, in_rows.shape[-1]), DATA, axis=0, tiled=True)

    pairs = exchange_cores(head_out.astype(bf16).reshape(line, 2, piece_len, width))
    pairs, out_half = together(pairs, out_half)
    attended = exchange_chips(pairs, LINE)
    out_half = out_half.reshape(-1, out_weight.shape[0], D)
    out_full = by_core(out_half, swap(out_half)).reshape(D, D)
    attended_low = attended.reshape(line * 2, piece_len, width).transpose(1, 0, 2)
    attended_low = attended_low.reshape(piece_len, D)
    branch = product(attended_low, out_full)
    branch_normed, branch_factor = norm_forward(branch, norm_gains[2])
    residual = own_input.astype(f32) + branch_normed
    residual_low = residual.astype(bf16)

    def rows_of(same, other):
        return jnp.concatenate([b for b in (same, other) if b is not None], axis=0)

    def chip_sums(results):
        def parts(k):
            return scatter_sum(results[k][-1][:piece_len], results[k + 1][-1][-piece_len:])

        return parts

    def forward_chip(k, same, other):
        rows = rows_of(same, other)
        gate_up = product(rows, in_here)
        gate_part, up_part = gate_up[:, :units], gate_up[:, units:]
        hidden = (gate_part * jax.nn.sigmoid(gate_part) * up_part).astype(bf16)
        return rows, gate_up, hidden, product(hidden, down_here).astype(bf16)

    plan = [[], [], [0, 1, 2]] + [[k] for k in range(3, line)]
    forward, _ = row.gather(residual_low, forward_chip, plan=plan)
    second, _ = row.scatter(chip_sums(forward))
    second_normed, second_factor = norm_forward(second, norm_gains[3])
    result = residual + second_normed
    live_places = ctx_place * piece_len + jnp.arange(piece_len, dtype=jnp.int32)
    live_rows = (live_places < jnp.sum(lengths)).astype(f32)[:, None]
    sums = jnp.stack(
        [
            jnp.sum(result * result * live_rows),
            jnp.sum(branch * branch * live_rows),
            jnp.sum(second * second * live_rows),
        ]
    )

    incoming = upstream.reshape(piece_len, model_width).astype(f32)
    second_grad, second_gain_grad = norm_backward(second, second_factor, norm_gains[3], incoming)

    def backward_chip(k, same, other):
        rows = rows_of(same, other)
        gate_up = forward[k][1]
        hidden_grad = product_right(rows, down_here)
        gate_part, up_part = gate_up[:, :units], gate_up[:, units:]
        sigmoid_gate = jax.nn.sigmoid(gate_part)
        gate_grad = hidden_grad * up_part * sigmoid_gate * (1.0 + gate_part * (1.0 - sigmoid_gate))
        up_grad = hidden_grad * gate_part * sigmoid_gate
        gate_up_low = jnp.concatenate([gate_grad, up_grad], axis=1).astype(bf16)
        return rows, gate_up_low, product_right(gate_up_low, in_here).astype(bf16)

    backward, _ = row.gather(second_grad.astype(bf16), backward_chip)

    def weight_grads(slot, tied):
        if slot == 1:
            gate_up_all = jnp.concatenate([b[1] for b in backward], axis=0)
            residual_all = jnp.concatenate([f[0] for f in forward], axis=0)
            return (product_left(residual_all, gate_up_all).astype(bf16),)
        if slot == 2:
            hidden_all = jnp.concatenate([f[2] for f in forward], axis=0)
            second_grad_all = jnp.concatenate([b[0] for b in backward], axis=0)
            return (product_left(hidden_all, second_grad_all).astype(bf16),)
        return ()

    residual_part, tied = row.scatter(chip_sums(backward), weight_grads)
    grad_in, grad_down = tied[0][0], tied[1][0]
    residual_grad = incoming + residual_part
    grad_in = scatter_over(grad_in, DATA).reshape(in_rows.shape)
    grad_down = scatter_over(grad_down, DATA).astype(f32)

    branch_grad, branch_gain_grad = norm_backward(
        branch, branch_factor, norm_gains[2], residual_grad
    )
    branch_grad_low = branch_grad.astype(bf16)
    attended_grad = product_right(branch_grad_low, out_full).astype(bf16)
    attended_grad = attended_grad.reshape(piece_len, line, 2, width).transpose(1, 2, 0, 3)
    pairs, branch_grad_low = together(exchange_cores(attended_grad), branch_grad_low)
    head_grad = exchange_chips(pairs, LINE).reshape(length, width)

    out_grad = product_left(attended_low, branch_grad_low).astype(bf16)
    out_grad = out_grad.reshape(-1, 2, out_weight.shape[0], D)
    out_keep, out_got = pick(out_grad, core, 1), swap(pick(out_grad, 1 - core, 1))
    in_pairs = exchange_cores(grad_in.reshape((line, 2) + in_rows.shape[2:]))
    head_grad, in_pairs = together(head_grad, in_pairs)
    grad_in = exchange_chips(in_pairs, LINE)

    query_grad, key_grad, value_grad = attend_back(
        lows, starts_row, query_low, key_low, value_low, head_out, log_total, head_grad
    )
    query_grad, out_keep = together(query_grad, out_keep)
    out_grad = (out_keep.astype(f32) + out_got.astype(f32)).astype(bf16).reshape(D // 2, D)
    out_grad = scatter_over(out_grad, DATA).reshape((line,) + out_weight.shape)
    weighted, mixing, gain_grads = unturn(
        query_grad, key_grad, projected, factors, gains_here, cosine, sine_part
    )
    mixing, grad_down = together(mixing, grad_down)
    mixing = small_sum(mixing, CTX) / D
    projected_grad = finish(weighted, projected, factors, mixing, value_grad)

    grad_blocks = projected_grad.reshape(line, 2, piece_len, 3 * width)

    later = []

    def input_chip(k):
        rows = pick(grad_blocks, row.served(k))
        rows = jnp.concatenate([pick(rows, core), pick(rows, 1 - core)], axis=0)
        part = product_right(rows, qkv_here).astype(bf16)
        part = scatter_sum(part[:piece_len], part[piece_len:])
        if not later:
            part, grads = together(part, projected_grad)
            later.append(grads)
        return part

    gain_rows = jnp.zeros((5, D), f32)
    gain_rows = lax.dynamic_update_slice(gain_rows, gain_grads, (0, ctx_place * width))
    gain_rows = gain_rows.at[2].set(branch_gain_grad).at[3].set(second_gain_grad)
    gain_rows = gain_rows.at[4, :3].set(sums)

    def last_grads(slot, tied):
        if slot == 1:
            part = product_left(full_input, later[0]).astype(bf16)
            return (part, small_sum(gain_rows, AXES[2:]), out_grad, grad_in)
        if slot == 2:
            return (scatter_over(tied[0][0], DATA), small_sum(tied[0][1], AXES[:2]))
        if slot == line - 1:
            blocks = tied[1][0].reshape(line, 2, row_count, 3 * width)
            return (exchange_cores(blocks),)
        return ()

    input_part, tied = row.scatter(input_chip, last_grads)
    (_, _, out_grad, grad_in), (_, gain_rows), (grad_qkv,) = tied[0], tied[1], tied[line - 2]
    input_grad = residual_grad + input_part
    grad_in = collect(grad_in.reshape((owners,) + grad_in.shape[2:]), 2 * data_count)
    grad_qkv = exchange_chips(grad_qkv, LINE)
    grad_qkv = collect(grad_qkv.reshape(owners, row_count, 3 * width), 3)
    grad_out = None
    for steps in offsets(LINE):
        part = shift(pick(out_grad, place(LINE, steps)), LINE, steps).astype(f32)
        grad_out = part if grad_out is None else grad_out + part

    live_count = jnp.sum(seq_lengths).astype(f32)
    rms_values = jnp.sqrt(gain_rows[4, :3] / (live_count * model_width))
    return (
        result.astype(bf16)[None],
        input_grad[None],
        grad_qkv,
        grad_out,
        grad_in,
        grad_down,
        gain_rows[:4],
        rms_values,
    )


def solution(mesh):
    dp, ctx = mesh.shape["dp"], mesh.shape["ctx"]
    fine = Mesh(mesh.devices.reshape(2, dp // 2, 2, ctx // 4, 2), AXES)
    return jax.shard_map(
        on_device,
        mesh=fine,
        in_specs=(
            P(DATA, CTX, None),
            P(),
            P(AXES, None),
            P(AXES, None),
            P(AXES, None),
            P(AXES, None),
            P(),
            P(DATA, CTX, None),
        ),
        out_specs=(
            P(DATA, CTX, None),
            P(DATA, CTX, None),
            P(AXES, None),
            P(AXES, None),
            P(AXES, None),
            P(AXES, None),
            P(),
            P(),
        ),
        check_vma=False,
    )
```

```python
import itertools

import jax
import jax.numpy as jnp
import numpy as np
from jax import lax
from jax.experimental import pallas as pl
from jax.experimental.pallas import tpu as pltpu
from jax.sharding import Mesh
from jax.sharding import PartitionSpec as P

D = 2048
HEADS = 16
HEAD_DIM = 128
FF = 8192

norm_epsilon = 1e-06
rope_base = 500000.0
masked_score = -1e30
scale_factor = HEAD_DIM ** (-0.5)

AXES = ("dh", "dl", "zh", "zl", "c")
DATA = ("dh", "dl")
LINE = ("zh", "zl")
CTX = ("zh", "zl", "c")

BLOCK_Q = 512
BLOCK_K = 512

bf16 = jnp.bfloat16
f32 = jnp.float32


def sizes_of(axes):
    return tuple(lax.axis_size(a) for a in axes)


def offsets(axes):
    return list(itertools.product(*[range(n) for n in sizes_of(axes)]))


def linear(index, sizes):
    total = 0
    for i, n in zip(index, sizes):
        total = total * n + i
    return total


def shift(value, axes, steps):
    if not any(steps):
        return value
    sizes = sizes_of(axes)
    pairs = []
    for index in itertools.product(*[range(n) for n in sizes]):
        target = tuple((i + s) % n for i, s, n in zip(index, steps, sizes))
        pairs.append((linear(index, sizes), linear(target, sizes)))
    return lax.ppermute(value, axes, pairs)


def swap(value):
    return lax.ppermute(value, "c", [(0, 1), (1, 0)])


def place(axes, steps, sign=1):
    sizes = sizes_of(axes)
    here = [(lax.axis_index(a) + sign * s) % n for a, s, n in zip(axes, steps, sizes)]
    return linear(here, sizes)


def pick(value, index, axis=0):
    return lax.dynamic_index_in_dim(value, index, axis, keepdims=False)


def put(buffer, value, index):
    return lax.dynamic_update_slice_in_dim(buffer, value[None], index, 0)


def together(*values):
    return lax.optimization_barrier(values)


def line_order(count):
    return np.array(
        [sorted(range(count), key=lambda j: (abs(i - j), j != i ^ 1)) for i in range(count)],
        dtype=np.int32,
    )


class Line:
    def __init__(self, axes):
        self.axes = axes
        sizes = sizes_of(axes)
        self.count = sizes[0] * sizes[1]
        self.place = linear([lax.axis_index(a) for a in axes], sizes)
        self.order = line_order(self.count)

    def served(self, k):
        return jnp.asarray(self.order[:, k])[self.place]

    def hop(self, value, step, keep=lambda i: True):
        pairs = [
            (i, i + step) for i in range(self.count) if 0 <= i + step < self.count and keep(i)
        ]
        return lax.ppermute(value, self.axes, pairs)

    def choose(self, options, wanted):
        used = sorted({w for w in wanted if w is not None})
        value = options[used[0]]
        for w in used[1:]:
            mask = np.array([v == w for v in wanted])
            value = jnp.where(jnp.asarray(mask)[self.place], options[w], value)
        return value

    def gather(self, block, work, extra=None, plan=None, late=False):
        plan = plan or [[k] for k in range(self.count - 1)]
        plan = plan + [[]]
        options, results, tied, arrived, swapped = {}, [], [], [], [None]
        for slot in range(self.count):
            if slot:
                wanted = []
                for i in range(self.count):
                    j = self.order[i, slot]
                    wanted.append((1, i - j) if j < i else (-1, j - i))
                arrived.append(self.choose(options, wanted))
            else:
                arrived.append(block)
            moved = ()
            if slot + 1 < self.count:
                moved = tuple(
                    self.hop(options[(step, slot)] if slot else block, step) for step in (1, -1)
                )
            other = swap(arrived[slot])
            done = [work(k, arrived[k], swapped[k]) for k in plan[slot]]
            more = extra(slot, tied) if extra else ()
            moved, other, done, more = together(moved, other, done, more)
            if moved:
                options[(1, slot + 1)], options[(-1, slot + 1)] = moved
            swapped.append(other)
            tied.append(more)
            results += done
        last = self.count - 1
        results.append(work(last, arrived[last], swapped[self.count]))
        if not late:
            results.append(work(self.count, None, swapped[last]))
        else:
            results.append(lambda gate: self.later(work, swapped[last], gate))
        return results, tied

    def later(self, work, block, gate):
        gate, block = together(gate, block)
        return gate, lambda: work(self.count, None, block)

    def scatter(self, parts, fill=None):
        count = self.count
        made = {count - 1: parts(count - 1)}
        last = {1: None, -1: None}
        tied = []
        for slot in range(1, count):
            far = count - slot
            moved = []
            for step in (1, -1):
                wanted = []
                for i in range(count):
                    j = i + step * far
                    wanted.append(int(np.argmax(self.order[i] == j)) if 0 <= j < count else None)
                value = self.choose(made, wanted)
                if last[step] is not None:
                    value = value.astype(f32) + last[step].astype(f32)
                keep = lambda i: 0 <= i + step * far < count
                moved.append(self.hop(value.astype(bf16), step, keep))
            done = parts(far - 1)
            more = fill(slot, tied) if fill else ()
            moved, done, more = together(moved, done, more)
            tied.append(more)
            made[far - 1] = done
            last[1], last[-1] = moved
        total = made[0].astype(f32) + last[1].astype(f32) + last[-1].astype(f32)
        return total, tied


def scatter_sum(for_same, for_other):
    return (for_same.astype(f32) + swap(for_other.astype(bf16)).astype(f32)).astype(bf16)


def cores_start(blocks):
    core = lax.axis_index("c")
    return pick(blocks, core, 1), swap(pick(blocks, 1 - core, 1))


def exchange_cores(blocks):
    return by_core(*cores_start(blocks))


def by_core(mine, other):
    shape = (mine.shape[0], 2) + mine.shape[1:]
    here = lax.broadcasted_iota(jnp.int32, shape, 1) == lax.axis_index("c")
    return jnp.where(here, mine[:, None], other[:, None])


def assemble_kernel(*refs):
    out_ref = refs[-1]
    for i, piece in enumerate(refs[1:-1]):

        @pl.when(pl.program_id(0) == i)
        def _(piece=piece):
            out_ref[0] = piece[...]


def assemble(pieces, places):
    shape = pieces[0].shape
    block = pl.BlockSpec(shape, lambda i, places: (0,) * len(shape))
    return pl.pallas_call(
        assemble_kernel,
        grid_spec=pltpu.PrefetchScalarGridSpec(
            num_scalar_prefetch=1,
            grid=(len(pieces),),
            in_specs=[block] * len(pieces),
            out_specs=pl.BlockSpec((1,) + shape, lambda i, places: (places[i],) + (0,) * len(shape)),
        ),
        out_shape=jax.ShapeDtypeStruct((len(pieces),) + shape, pieces[0].dtype),
        compiler_params=pltpu.CompilerParams(vmem_limit_bytes=32 << 20),
        cost_estimate=cost(2),
        name="assemble",
    )(jnp.stack(places).astype(jnp.int32), *pieces)


def shifts(value_for, chips):
    return tuple(shift(value_for(steps), chips, steps) for steps in offsets(chips))


def by_source(pieces, chips):
    return assemble(pieces, [place(chips, steps, -1) for steps in offsets(chips)])


def chips_start(pairs, chips):
    return shifts(lambda steps: pick(pairs, place(chips, steps)), chips)


def exchange_chips(pairs, chips):
    return by_source(chips_start(pairs, chips), chips)


def exchange(blocks, chips):
    return exchange_chips(exchange_cores(blocks), chips)


def small_sum(value, axes):
    for axis in axes:
        if lax.axis_size(axis) == 2:
            value = value + lax.ppermute(value, axis, [(0, 1), (1, 0)])
        else:
            value = lax.psum(value, axis)
    return value


def product(left_side, right_side):
    return jnp.dot(left_side, right_side, preferred_element_type=f32)


def product_left(left_side, right_side):
    return lax.dot_general(
        left_side, right_side, (((0,), (0,)), ((), ())), preferred_element_type=f32
    )


def product_right(left_side, right_side):
    return lax.dot_general(
        left_side, right_side, (((1,), (1,)), ((), ())), preferred_element_type=f32
    )


def cost(microseconds):
    return pl.CostEstimate(
        flops=int(microseconds * 1.0e9),
        transcendentals=0,
        bytes_accessed=int(microseconds * 3.0e6),
    )


def allowed_keys(shape, key_start, query_start, starts):
    key_place = key_start + lax.broadcasted_iota(jnp.int32, shape, 0)
    query_place = query_start + lax.broadcasted_iota(jnp.int32, shape, 1)
    return (key_place >= starts) & (key_place <= query_place)


def attend_kernel(low_ref, starts_ref, q_ref, k_ref, v_ref, out_ref, log_ref):
    block = pl.program_id(1)
    bq, bk = q_ref.shape[0], BLOCK_K
    queries, starts = q_ref[...], starts_ref[...]

    def step(j, carry):
        top, total, acc = carry
        rows = pl.ds(pl.multiple_of(j * bk, bk), bk)
        scores = product_right(k_ref[rows, :], queries) * scale_factor
        ok = allowed_keys(scores.shape, j * bk, block * bq, starts)
        scores = jnp.where(ok, scores, masked_score)
        new_top = jnp.maximum(top, jnp.max(scores, axis=0, keepdims=True))
        ratio = jnp.exp(top - new_top)
        expanded = jnp.exp(scores - new_top)
        total = total * ratio + jnp.sum(expanded, axis=0, keepdims=True)
        acc = acc * ratio + product_left(v_ref[rows, :], expanded.astype(bf16))
        return (new_top, total, acc)

    init = (
        jnp.full((1, bq), masked_score, f32),
        jnp.zeros((1, bq), f32),
        jnp.zeros((HEAD_DIM, bq), f32),
    )
    top, total, acc = lax.fori_loop(low_ref[block], (block * bq + bq) // bk, step, init)
    out_ref[...] = (acc / total).T
    log_ref[0] = top + jnp.log(total)


def attend(lows, starts, queries, keys, values):
    length, width = queries.shape
    heads, bq = width // HEAD_DIM, BLOCK_Q
    return pl.pallas_call(
        attend_kernel,
        grid_spec=pltpu.PrefetchScalarGridSpec(
            num_scalar_prefetch=1,
            grid=(heads, length // bq),
            in_specs=[
                pl.BlockSpec((1, bq), lambda h, i, low: (0, i)),
                pl.BlockSpec((bq, HEAD_DIM), lambda h, i, low: (i, h)),
                pl.BlockSpec((length, HEAD_DIM), lambda h, i, low: (0, h)),
                pl.BlockSpec((length, HEAD_DIM), lambda h, i, low: (0, h)),
            ],
            out_specs=[
                pl.BlockSpec((bq, HEAD_DIM), lambda h, i, low: (i, h)),
                pl.BlockSpec((1, 1, bq), lambda h, i, low: (h, 0, i)),
            ],
        ),
        out_shape=[
            jax.ShapeDtypeStruct((length, width), f32),
            jax.ShapeDtypeStruct((heads, 1, length), f32),
        ],
        compiler_params=pltpu.CompilerParams(vmem_limit_bytes=48 << 20),
        cost_estimate=cost(16),
        name="attend",
    )(lows, starts, queries, keys, values)


def attend_back_kernel(
    low_ref, starts_ref, q_ref, k_ref, v_ref, out_ref, log_ref, grad_ref, dq_ref, dk_ref, dv_ref
):
    length = q_ref.shape[0]
    bq, bk = BLOCK_Q, BLOCK_K
    dk_ref[...] = jnp.zeros_like(dk_ref)
    dv_ref[...] = jnp.zeros_like(dv_ref)

    def query_step(i, carry):
        queries_at = pl.ds(pl.multiple_of(i * bq, bq), bq)
        queries, grads = q_ref[queries_at, :], grad_ref[queries_at, :]
        starts = starts_ref[:, queries_at]
        log_total = log_ref[0, :, queries_at]
        inner = jnp.sum((grads.astype(f32) * out_ref[queries_at, :]).T, axis=0, keepdims=True)

        def step(j, acc):
            rows = pl.ds(pl.multiple_of(j * bk, bk), bk)
            keys = k_ref[rows, :]
            scores = product_right(keys, queries) * scale_factor
            ok = allowed_keys(scores.shape, j * bk, i * bq, starts)
            probs = jnp.where(ok, jnp.exp(scores - log_total), 0.0)
            dv_ref[rows, :] += product(probs.astype(bf16), grads)
            prob_grad = product_right(v_ref[rows, :], grads)
            score_grad = (probs * (prob_grad - inner)).astype(bf16)
            dk_ref[rows, :] += product(score_grad, queries) * scale_factor
            return acc + product_left(keys, score_grad)

        acc = lax.fori_loop(
            low_ref[i], (i * bq + bq) // bk, step, jnp.zeros((HEAD_DIM, bq), f32)
        )
        dq_ref[queries_at, :] = (acc * scale_factor).T
        return carry

    lax.fori_loop(0, length // bq, query_step, 0)


def attend_back(lows, starts, queries, keys, values, out, log_total, grads):
    length, width = queries.shape
    heads = width // HEAD_DIM
    column = pl.BlockSpec((length, HEAD_DIM), lambda h, low: (0, h))
    return pl.pallas_call(
        attend_back_kernel,
        grid_spec=pltpu.PrefetchScalarGridSpec(
            num_scalar_prefetch=1,
            grid=(heads,),
            in_specs=[
                pl.BlockSpec((1, length), lambda h, low: (0, 0)),
                column,
                column,
                column,
                column,
                pl.BlockSpec((1, 1, length), lambda h, low: (h, 0, 0)),
                column,
            ],
            out_specs=[column, column, column],
        ),
        out_shape=[jax.ShapeDtypeStruct((length, width), f32)] * 3,
        compiler_params=pltpu.CompilerParams(vmem_limit_bytes=56 << 20),
        cost_estimate=cost(26),
        name="attend_back",
    )(lows, starts, queries, keys, values, out, log_total, grads)


def spread_kernel(in_ref, out_ref):
    unit = out_ref.shape[2]
    for k in range(out_ref.shape[0]):
        out_ref[k] = in_ref[:, k * unit : (k + 1) * unit]


def spread(weight, groups, owners):
    rows, columns = weight.shape
    unit = columns // (groups * owners)
    if unit % 128:
        shaped = weight.reshape(rows, groups, owners, unit).transpose(2, 0, 1, 3)
        return shaped.reshape(owners, rows, groups * unit)
    return pl.pallas_call(
        spread_kernel,
        grid=(groups,),
        in_specs=[pl.BlockSpec((rows, owners * unit), lambda g: (0, g))],
        out_specs=pl.BlockSpec((owners, rows, unit), lambda g: (0, 0, g)),
        out_shape=jax.ShapeDtypeStruct((owners, rows, groups * unit), weight.dtype),
        cost_estimate=cost(4),
        name="spread",
    )(weight)


def collect_kernel(in_ref, out_ref):
    unit = in_ref.shape[2]
    for k in range(in_ref.shape[0]):
        out_ref[:, k * unit : (k + 1) * unit] = in_ref[k].astype(f32)


def collect(blocks, groups):
    owners, rows, columns = blocks.shape
    unit = columns // groups
    if unit % 128:
        shaped = blocks.reshape(owners, rows, groups, unit).transpose(1, 2, 0, 3)
        return shaped.reshape(rows, groups * owners * unit).astype(f32)
    return pl.pallas_call(
        collect_kernel,
        grid=(groups,),
        in_specs=[pl.BlockSpec((owners, rows, unit), lambda g: (0, 0, g))],
        out_specs=pl.BlockSpec((rows, owners * unit), lambda g: (0, g)),
        out_shape=jax.ShapeDtypeStruct((rows, groups * owners * unit), f32),
        cost_estimate=cost(5),
        name="collect",
    )(blocks)


def columns_of(row):
    return jnp.broadcast_to(row, (HEAD_DIM, row.shape[1])).T


def halves_swapped(values):
    return pltpu.roll(values, HEAD_DIM // 2, 1)


def project_kernel(in_ref, weight_ref, out_ref, square_ref):
    width = out_ref.shape[1] // 3
    out = product(in_ref[...], weight_ref[...])
    out_ref[...] = out
    for part in range(2):
        total = None
        for h in range(0, width, HEAD_DIM):
            raw = out[:, part * width + h : part * width + h + HEAD_DIM]
            total = raw * raw if total is None else total + raw * raw
        square_ref[part : part + 1, :] = jnp.sum(total.T, axis=0, keepdims=True)


def project(inputs, weight):
    length, depth = inputs.shape
    columns = weight.shape[1]
    return pl.pallas_call(
        project_kernel,
        grid=(length // 256,),
        in_specs=[row_block(depth, 256), whole_block(depth, columns)],
        out_specs=[row_block(columns, 256), lane_block(2, 256)],
        out_shape=[
            jax.ShapeDtypeStruct((length, columns), f32),
            jax.ShapeDtypeStruct((2, length), f32),
        ],
        compiler_params=pltpu.CompilerParams(vmem_limit_bytes=32 << 20),
        cost_estimate=cost(10),
        name="project",
    )(inputs, weight)


def join_kernel(core_ref, full_ref, got_ref, out_ref):
    out_ref[...] = (full_ref[:, 0].astype(f32) + got_ref[...].astype(f32)).astype(bf16)


def join(full, got):
    count, _, rows, columns = full.shape
    step = 4 if count % 4 == 0 else 1
    part = pl.BlockSpec((step, rows, columns), lambda i, core: (i, 0, 0))
    return pl.pallas_call(
        join_kernel,
        grid_spec=pltpu.PrefetchScalarGridSpec(
            num_scalar_prefetch=1,
            grid=(count // step,),
            in_specs=[
                pl.BlockSpec((step, 1, rows, columns), lambda i, core: (i, core[0], 0, 0)),
                part,
            ],
            out_specs=part,
        ),
        out_shape=jax.ShapeDtypeStruct((count, rows, columns), bf16),
        cost_estimate=cost(4),
        name="join",
    )(lax.axis_index("c").astype(jnp.int32).reshape(1), full, got)


def turn_kernel(proj_ref, factor_ref, gain_ref, cos_ref, sin_ref, q_ref, k_ref, v_ref):
    width = q_ref.shape[1]
    cosine, sine_part = cos_ref[...], sin_ref[...]
    for part, out in enumerate((q_ref, k_ref)):
        factor = columns_of(factor_ref[part : part + 1, :])
        for h in range(0, width, HEAD_DIM):
            raw = proj_ref[:, part * width + h : part * width + h + HEAD_DIM]
            normed = raw * factor * gain_ref[part : part + 1, h : h + HEAD_DIM]
            turned = normed * cosine + halves_swapped(normed) * sine_part
            out[:, h : h + HEAD_DIM] = turned.astype(bf16)
    v_ref[...] = proj_ref[:, 2 * width :].astype(bf16)


def row_block(columns, rows=512):
    return pl.BlockSpec((rows, columns), lambda i: (i, 0))


def lane_block(lines, rows=512):
    return pl.BlockSpec((lines, rows), lambda i: (0, i))


def whole_block(*shape):
    return pl.BlockSpec(shape, lambda i: (0,) * len(shape))


def turn(projected, factors, gains, cosine, sine_part):
    length, columns = projected.shape
    width = columns // 3
    return pl.pallas_call(
        turn_kernel,
        grid=(length // 512,),
        in_specs=[
            row_block(columns),
            lane_block(2),
            whole_block(2, width),
            row_block(HEAD_DIM),
            row_block(HEAD_DIM),
        ],
        out_specs=[row_block(width)] * 3,
        out_shape=[jax.ShapeDtypeStruct((length, width), bf16)] * 3,
        cost_estimate=cost(6),
        name="turn",
    )(projected, factors, gains, cosine, sine_part)


def unturn_kernel(
    dq_ref, dk_ref, proj_ref, factor_ref, gain_ref, cos_ref, sin_ref, out_ref, mix_ref, sum_ref
):
    width = dq_ref.shape[1]
    cosine, sine_part = cos_ref[...], sin_ref[...]

    @pl.when(pl.program_id(0) == 0)
    def _():
        sum_ref[...] = jnp.zeros_like(sum_ref)

    for part, grad_ref in enumerate((dq_ref, dk_ref)):
        factor = columns_of(factor_ref[part : part + 1, :])
        mixed = None
        for h in range(0, width, HEAD_DIM):
            at = part * width + h
            grad = grad_ref[:, h : h + HEAD_DIM]
            turned = grad * cosine - halves_swapped(grad) * sine_part
            raw = proj_ref[:, at : at + HEAD_DIM]
            sums = jnp.sum(turned * raw * factor, axis=0, keepdims=True)
            sum_ref[part : part + 1, h : h + HEAD_DIM] += sums
            weighted = turned * gain_ref[part : part + 1, h : h + HEAD_DIM]
            out_ref[:, at : at + HEAD_DIM] = weighted
            mixed = weighted * raw if mixed is None else mixed + weighted * raw
        mix_ref[part : part + 1, :] = jnp.sum(mixed.T, axis=0, keepdims=True)


def unturn(query_grad, key_grad, projected, factors, gains, cosine, sine_part):
    length, width = query_grad.shape
    return pl.pallas_call(
        unturn_kernel,
        grid=(length // 512,),
        in_specs=[
            row_block(width),
            row_block(width),
            row_block(3 * width),
            lane_block(2),
            whole_block(2, width),
            row_block(HEAD_DIM),
            row_block(HEAD_DIM),
        ],
        out_specs=[row_block(2 * width), lane_block(2), whole_block(2, width)],
        out_shape=[
            jax.ShapeDtypeStruct((length, 2 * width), f32),
            jax.ShapeDtypeStruct((2, length), f32),
            jax.ShapeDtypeStruct((2, width), f32),
        ],
        cost_estimate=cost(7),
        name="unturn",
    )(query_grad, key_grad, projected, factors, gains, cosine, sine_part)


def finish_kernel(weighted_ref, proj_ref, factor_ref, mix_ref, dv_ref, out_ref):
    width = dv_ref.shape[1]
    for part in range(2):
        factor = columns_of(factor_ref[part : part + 1, :])
        mixing = columns_of(mix_ref[part : part + 1, :])
        for h in range(0, width, HEAD_DIM):
            at = pl.ds(part * width + h, HEAD_DIM)
            grad = weighted_ref[:, at] - proj_ref[:, at] * factor * factor * mixing
            out_ref[:, at] = (factor * grad).astype(bf16)
    out_ref[:, 2 * width :] = dv_ref[...].astype(bf16)


def finish(weighted, projected, factors, mixing, value_grad):
    length, width = value_grad.shape
    return pl.pallas_call(
        finish_kernel,
        grid=(length // 512,),
        in_specs=[
            row_block(2 * width),
            row_block(3 * width),
            lane_block(2),
            lane_block(2),
            row_block(width),
        ],
        out_specs=row_block(3 * width),
        out_shape=jax.ShapeDtypeStruct((length, 3 * width), bf16),
        cost_estimate=cost(7),
        name="finish",
    )(weighted, projected, factors, mixing, value_grad)


def norm_forward(values, gain_row):
    factor = lax.rsqrt(jnp.mean(values * values, axis=-1, keepdims=True) + norm_epsilon)
    return (values * factor * gain_row, factor)


def norm_backward(values, factor, gain_row, incoming):
    weighted = incoming * gain_row
    mixing = jnp.mean(weighted * values, axis=-1, keepdims=True)
    return (
        factor * (weighted - values * factor * factor * mixing),
        jnp.sum(incoming * values * factor, axis=0),
    )


def arrange(lengths, positions):
    finish = jnp.cumsum(lengths)
    has_ended = finish[None, :] <= positions[:, None]
    return jnp.sum(jnp.where(has_ended, lengths[None, :], 0), axis=1).astype(jnp.int32)


def scatter_over(value, axes):
    return lax.psum_scatter(value.astype(bf16), axes, scatter_dimension=0, tiled=True)


def on_device(
    hidden_in, seq_lengths, qkv_weight, out_weight, in_weight, down_weight, norm_gains, upstream
):
    piece_len, model_width = hidden_in.shape[1:]
    line_sizes = sizes_of(LINE)
    line = line_sizes[0] * line_sizes[1]
    length = piece_len * line * 2
    width = D // (line * 2)
    core = lax.axis_index("c")
    ctx_place = linear([lax.axis_index(a) for a in CTX], sizes_of(CTX))
    data_place = linear([lax.axis_index(a) for a in DATA], sizes_of(DATA))
    line_place = linear([lax.axis_index(a) for a in LINE], line_sizes)
    lengths = lax.dynamic_index_in_dim(seq_lengths, data_place, 0, keepdims=False)
    places = jnp.arange(length, dtype=jnp.int32)
    starts = arrange(lengths, places)
    offset = (places - starts).astype(f32)
    lows = starts[::BLOCK_Q] // BLOCK_K
    starts_row = starts.reshape(1, length)
    inverse = rope_base ** (-2.0 * jnp.arange(HEAD_DIM // 2, dtype=f32) / HEAD_DIM)
    angles = offset[:, None] * inverse[None, :]
    cosine, sine_part = jnp.cos(angles), jnp.sin(angles)
    cosine = jnp.concatenate([cosine, cosine], axis=1)
    sine_part = jnp.concatenate([-sine_part, sine_part], axis=1)

    own_input = hidden_in.reshape(piece_len, model_width)

    row = Line(LINE)

    row_count = qkv_weight.shape[0]
    owners = line * 2
    data_count = sizes_of(DATA)[0] * sizes_of(DATA)[1]
    buffer = [jnp.zeros((line, 2, piece_len, model_width), bf16)]

    def keep_input(k, same, other):
        of_other = k if k == line - 1 else k - 1 if k < line else line - 2
        for at_core, block, at in ((core, same, k), (1 - core, other, of_other)):
            if block is not None:
                buffer[0] = lax.dynamic_update_slice(
                    buffer[0], block[None, None], (row.served(at), at_core, 0, 0)
                )
        return ()

    def weights_step(slot, tied):
        if slot == 0:
            blocks = spread(qkv_weight, 3, owners)
            blocks = exchange_cores(blocks.reshape(line, 2, row_count, 3 * width))
            return (blocks, in_weight)
        if slot == 1:
            down = lax.all_gather(down_weight, DATA, axis=0, tiled=True)
            blocks = spread(tied[0][1], 2 * data_count, owners)
            in_cores = cores_start(blocks.reshape((line, 2) + blocks.shape[1:]))
            return (exchange_chips(tied[0][0], LINE), down, in_cores)
        if slot == line - 1:
            return (out_weight, tied[1][2])
        return ()

    _, tied = row.gather(own_input, keep_input, weights_step)
    full_input = buffer[0].reshape(length, model_width)
    qkv_here = lax.all_gather(tied[1][0].reshape(-1, 3 * width), DATA, axis=0, tiled=True)
    down_here = tied[1][1]
    units = down_here.shape[0]
    out_shuffled, (in_keep, in_got) = tied[line - 1]
    out_pieces = shifts(lambda steps: out_shuffled, LINE)

    projected, squares = project(full_input, qkv_here)
    squares, out_pieces, in_got = together(squares, out_pieces, in_got)
    out_line = by_source(out_pieces, LINE)
    out_half = lax.all_gather(out_line.reshape(-1, D), DATA, axis=0, tiled=True)
    in_pieces = chips_start(by_core(in_keep, in_got), LINE)
    factors = lax.rsqrt(small_sum(squares, CTX) / D + norm_epsilon)
    gains_here = lax.dynamic_slice(norm_gains, (0, ctx_place * width), (2, width))
    query_low, key_low, value_low = turn(projected, factors, gains_here, cosine, sine_part)
    head_out, log_total = attend(lows, starts_row, query_low, key_low, value_low)

    head_out, in_pieces, out_half = together(head_out, in_pieces, out_half)
    blocks = head_out.astype(bf16).reshape(line, 2, piece_len, width)
    keep, got = cores_start(blocks)
    out_half = out_half.reshape(-1, out_weight.shape[0], D)
    out_other = swap(out_half)
    in_rows = by_source(in_pieces, LINE)
    in_here = lax.all_gather(in_rows.reshape(-1, in_rows.shape[-1]), DATA, axis=0, tiled=True)
    attended = exchange_chips(by_core(keep, got), LINE)
    out_full = by_core(out_half, out_other).reshape(D, D)
    attended_low = attended.reshape(line * 2, piece_len, width).transpose(1, 0, 2)
    attended_low = attended_low.reshape(piece_len, D)
    branch = product(attended_low, out_full)
    branch_normed, branch_factor = norm_forward(branch, norm_gains[2])
    residual = own_input.astype(f32) + branch_normed
    residual_low = residual.astype(bf16)

    def rows_of(same, other):
        return jnp.concatenate([b for b in (same, other) if b is not None], axis=0)

    def chip_sums(results):
        def parts(k):
            same = results[k][-1][:piece_len]
            if k == line - 1:
                got = swap(results[k][-1][piece_len:])
                if callable(results[line]):
                    got, results[line] = results[line](got)
                return (same.astype(f32) + got.astype(f32)).astype(bf16)
            if k == line - 2 and callable(results[line]):
                results[line] = results[line]()
            return scatter_sum(same, results[line if k == line - 2 else k + 1][-1][-piece_len:])

        return parts

    def forward_chip(k, same, other):
        rows = rows_of(same, other)
        gate_up = product(rows, in_here)
        gate_part, up_part = gate_up[:, :units], gate_up[:, units:]
        hidden = (gate_part * jax.nn.sigmoid(gate_part) * up_part).astype(bf16)
        return rows, gate_up.astype(bf16), hidden, product(hidden, down_here).astype(bf16)

    plan = [[], [0], [1, 2]] + [[k] for k in range(3, line - 1)]
    forward, _ = row.gather(residual_low, forward_chip, plan=plan)
    def join_rows(slot, tied):
        if slot == 1:
            return ([f[0] for f in forward], [f[2] for f in forward])
        if slot == 2:
            return (jnp.concatenate(tied[0][0], axis=0), tied[0][1])
        if slot == 3:
            return (jnp.concatenate(tied[1][1], axis=0),)
        return ()

    second, tied = row.scatter(chip_sums(forward), join_rows)
    residual_all, hidden_all = tied[1][0], tied[2][0]
    second_normed, second_factor = norm_forward(second, norm_gains[3])
    result = residual + second_normed
    live_places = ctx_place * piece_len + jnp.arange(piece_len, dtype=jnp.int32)
    live_rows = (live_places < jnp.sum(lengths)).astype(f32)[:, None]
    sums = jnp.stack(
        [
            jnp.sum(result * result * live_rows),
            jnp.sum(branch * branch * live_rows),
            jnp.sum(second * second * live_rows),
        ]
    )

    incoming = upstream.reshape(piece_len, model_width).astype(f32)
    second_grad, second_gain_grad = norm_backward(second, second_factor, norm_gains[3], incoming)

    def backward_chip(k, same, other):
        rows = rows_of(same, other)
        gate_up = forward[k][1].astype(f32)
        hidden_grad = product_right(rows, down_here)
        gate_part, up_part = gate_up[:, :units], gate_up[:, units:]
        sigmoid_gate = jax.nn.sigmoid(gate_part)
        gate_grad = hidden_grad * up_part * sigmoid_gate * (1.0 + gate_part * (1.0 - sigmoid_gate))
        up_grad = hidden_grad * gate_part * sigmoid_gate
        gate_up_low = jnp.concatenate([gate_grad, up_grad], axis=1).astype(bf16)
        return rows, gate_up_low, product_right(gate_up_low, in_here).astype(bf16)

    backward, _ = row.gather(second_grad.astype(bf16), backward_chip)

    def weight_grads(slot, tied):
        if slot == 1:
            gate_up_all = jnp.concatenate([b[1] for b in backward], axis=0)
            grads = product_left(residual_all, gate_up_all).astype(bf16)
            return (grads, [b[0] for b in backward])
        if slot == 2:
            second_grad_all = jnp.concatenate(tied[0][1], axis=0)
            return (product_left(hidden_all, second_grad_all).astype(bf16),)
        return ()

    residual_part, tied = row.scatter(chip_sums(backward), weight_grads)
    grad_in, grad_down = tied[0][0], tied[1][0]
    residual_grad = incoming + residual_part
    grad_in = scatter_over(grad_in, DATA).reshape(in_rows.shape)
    grad_down = scatter_over(grad_down, DATA)

    branch_grad, branch_gain_grad = norm_backward(
        branch, branch_factor, norm_gains[2], residual_grad
    )
    branch_grad_low = branch_grad.astype(bf16)
    attended_grad = product_right(branch_grad_low, out_full).astype(bf16)
    attended_grad = attended_grad.reshape(piece_len, line, 2, width).transpose(1, 2, 0, 3)
    keep, give = pick(attended_grad, core, 1), pick(attended_grad, 1 - core, 1)
    give, branch_grad_low = together(give, branch_grad_low)
    out_grad = product_left(attended_low, branch_grad_low).astype(bf16)
    out_grad = out_grad.reshape(-1, 2, out_weight.shape[0], D)
    got, out_grad, grad_in = together(swap(give), out_grad, grad_in)
    pieces = chips_start(by_core(keep, got), LINE)
    in_keep, in_got = cores_start(grad_in.reshape((line, 2) + in_rows.shape[2:]))
    out_got = swap(pick(out_grad, 1 - core, 1))
    pieces, in_got, out_got = together(pieces, in_got, out_got)
    head_grad = by_source(pieces, LINE).reshape(length, width)
    in_pieces = chips_start(by_core(in_keep, in_got), LINE)
    out_grad = join(out_grad, out_got)
    head_grad, out_grad = together(head_grad, out_grad)
    out_grad = scatter_over(out_grad.reshape(D // 2, D), DATA)
    out_grad = out_grad.reshape((line,) + out_weight.shape)

    query_grad, key_grad, value_grad = attend_back(
        lows, starts_row, query_low, key_low, value_low, head_out, log_total, head_grad
    )
    weighted, mixing, gain_grads = unturn(
        query_grad, key_grad, projected, factors, gains_here, cosine, sine_part
    )
    mixing, in_pieces = together(mixing, in_pieces)
    mixing = small_sum(mixing, CTX) / D
    projected_grad = finish(weighted, projected, factors, mixing, value_grad)
    projected_grad, grad_down = together(projected_grad, grad_down)
    grad_blocks = projected_grad.reshape(line, 2, piece_len, 3 * width)

    later = []

    def input_chip(k):
        rows = pick(grad_blocks, row.served(k))
        rows = jnp.concatenate([pick(rows, core), pick(rows, 1 - core)], axis=0)
        part = product_right(rows, qkv_here).astype(bf16)
        part = scatter_sum(part[:piece_len], part[piece_len:])
        if not later:
            later.extend(together(part, projected_grad))
            part = later[0]
        return part

    def step(rows, axis):
        if lax.axis_size(axis) == 2:
            return (rows, lax.ppermute(rows, axis, [(0, 1), (1, 0)]))
        return (lax.psum(rows, axis),)

    def last_grads(slot, tied):
        if slot == 1:
            grads = product_left(full_input, later[1]).astype(bf16)
            return (grads, gain_grads, chips_start(out_grad, LINE))
        if slot == 2:
            rows = jnp.zeros((5, D), f32)
            rows = lax.dynamic_update_slice(rows, tied[0][1], (0, ctx_place * width))
            rows = rows.at[2].set(branch_gain_grad).at[3].set(second_gain_grad)
            rows = rows.at[4, :3].set(sums)
            return (scatter_over(tied[0][0], DATA), step(rows, "c"))
        if slot == line - 1:
            blocks = tied[1][0].reshape(line, 2, row_count, 3 * width)
            rows = step(sum(tied[1][1]), "zl")
            return (cores_start(blocks), rows, in_pieces, grad_down)
        return ()

    input_part, tied = row.scatter(input_chip, last_grads)
    qkv_cores, gain_rows, in_pieces, grad_down = tied[line - 2]
    out_pieces = tied[0][2]
    qkv_pieces = chips_start(by_core(*qkv_cores), LINE)
    gain_rows = small_sum(sum(gain_rows), ("zh", "dl", "dh"))
    input_grad = residual_grad + input_part
    grad_in = by_source(in_pieces, LINE)
    grad_in = collect(grad_in.reshape((owners,) + grad_in.shape[2:]), 2 * data_count)
    grad_down = grad_down.astype(f32)
    grad_out = sum(piece.astype(f32) for piece in out_pieces)
    qkv_pieces, grad_in, grad_down = together(qkv_pieces, grad_in, grad_down)
    grad_qkv = by_source(qkv_pieces, LINE)
    grad_qkv = collect(grad_qkv.reshape(owners, row_count, 3 * width), 3)
    live_count = jnp.sum(seq_lengths).astype(f32)
    rms_values = jnp.sqrt(gain_rows[4, :3] / (live_count * model_width))
    return (
        result.astype(bf16)[None],
        input_grad[None],
        grad_qkv,
        grad_out,
        grad_in,
        grad_down,
        gain_rows[:4],
        rms_values,
    )


def solution(mesh):
    dp, ctx = mesh.shape["dp"], mesh.shape["ctx"]
    fine = Mesh(mesh.devices.reshape(2, dp // 2, 2, ctx // 4, 2), AXES)
    return jax.shard_map(
        on_device,
        mesh=fine,
        in_specs=(
            P(DATA, CTX, None),
            P(),
            P(AXES, None),
            P(AXES, None),
            P(AXES, None),
            P(AXES, None),
            P(),
            P(DATA, CTX, None),
        ),
        out_specs=(
            P(DATA, CTX, None),
            P(DATA, CTX, None),
            P(AXES, None),
            P(AXES, None),
            P(AXES, None),
            P(AXES, None),
            P(),
            P(),
        ),
        check_vma=False,
    )
```

```python
import functools
import itertools

import jax
import jax.numpy as jnp
import numpy as np
from jax import lax
from jax.experimental import pallas as pl
from jax.experimental.pallas import tpu as pltpu
from jax.sharding import Mesh
from jax.sharding import PartitionSpec as P

D = 2048
HEADS = 16
HEAD_DIM = 128
FF = 8192

norm_epsilon = 1e-06
rope_base = 500000.0
masked_score = -1e30
scale_factor = HEAD_DIM ** (-0.5)

AXES = ("dh", "dl", "zh", "zl", "c")
DATA = ("dh", "dl")
LINE = ("zh", "zl")
CTX = ("zh", "zl", "c")

BLOCK_Q = 512
BLOCK_K = 512

bf16 = jnp.bfloat16
f32 = jnp.float32


def sizes_of(axes):
    return tuple(lax.axis_size(a) for a in axes)


def offsets(axes):
    return list(itertools.product(*[range(n) for n in sizes_of(axes)]))


def linear(index, sizes):
    total = 0
    for i, n in zip(index, sizes):
        total = total * n + i
    return total


def shift(value, axes, steps):
    if not any(steps):
        return value
    sizes = sizes_of(axes)
    pairs = []
    for index in itertools.product(*[range(n) for n in sizes]):
        target = tuple((i + s) % n for i, s, n in zip(index, steps, sizes))
        pairs.append((linear(index, sizes), linear(target, sizes)))
    return lax.ppermute(value, axes, pairs)


def swap(value):
    return lax.ppermute(value, "c", [(0, 1), (1, 0)])


def place(axes, steps, sign=1):
    sizes = sizes_of(axes)
    here = [(lax.axis_index(a) + sign * s) % n for a, s, n in zip(axes, steps, sizes)]
    return linear(here, sizes)


def pick(value, index, axis=0):
    return lax.dynamic_index_in_dim(value, index, axis, keepdims=False)


def put(buffer, value, index):
    return lax.dynamic_update_slice_in_dim(buffer, value[None], index, 0)


def together(*values):
    return lax.optimization_barrier(values)


def line_order(count):
    return np.array(
        [sorted(range(count), key=lambda j: (abs(i - j), j != i ^ 1)) for i in range(count)],
        dtype=np.int32,
    )


class Line:
    def __init__(self, axes):
        self.axes = axes
        sizes = sizes_of(axes)
        self.count = sizes[0] * sizes[1]
        self.place = linear([lax.axis_index(a) for a in axes], sizes)
        self.order = line_order(self.count)

    def served(self, k):
        return jnp.asarray(self.order[:, k])[self.place]

    def hop(self, value, step, keep=lambda i: True):
        pairs = [
            (i, i + step) for i in range(self.count) if 0 <= i + step < self.count and keep(i)
        ]
        return lax.ppermute(value, self.axes, pairs)

    def choose(self, options, wanted):
        used = sorted({w for w in wanted if w is not None})
        value = options[used[0]]
        for w in used[1:]:
            mask = np.array([v == w for v in wanted])
            value = jnp.where(jnp.asarray(mask)[self.place], options[w], value)
        return value

    def gather(self, block, work, extra=None, plan=None, swaps=None):
        last = self.count - 1
        plan = plan or [[k] for k in range(last)] + [[]]
        swaps = swaps or [[k] for k in range(last + 1)]
        options, results, tied, arrived, other = {}, [], [], [], {-1: None}
        for slot in range(self.count):
            if slot:
                wanted = []
                for i in range(self.count):
                    j = self.order[i, slot]
                    wanted.append((1, i - j) if j < i else (-1, j - i))
                arrived.append(self.choose(options, wanted))
            else:
                arrived.append(block)
            moved = ()
            if slot < last:
                moved = tuple(
                    self.hop(options[(step, slot)] if slot else block, step) for step in (1, -1)
                )
            swapped = [swap(arrived[k]) for k in swaps[slot]]
            done = [work(k, arrived[k], other[k - 1]) for k in plan[slot]]
            more = extra(slot, tied) if extra else ()
            moved, swapped, done, more = together(moved, swapped, done, more)
            if moved:
                options[(1, slot + 1)], options[(-1, slot + 1)] = moved
            other.update(zip(swaps[slot], swapped))
            tied.append(more)
            results += done
        results.append(work(last, arrived[last], other[last]))
        results.append(work(self.count, None, other[last - 1]))
        return results, tied

    def hop_values(self, made, far, last):
        wanted = {}
        for step in (1, -1):
            wanted[step] = []
            for i in range(self.count):
                j = i + step * far
                known = 0 <= j < self.count
                wanted[step].append(int(np.argmax(self.order[i] == j)) if known else None)
        values = []
        for step in (1, -1):
            value = self.choose(made, wanted[step])
            if last[step] is not None:
                value = value.astype(f32) + last[step].astype(f32)
            values.append(value.astype(bf16))
        return values

    def scatter(self, parts, fill=None, plan=None):
        count = self.count
        plan = plan or [[k] for k in range(count - 2, -1, -1)]
        made = {count - 1: parts(count - 1)}
        last = {1: None, -1: None}
        tied = []
        for slot in range(1, count):
            far = count - slot
            values = self.hop_values(made, far, last)
            moved = []
            for step, value in zip((1, -1), values):
                keep = lambda i: 0 <= i + step * far < count
                moved.append(self.hop(value, step, keep))
            done = [parts(k) for k in plan[slot - 1]]
            more = fill(slot, tied) if fill else ()
            moved, done, more = together(moved, done, more)
            tied.append(more)
            made.update(zip(plan[slot - 1], done))
            last[1], last[-1] = moved
        total = made[0].astype(f32) + last[1].astype(f32) + last[-1].astype(f32)
        return total, tied


def scatter_sum(for_same, for_other):
    return (for_same.astype(f32) + swap(for_other.astype(bf16)).astype(f32)).astype(bf16)


def cores_start(blocks):
    core = lax.axis_index("c")
    return pick(blocks, core, 1), swap(pick(blocks, 1 - core, 1))


def exchange_cores(blocks):
    return by_core(*cores_start(blocks))


def by_core(mine, other):
    shape = (mine.shape[0], 2) + mine.shape[1:]
    here = lax.broadcasted_iota(jnp.int32, shape, 1) == lax.axis_index("c")
    return jnp.where(here, mine[:, None], other[:, None])


def assemble_kernel(*refs):
    out_ref = refs[-1]
    for i, piece in enumerate(refs[1:-1]):

        @pl.when(pl.program_id(0) == i)
        def _(piece=piece):
            out_ref[0] = piece[...]


def assemble(pieces, places):
    shape = pieces[0].shape
    block = pl.BlockSpec(shape, lambda i, places: (0,) * len(shape))
    return pl.pallas_call(
        assemble_kernel,
        grid_spec=pltpu.PrefetchScalarGridSpec(
            num_scalar_prefetch=1,
            grid=(len(pieces),),
            in_specs=[block] * len(pieces),
            out_specs=pl.BlockSpec((1,) + shape, lambda i, places: (places[i],) + (0,) * len(shape)),
        ),
        out_shape=jax.ShapeDtypeStruct((len(pieces),) + shape, pieces[0].dtype),
        compiler_params=pltpu.CompilerParams(vmem_limit_bytes=32 << 20),
        cost_estimate=cost(2),
        name="assemble",
    )(jnp.stack(places).astype(jnp.int32), *pieces)


def shifts(value_for, chips):
    return tuple(shift(value_for(steps), chips, steps) for steps in offsets(chips))


def by_source(pieces, chips):
    return assemble(pieces, [place(chips, steps, -1) for steps in offsets(chips)])


def chips_start(pairs, chips):
    return shifts(lambda steps: pick(pairs, place(chips, steps)), chips)


def exchange_chips(pairs, chips):
    return by_source(chips_start(pairs, chips), chips)


def exchange(blocks, chips):
    return exchange_chips(exchange_cores(blocks), chips)


def small_sum(value, axes):
    for axis in axes:
        if lax.axis_size(axis) == 2:
            value = value + lax.ppermute(value, axis, [(0, 1), (1, 0)])
        else:
            value = lax.psum(value, axis)
    return value


def product(left_side, right_side):
    return jnp.dot(left_side, right_side, preferred_element_type=f32)


def product_left(left_side, right_side):
    return lax.dot_general(
        left_side, right_side, (((0,), (0,)), ((), ())), preferred_element_type=f32
    )


def product_right(left_side, right_side):
    return lax.dot_general(
        left_side, right_side, (((1,), (1,)), ((), ())), preferred_element_type=f32
    )


def cost(microseconds):
    return pl.CostEstimate(
        flops=int(microseconds * 1.0e9),
        transcendentals=0,
        bytes_accessed=int(microseconds * 3.0e6),
    )


def allowed_keys(shape, key_start, query_start, starts):
    key_place = key_start + lax.broadcasted_iota(jnp.int32, shape, 0)
    query_place = query_start + lax.broadcasted_iota(jnp.int32, shape, 1)
    return (key_place >= starts) & (key_place <= query_place)


def attend_kernel(low_ref, starts_ref, q_ref, k_ref, v_ref, out_ref, log_ref):
    block = pl.program_id(1)
    bq, bk = q_ref.shape[0], BLOCK_K
    queries, starts = q_ref[...], starts_ref[...]

    def step(j, carry):
        top, total, acc = carry
        rows = pl.ds(pl.multiple_of(j * bk, bk), bk)
        scores = product_right(k_ref[rows, :], queries) * scale_factor
        ok = allowed_keys(scores.shape, j * bk, block * bq, starts)
        scores = jnp.where(ok, scores, masked_score)
        new_top = jnp.maximum(top, jnp.max(scores, axis=0, keepdims=True))
        ratio = jnp.exp(top - new_top)
        expanded = jnp.exp(scores - new_top)
        total = total * ratio + jnp.sum(expanded, axis=0, keepdims=True)
        acc = acc * ratio + product_left(v_ref[rows, :], expanded.astype(bf16))
        return (new_top, total, acc)

    init = (
        jnp.full((1, bq), masked_score, f32),
        jnp.zeros((1, bq), f32),
        jnp.zeros((HEAD_DIM, bq), f32),
    )
    top, total, acc = lax.fori_loop(low_ref[block], (block * bq + bq) // bk, step, init)
    out_ref[...] = (acc / total).T
    log_ref[0] = top + jnp.log(total)


def attend(lows, starts, queries, keys, values):
    length, width = queries.shape
    heads, bq = width // HEAD_DIM, BLOCK_Q
    return pl.pallas_call(
        attend_kernel,
        grid_spec=pltpu.PrefetchScalarGridSpec(
            num_scalar_prefetch=1,
            grid=(heads, length // bq),
            in_specs=[
                pl.BlockSpec((1, bq), lambda h, i, low: (0, i)),
                pl.BlockSpec((bq, HEAD_DIM), lambda h, i, low: (i, h)),
                pl.BlockSpec((length, HEAD_DIM), lambda h, i, low: (0, h)),
                pl.BlockSpec((length, HEAD_DIM), lambda h, i, low: (0, h)),
            ],
            out_specs=[
                pl.BlockSpec((bq, HEAD_DIM), lambda h, i, low: (i, h)),
                pl.BlockSpec((1, 1, bq), lambda h, i, low: (h, 0, i)),
            ],
        ),
        out_shape=[
            jax.ShapeDtypeStruct((length, width), f32),
            jax.ShapeDtypeStruct((heads, 1, length), f32),
        ],
        compiler_params=pltpu.CompilerParams(vmem_limit_bytes=48 << 20),
        cost_estimate=cost(16),
        name="attend",
    )(lows, starts, queries, keys, values)


def attend_back_kernel(
    low_ref, starts_ref, q_ref, k_ref, v_ref, out_ref, log_ref, grad_ref, dq_ref, dk_ref, dv_ref
):
    length = q_ref.shape[0]
    bq, bk = BLOCK_Q, BLOCK_K
    dk_ref[...] = jnp.zeros_like(dk_ref)
    dv_ref[...] = jnp.zeros_like(dv_ref)

    def query_step(i, carry):
        queries_at = pl.ds(pl.multiple_of(i * bq, bq), bq)
        queries, grads = q_ref[queries_at, :], grad_ref[queries_at, :]
        starts = starts_ref[:, queries_at]
        log_total = log_ref[0, :, queries_at]
        inner = jnp.sum((grads.astype(f32) * out_ref[queries_at, :]).T, axis=0, keepdims=True)

        def step(j, acc):
            rows = pl.ds(pl.multiple_of(j * bk, bk), bk)
            keys = k_ref[rows, :]
            scores = product_right(keys, queries) * scale_factor
            ok = allowed_keys(scores.shape, j * bk, i * bq, starts)
            probs = jnp.where(ok, jnp.exp(scores - log_total), 0.0)
            dv_ref[rows, :] += product(probs.astype(bf16), grads)
            prob_grad = product_right(v_ref[rows, :], grads)
            score_grad = (probs * (prob_grad - inner)).astype(bf16)
            dk_ref[rows, :] += product(score_grad, queries) * scale_factor
            return acc + product_left(keys, score_grad)

        acc = lax.fori_loop(
            low_ref[i], (i * bq + bq) // bk, step, jnp.zeros((HEAD_DIM, bq), f32)
        )
        dq_ref[queries_at, :] = (acc * scale_factor).T
        return carry

    lax.fori_loop(0, length // bq, query_step, 0)


def attend_back(lows, starts, queries, keys, values, out, log_total, grads):
    length, width = queries.shape
    heads = width // HEAD_DIM
    column = pl.BlockSpec((length, HEAD_DIM), lambda h, low: (0, h))
    return pl.pallas_call(
        attend_back_kernel,
        grid_spec=pltpu.PrefetchScalarGridSpec(
            num_scalar_prefetch=1,
            grid=(heads,),
            in_specs=[
                pl.BlockSpec((1, length), lambda h, low: (0, 0)),
                column,
                column,
                column,
                column,
                pl.BlockSpec((1, 1, length), lambda h, low: (h, 0, 0)),
                column,
            ],
            out_specs=[column, column, column],
        ),
        out_shape=[jax.ShapeDtypeStruct((length, width), f32)] * 3,
        compiler_params=pltpu.CompilerParams(vmem_limit_bytes=56 << 20),
        cost_estimate=cost(26),
        name="attend_back",
    )(lows, starts, queries, keys, values, out, log_total, grads)


def spread_kernel(in_ref, out_ref):
    unit = out_ref.shape[2]
    for k in range(out_ref.shape[0]):
        out_ref[k] = in_ref[:, k * unit : (k + 1) * unit]


def spread(weight, groups, owners):
    rows, columns = weight.shape
    unit = columns // (groups * owners)
    if unit % 128:
        shaped = weight.reshape(rows, groups, owners, unit).transpose(2, 0, 1, 3)
        return shaped.reshape(owners, rows, groups * unit)
    return pl.pallas_call(
        spread_kernel,
        grid=(groups,),
        in_specs=[pl.BlockSpec((rows, owners * unit), lambda g: (0, g))],
        out_specs=pl.BlockSpec((owners, rows, unit), lambda g: (0, 0, g)),
        out_shape=jax.ShapeDtypeStruct((owners, rows, groups * unit), weight.dtype),
        cost_estimate=cost(4),
        name="spread",
    )(weight)


def collect_kernel(in_ref, out_ref):
    unit = in_ref.shape[2]
    for k in range(in_ref.shape[0]):
        out_ref[:, k * unit : (k + 1) * unit] = in_ref[k].astype(f32)


def collect(blocks, groups):
    owners, rows, columns = blocks.shape
    unit = columns // groups
    if unit % 128:
        shaped = blocks.reshape(owners, rows, groups, unit).transpose(1, 2, 0, 3)
        return shaped.reshape(rows, groups * owners * unit).astype(f32)
    return pl.pallas_call(
        collect_kernel,
        grid=(groups,),
        in_specs=[pl.BlockSpec((owners, rows, unit), lambda g: (0, 0, g))],
        out_specs=pl.BlockSpec((rows, owners * unit), lambda g: (0, g)),
        out_shape=jax.ShapeDtypeStruct((rows, groups * owners * unit), f32),
        cost_estimate=cost(5),
        name="collect",
    )(blocks)


def columns_of(row):
    return jnp.broadcast_to(row, (HEAD_DIM, row.shape[1])).T


def halves_swapped(values):
    return pltpu.roll(values, HEAD_DIM // 2, 1)


def project_kernel(in_ref, weight_ref, out_ref, square_ref):
    width = out_ref.shape[1] // 3
    out = product(in_ref[...], weight_ref[...])
    out_ref[...] = out
    for part in range(2):
        total = None
        for h in range(0, width, HEAD_DIM):
            raw = out[:, part * width + h : part * width + h + HEAD_DIM]
            total = raw * raw if total is None else total + raw * raw
        square_ref[part : part + 1, :] = jnp.sum(total.T, axis=0, keepdims=True)


def project(inputs, weight):
    length, depth = inputs.shape
    columns = weight.shape[1]
    return pl.pallas_call(
        project_kernel,
        grid=(length // 256,),
        in_specs=[row_block(depth, 256), whole_block(depth, columns)],
        out_specs=[row_block(columns, 256), lane_block(2, 256)],
        out_shape=[
            jax.ShapeDtypeStruct((length, columns), f32),
            jax.ShapeDtypeStruct((2, length), f32),
        ],
        compiler_params=pltpu.CompilerParams(vmem_limit_bytes=32 << 20),
        cost_estimate=cost(10),
        name="project",
    )(inputs, weight)


def join_kernel(core_ref, full_ref, got_ref, out_ref):
    out_ref[...] = (full_ref[:, 0].astype(f32) + got_ref[...].astype(f32)).astype(bf16)


def join(full, got):
    count, _, rows, columns = full.shape
    step = 4 if count % 4 == 0 else 1
    part = pl.BlockSpec((step, rows, columns), lambda i, core: (i, 0, 0))
    return pl.pallas_call(
        join_kernel,
        grid_spec=pltpu.PrefetchScalarGridSpec(
            num_scalar_prefetch=1,
            grid=(count // step,),
            in_specs=[
                pl.BlockSpec((step, 1, rows, columns), lambda i, core: (i, core[0], 0, 0)),
                part,
            ],
            out_specs=part,
        ),
        out_shape=jax.ShapeDtypeStruct((count, rows, columns), bf16),
        cost_estimate=cost(1),
        name="join",
    )(lax.axis_index("c").astype(jnp.int32).reshape(1), full, got)


def turn_kernel(proj_ref, factor_ref, gain_ref, cos_ref, sin_ref, q_ref, k_ref, v_ref):
    width = q_ref.shape[1]
    cosine, sine_part = cos_ref[...], sin_ref[...]
    for part, out in enumerate((q_ref, k_ref)):
        factor = columns_of(factor_ref[part : part + 1, :])
        for h in range(0, width, HEAD_DIM):
            raw = proj_ref[:, part * width + h : part * width + h + HEAD_DIM]
            normed = raw * factor * gain_ref[part : part + 1, h : h + HEAD_DIM]
            turned = normed * cosine + halves_swapped(normed) * sine_part
            out[:, h : h + HEAD_DIM] = turned.astype(bf16)
    v_ref[...] = proj_ref[:, 2 * width :].astype(bf16)


def row_block(columns, rows=512):
    return pl.BlockSpec((rows, columns), lambda i: (i, 0))


def lane_block(lines, rows=512):
    return pl.BlockSpec((lines, rows), lambda i: (0, i))


def whole_block(*shape):
    return pl.BlockSpec(shape, lambda i: (0,) * len(shape))


def turn(projected, factors, gains, cosine, sine_part):
    length, columns = projected.shape
    width = columns // 3
    return pl.pallas_call(
        turn_kernel,
        grid=(length // 512,),
        in_specs=[
            row_block(columns),
            lane_block(2),
            whole_block(2, width),
            row_block(HEAD_DIM),
            row_block(HEAD_DIM),
        ],
        out_specs=[row_block(width)] * 3,
        out_shape=[jax.ShapeDtypeStruct((length, width), bf16)] * 3,
        cost_estimate=cost(1),
        name="turn",
    )(projected, factors, gains, cosine, sine_part)


def unturn_kernel(
    dq_ref, dk_ref, proj_ref, factor_ref, gain_ref, cos_ref, sin_ref, out_ref, mix_ref, sum_ref
):
    width = dq_ref.shape[1]
    cosine, sine_part = cos_ref[...], sin_ref[...]

    @pl.when(pl.program_id(0) == 0)
    def _():
        sum_ref[...] = jnp.zeros_like(sum_ref)

    for part, grad_ref in enumerate((dq_ref, dk_ref)):
        factor = columns_of(factor_ref[part : part + 1, :])
        mixed = None
        for h in range(0, width, HEAD_DIM):
            at = part * width + h
            grad = grad_ref[:, h : h + HEAD_DIM]
            turned = grad * cosine - halves_swapped(grad) * sine_part
            raw = proj_ref[:, at : at + HEAD_DIM]
            sums = jnp.sum(turned * raw * factor, axis=0, keepdims=True)
            sum_ref[part : part + 1, h : h + HEAD_DIM] += sums
            weighted = turned * gain_ref[part : part + 1, h : h + HEAD_DIM]
            out_ref[:, at : at + HEAD_DIM] = weighted
            mixed = weighted * raw if mixed is None else mixed + weighted * raw
        mix_ref[part : part + 1, :] = jnp.sum(mixed.T, axis=0, keepdims=True)


def unturn(query_grad, key_grad, projected, factors, gains, cosine, sine_part):
    length, width = query_grad.shape
    return pl.pallas_call(
        unturn_kernel,
        grid=(length // 512,),
        in_specs=[
            row_block(width),
            row_block(width),
            row_block(3 * width),
            lane_block(2),
            whole_block(2, width),
            row_block(HEAD_DIM),
            row_block(HEAD_DIM),
        ],
        out_specs=[row_block(2 * width), lane_block(2), whole_block(2, width)],
        out_shape=[
            jax.ShapeDtypeStruct((length, 2 * width), f32),
            jax.ShapeDtypeStruct((2, length), f32),
            jax.ShapeDtypeStruct((2, width), f32),
        ],
        cost_estimate=cost(1),
        name="unturn",
    )(query_grad, key_grad, projected, factors, gains, cosine, sine_part)


def finish_kernel(weighted_ref, proj_ref, factor_ref, mix_ref, dv_ref, out_ref):
    width = dv_ref.shape[1]
    for part in range(2):
        factor = columns_of(factor_ref[part : part + 1, :])
        mixing = columns_of(mix_ref[part : part + 1, :])
        for h in range(0, width, HEAD_DIM):
            at = pl.ds(part * width + h, HEAD_DIM)
            grad = weighted_ref[:, at] - proj_ref[:, at] * factor * factor * mixing
            out_ref[:, at] = (factor * grad).astype(bf16)
    out_ref[:, 2 * width :] = dv_ref[...].astype(bf16)


def finish(weighted, projected, factors, mixing, value_grad):
    length, width = value_grad.shape
    return pl.pallas_call(
        finish_kernel,
        grid=(length // 512,),
        in_specs=[
            row_block(2 * width),
            row_block(3 * width),
            lane_block(2),
            lane_block(2),
            row_block(width),
        ],
        out_specs=row_block(3 * width),
        out_shape=jax.ShapeDtypeStruct((length, 3 * width), bf16),
        cost_estimate=cost(1),
        name="finish",
    )(weighted, projected, factors, mixing, value_grad)


UNITS = 512
COLUMNS = 1024


class Steps:
    def __init__(self, units):
        self.first, self.second = units // UNITS, D // COLUMNS
        self.count = self.first + self.second

    def unit(self, i):
        return jnp.minimum(i, self.first - 1)

    def column(self, i):
        return jnp.maximum(i - self.first, 0)


def feed_call(kernel, name, blocks, chip, length, specs, weights, widths, held):
    count, piece = len(blocks), blocks[0].shape[0]
    rows, steps = piece * count, Steps(weights[1].shape[0])
    inputs, outputs, scratch = specs(steps, rows, chip)
    held = list(held or ())
    in_specs = [pl.BlockSpec((piece, D), lambda i: (0, 0))] * count + [s for s, _ in inputs]
    first = len(in_specs)
    part = pl.BlockSpec((piece, COLUMNS), lambda i: (0, steps.column(i)))
    results = pl.pallas_call(
        functools.partial(kernel, steps.first, count, len(held)),
        grid=(steps.count,),
        in_specs=in_specs + [pl.BlockSpec(memory_space=pl.ANY)] * len(held),
        out_specs=outputs + [part] * count,
        out_shape=[jax.ShapeDtypeStruct((length, w), bf16) for w in widths]
        + [jax.ShapeDtypeStruct((piece, D), bf16)] * count,
        scratch_shapes=[pltpu.VMEM((rows, D), bf16)]
        + [pltpu.VMEM((rows, width), bf16) for width in scratch],
        input_output_aliases={first + i: i for i in range(len(held))},
        cost_estimate=cost(1),
        compiler_params=pltpu.CompilerParams(vmem_limit_bytes=40 << 20),
        name=name,
    )(*blocks, *[array for _, array in inputs], *held)
    return list(results[: len(widths)]), tuple(results[len(widths) :])


def feed(blocks, chip, length, weights, held):
    units = weights[1].shape[0]

    def specs(steps, rows, chip):
        by_unit = pl.BlockSpec((rows, UNITS), lambda i: (chip, steps.unit(i)))
        inputs = [
            (pl.BlockSpec((D, UNITS), lambda i: (0, steps.unit(i))), weights[0]),
            (pl.BlockSpec((D, UNITS), lambda i: (0, steps.first + steps.unit(i))), weights[0]),
            (pl.BlockSpec((units, COLUMNS), lambda i: (0, steps.column(i))), weights[1]),
        ]
        rows_out = pl.BlockSpec((rows, D // steps.first), lambda i: (chip, steps.unit(i)))
        return inputs, [rows_out, by_unit, by_unit, by_unit], [units]

    widths = (D, units, units, units)
    return feed_call(feed_kernel, "feed", blocks, chip, length, specs, weights, widths, held)


def feed_back(blocks, chip, length, gate_all, up_all, weights, held):
    units = weights[1].shape[0]

    def specs(steps, rows, chip):
        by_unit = pl.BlockSpec((rows, UNITS), lambda i: (chip, steps.unit(i)))
        inputs = [
            (by_unit, gate_all),
            (by_unit, up_all),
            (pl.BlockSpec((UNITS, D), lambda i: (steps.unit(i), 0)), weights[1]),
            (pl.BlockSpec((COLUMNS, 2 * units), lambda i: (steps.column(i), 0)), weights[0]),
        ]
        rows_out = pl.BlockSpec((rows, D // steps.first), lambda i: (chip, steps.unit(i)))
        grads = pl.BlockSpec((rows, 2 * units // steps.second), lambda i: (chip, steps.column(i)))
        return inputs, [rows_out, grads], [2 * units]

    widths = (D, 2 * units)
    return feed_call(
        feed_back_kernel, "feed_back", blocks, chip, length, specs, weights, widths, held
    )


def chunk(step, size, offset=0):
    return pl.ds(pl.multiple_of(step * size, size) + offset, size)


def take_rows(block_refs, rows, rows_out):
    step = pl.program_id(0)

    @pl.when(step == 0)
    def _():
        piece = block_refs[0].shape[0]
        for i, block in enumerate(block_refs):
            rows[i * piece : (i + 1) * piece, :] = block[...]

    size = rows_out.shape[1]
    rows_out[...] = rows[:, chunk(step, size)]


def give_parts(part, part_refs):
    piece = part_refs[0].shape[0]
    for i, out in enumerate(part_refs):
        out[...] = part[i * piece : (i + 1) * piece].astype(bf16)


def feed_kernel(first, count, held, *refs):
    block_refs, (gate_w, up_w, down_w) = refs[:count], refs[count : count + 3]
    outs = refs[count + 3 + held :]
    rows_out, gate_out, up_out, hidden_out = outs[:4]
    part_refs, (rows, all_hidden) = outs[4 : 4 + count], outs[4 + count :]
    step = pl.program_id(0)

    @pl.when(step < first)
    def _():
        take_rows(block_refs, rows, rows_out)
        gate, up = product(rows[...], gate_w[...]), product(rows[...], up_w[...])
        hidden = (gate * jax.nn.sigmoid(gate) * up).astype(bf16)
        gate_out[...], up_out[...] = gate.astype(bf16), up.astype(bf16)
        hidden_out[...] = hidden
        all_hidden[:, chunk(step, UNITS)] = hidden

    @pl.when(step >= first)
    def _():
        give_parts(product(all_hidden[...], down_w[...]), part_refs)


def feed_back_kernel(first, count, held, *refs):
    block_refs, (gate_in, up_in, down_w, in_w) = refs[:count], refs[count : count + 4]
    outs = refs[count + 4 + held :]
    rows_out, grads_out = outs[:2]
    part_refs, (rows, grads) = outs[2 : 2 + count], outs[2 + count :]
    units = grads.shape[1] // 2
    step = pl.program_id(0)

    @pl.when(step < first)
    def _():
        take_rows(block_refs, rows, rows_out)
        hidden_grad = product_right(rows[...], down_w[...])
        gate, up = gate_in[...].astype(f32), up_in[...].astype(f32)
        sigmoid_gate = jax.nn.sigmoid(gate)
        gate_grad = hidden_grad * up * sigmoid_gate * (1.0 + gate * (1.0 - sigmoid_gate))
        grads[:, chunk(step, UNITS)] = gate_grad.astype(bf16)
        grads[:, chunk(step, UNITS, units)] = (hidden_grad * gate * sigmoid_gate).astype(bf16)

    @pl.when(step >= first)
    def _():
        size = grads_out.shape[1]
        grads_out[...] = grads[:, chunk(step - first, size)]
        give_parts(product_right(grads[...], in_w[...]), part_refs)


def norm_forward(values, gain_row):
    factor = lax.rsqrt(jnp.mean(values * values, axis=-1, keepdims=True) + norm_epsilon)
    return (values * factor * gain_row, factor)


def norm_backward(values, factor, gain_row, incoming):
    weighted = incoming * gain_row
    mixing = jnp.mean(weighted * values, axis=-1, keepdims=True)
    return (
        factor * (weighted - values * factor * factor * mixing),
        jnp.sum(incoming * values * factor, axis=0),
    )


def arrange(lengths, positions):
    finish = jnp.cumsum(lengths)
    has_ended = finish[None, :] <= positions[:, None]
    return jnp.sum(jnp.where(has_ended, lengths[None, :], 0), axis=1).astype(jnp.int32)


def scatter_over(value, axes):
    return lax.psum_scatter(value.astype(bf16), axes, scatter_dimension=0, tiled=True)


def on_device(
    hidden_in, seq_lengths, qkv_weight, out_weight, in_weight, down_weight, norm_gains, upstream
):
    piece_len, model_width = hidden_in.shape[1:]
    line_sizes = sizes_of(LINE)
    line = line_sizes[0] * line_sizes[1]
    length = piece_len * line * 2
    width = D // (line * 2)
    core = lax.axis_index("c")
    ctx_place = linear([lax.axis_index(a) for a in CTX], sizes_of(CTX))
    data_place = linear([lax.axis_index(a) for a in DATA], sizes_of(DATA))
    line_place = linear([lax.axis_index(a) for a in LINE], line_sizes)
    lengths = lax.dynamic_index_in_dim(seq_lengths, data_place, 0, keepdims=False)
    places = jnp.arange(length, dtype=jnp.int32)
    starts = arrange(lengths, places)
    offset = (places - starts).astype(f32)
    lows = starts[::BLOCK_Q] // BLOCK_K
    starts_row = starts.reshape(1, length)
    inverse = rope_base ** (-2.0 * jnp.arange(HEAD_DIM // 2, dtype=f32) / HEAD_DIM)

    def tables(offset):
        angles = offset[:, None] * inverse[None, :]
        cosine, sine_part = jnp.cos(angles), jnp.sin(angles)
        cosine = jnp.concatenate([cosine, cosine], axis=1)
        return cosine, jnp.concatenate([-sine_part, sine_part], axis=1)

    own_input = hidden_in.reshape(piece_len, model_width)

    row = Line(LINE)

    row_count = qkv_weight.shape[0]
    owners = line * 2
    data_count = sizes_of(DATA)[0] * sizes_of(DATA)[1]
    buffer = [jnp.zeros((line, 2, piece_len, model_width), bf16)]

    def keep_input(k, same, other):
        of_other = k if k == line - 1 else k - 1 if k < line else line - 2
        for at_core, block, at in ((core, same, k), (1 - core, other, of_other)):
            if block is not None:
                buffer[0] = lax.dynamic_update_slice(
                    buffer[0], block[None, None], (row.served(at), at_core, 0, 0)
                )
        return ()

    def weights_step(slot, tied):
        if slot == 0:
            blocks = spread(qkv_weight, 3, owners)
            blocks = exchange_cores(blocks.reshape(line, 2, row_count, 3 * width))
            return (blocks, in_weight, offset)
        if slot == 1:
            down = lax.all_gather(down_weight, DATA, axis=0, tiled=True)
            blocks = spread(tied[0][1], 2 * data_count, owners)
            return (chips_start(tied[0][0], LINE), down, blocks, tables(tied[0][2]))
        if slot == 2:
            return cores_start(tied[1][2].reshape((line, 2) + tied[1][2].shape[1:]))
        if slot == line - 1:
            return (out_weight, tied[2])
        return ()

    plan = [[0], [1], []] + [[slot - 1] for slot in range(3, line)]
    swaps = [[0], [], [1, 2]] + [[k] for k in range(3, line)]
    _, tied = row.gather(own_input, keep_input, weights_step, plan, swaps)
    full_input = buffer[0].reshape(length, model_width)
    qkv_rows = by_source(tied[1][0], LINE).reshape(-1, 3 * width)
    qkv_here = lax.all_gather(qkv_rows, DATA, axis=0, tiled=True)
    down_here, (cosine, sine_part) = tied[1][1], tied[1][3]
    units = down_here.shape[0]
    out_shuffled, (in_keep, in_got) = tied[line - 1]
    out_pieces = shifts(lambda steps: out_shuffled, LINE)

    projected, squares = project(full_input, qkv_here)
    squares, out_pieces, in_got = together(squares, out_pieces, in_got)
    out_line = by_source(out_pieces, LINE)
    out_half = lax.all_gather(out_line.reshape(-1, D), DATA, axis=0, tiled=True)
    in_pieces = chips_start(by_core(in_keep, in_got), LINE)
    factors = lax.rsqrt(small_sum(squares, CTX) / D + norm_epsilon)
    gains_here = lax.dynamic_slice(norm_gains, (0, ctx_place * width), (2, width))
    query_low, key_low, value_low = turn(projected, factors, gains_here, cosine, sine_part)
    head_out, log_total = attend(lows, starts_row, query_low, key_low, value_low)

    blocks = head_out.astype(bf16).reshape(line, 2, piece_len, width)
    keep, got = cores_start(blocks)
    got, in_pieces, out_half = together(got, in_pieces, out_half)
    out_half = out_half.reshape(-1, out_weight.shape[0], D)
    out_other = swap(out_half)
    in_rows = by_source(in_pieces, LINE)
    in_here = lax.all_gather(in_rows.reshape(-1, in_rows.shape[-1]), DATA, axis=0, tiled=True)
    out_full = by_core(out_half, out_other).reshape(D, D)
    pieces, out_full = together(chips_start(by_core(keep, got), LINE), out_full)
    attended = by_source(pieces, LINE)
    attended_low = attended.reshape(line * 2, piece_len, width).transpose(1, 0, 2)
    attended_low = attended_low.reshape(piece_len, D)
    branch = product(attended_low, out_full)
    branch_normed, branch_factor = norm_forward(branch, norm_gains[2])
    residual = own_input.astype(f32) + branch_normed
    residual_low = residual.astype(bf16)

    def chip_sums(results):
        def parts(k):
            if k == line - 1:
                other = results[k][1]
            else:
                other = results[line][0] if k == line - 2 else results[k + 1][1]
            return scatter_sum(results[k][0], other)

        return parts

    def window_of(k):
        return 2 * line - 2 if k == 0 else 2 * line - 1 if k == line else k - 1

    held = {}

    def forward_chip(k, same, other):
        blocks = [b for b in (same, other) if b is not None]
        held["forward"], parts = feed(
            blocks, window_of(k), length, (in_here, down_here), held.get("forward")
        )
        return parts

    plan = [[], [0], [1, 2]] + [[k] for k in range(3, line - 1)] + [[]]
    forward, _ = row.gather(residual_low, forward_chip, plan=plan)
    residual_all, gate_all, up_all, hidden_all = held["forward"]
    second, _ = row.scatter(chip_sums(forward))
    second_normed, second_factor = norm_forward(second, norm_gains[3])
    result = residual + second_normed
    live_places = ctx_place * piece_len + jnp.arange(piece_len, dtype=jnp.int32)
    live_rows = (live_places < jnp.sum(lengths)).astype(f32)[:, None]
    sums = jnp.stack(
        [
            jnp.sum(result * result * live_rows),
            jnp.sum(branch * branch * live_rows),
            jnp.sum(second * second * live_rows),
        ]
    )

    incoming = upstream.reshape(piece_len, model_width).astype(f32)
    second_grad, second_gain_grad = norm_backward(second, second_factor, norm_gains[3], incoming)

    def backward_chip(k, same, other):
        blocks = [b for b in (same, other) if b is not None]
        held["backward"], parts = feed_back(
            blocks, window_of(k), length, gate_all, up_all, (in_here, down_here),
            held.get("backward"),
        )
        return parts

    backward, _ = row.gather(second_grad.astype(bf16), backward_chip)
    second_grad_all, gate_up_grads = held["backward"]

    def weight_grads(slot, tied):
        if slot == 1:
            return (product_left(residual_all, gate_up_grads).astype(bf16),)
        if slot == 2:
            return (product_left(hidden_all, second_grad_all).astype(bf16),)
        return ()

    residual_part, tied = row.scatter(chip_sums(backward), weight_grads)
    grad_in, grad_down = tied[0][0], tied[1][0]
    residual_grad = incoming + residual_part
    grad_in = scatter_over(grad_in, DATA).reshape(in_rows.shape)

    branch_grad, branch_gain_grad = norm_backward(
        branch, branch_factor, norm_gains[2], residual_grad
    )
    branch_grad_low = branch_grad.astype(bf16)
    attended_grad = product_right(branch_grad_low, out_full).astype(bf16)
    attended_grad = attended_grad.reshape(piece_len, line, 2, width).transpose(1, 2, 0, 3)
    keep, give = pick(attended_grad, core, 1), pick(attended_grad, 1 - core, 1)
    give, branch_grad_low = together(give, branch_grad_low)
    out_grad = product_left(attended_low, branch_grad_low).astype(bf16)
    out_grad = out_grad.reshape(-1, 2, out_weight.shape[0], D)
    got, out_grad, grad_in = together(swap(give), out_grad, grad_in)
    pieces = chips_start(by_core(keep, got), LINE)
    in_keep, in_got = cores_start(grad_in.reshape((line, 2) + in_rows.shape[2:]))
    out_got = swap(pick(out_grad, 1 - core, 1))
    pieces, in_got, out_got = together(pieces, in_got, out_got)
    head_grad = by_source(pieces, LINE).reshape(length, width)
    in_pieces = chips_start(by_core(in_keep, in_got), LINE)
    out_grad = join(out_grad, out_got)
    head_grad, out_grad = together(head_grad, out_grad)
    out_grad = scatter_over(out_grad.reshape(D // 2, D), DATA)
    out_grad = out_grad.reshape((line,) + out_weight.shape)

    query_grad, key_grad, value_grad = attend_back(
        lows, starts_row, query_low, key_low, value_low, head_out, log_total, head_grad
    )
    weighted, mixing, gain_grads = unturn(
        query_grad, key_grad, projected, factors, gains_here, cosine, sine_part
    )
    mixing, in_pieces, grad_down = together(mixing, in_pieces, grad_down)
    grad_down = scatter_over(grad_down, DATA)
    mixing = small_sum(mixing, CTX) / D
    projected_grad = finish(weighted, projected, factors, mixing, value_grad)
    projected_grad, out_pieces = together(projected_grad, chips_start(out_grad, LINE))
    grad_blocks = projected_grad.reshape(line, 2, piece_len, 3 * width)

    later = []

    def input_chip(k):
        rows = pick(grad_blocks, row.served(k))
        rows = jnp.concatenate([pick(rows, core), pick(rows, 1 - core)], axis=0)
        part = product_right(rows, qkv_here).astype(bf16)
        part = scatter_sum(part[:piece_len], part[piece_len:])
        if not later:
            later.extend(together(part, projected_grad))
            part = later[0]
        return part

    def step(rows, axis):
        if lax.axis_size(axis) == 2:
            return (rows, lax.ppermute(rows, axis, [(0, 1), (1, 0)]))
        return (lax.psum(rows, axis),)

    def last_grads(slot, tied):
        if slot == 1:
            return (product_left(full_input, later[1]).astype(bf16), gain_grads)
        if slot == 2:
            rows = jnp.zeros((5, D), f32)
            rows = lax.dynamic_update_slice(rows, tied[0][1], (0, ctx_place * width))
            rows = rows.at[2].set(branch_gain_grad).at[3].set(second_gain_grad)
            rows = rows.at[4, :3].set(sums)
            return (scatter_over(tied[0][0], DATA), step(rows, "c"), grad_down)
        if slot == line - 1:
            blocks = tied[1][0].reshape(line, 2, row_count, 3 * width)
            return (cores_start(blocks), step(sum(tied[1][1]), "zl"), in_pieces, tied[1][2])
        return ()

    plan = [[line - 2, line - 3]] + [[k] for k in range(line - 4, -1, -1)] + [[]]
    input_part, tied = row.scatter(input_chip, last_grads, plan)
    qkv_cores, gain_rows, in_pieces, grad_down = tied[line - 2]
    qkv_pieces = chips_start(by_core(*qkv_cores), LINE)
    gain_rows, qkv_pieces = together(step(sum(gain_rows), "zh"), qkv_pieces)
    gain_rows = small_sum(sum(gain_rows), ("dl", "dh"))
    input_grad = residual_grad + input_part
    grad_in = by_source(in_pieces, LINE)
    grad_in = collect(grad_in.reshape((owners,) + grad_in.shape[2:]), 2 * data_count)
    grad_down = grad_down.astype(f32)
    grad_out = sum(piece.astype(f32) for piece in out_pieces)
    grad_qkv = by_source(qkv_pieces, LINE)
    grad_qkv = collect(grad_qkv.reshape(owners, row_count, 3 * width), 3)
    live_count = jnp.sum(seq_lengths).astype(f32)
    rms_values = jnp.sqrt(gain_rows[4, :3] / (live_count * model_width))
    return (
        result.astype(bf16)[None],
        input_grad[None],
        grad_qkv,
        grad_out,
        grad_in,
        grad_down,
        gain_rows[:4],
        rms_values,
    )


def solution(mesh):
    dp, ctx = mesh.shape["dp"], mesh.shape["ctx"]
    fine = Mesh(mesh.devices.reshape(2, dp // 2, 2, ctx // 4, 2), AXES)
    return jax.shard_map(
        on_device,
        mesh=fine,
        in_specs=(
            P(DATA, CTX, None),
            P(),
            P(AXES, None),
            P(AXES, None),
            P(AXES, None),
            P(AXES, None),
            P(),
            P(DATA, CTX, None),
        ),
        out_specs=(
            P(DATA, CTX, None),
            P(DATA, CTX, None),
            P(AXES, None),
            P(AXES, None),
            P(AXES, None),
            P(AXES, None),
            P(),
            P(),
        ),
        check_vma=False,
    )
```

```python
import functools
import itertools

import jax
import jax.numpy as jnp
import numpy as np
from jax import lax
from jax.experimental import pallas as pl
from jax.experimental.pallas import tpu as pltpu
from jax.sharding import Mesh
from jax.sharding import PartitionSpec as P

D = 2048
HEADS = 16
HEAD_DIM = 128
FF = 8192

norm_epsilon = 1e-06
rope_base = 500000.0
masked_score = -1e30
scale_factor = HEAD_DIM ** (-0.5)

AXES = ("dh", "dl", "zh", "zl", "c")
DATA = ("dh", "dl")
LINE = ("zh", "zl")
CTX = ("zh", "zl", "c")

BLOCK_Q = 512
BLOCK_K = 512

bf16 = jnp.bfloat16
f32 = jnp.float32


def sizes_of(axes):
    return tuple(lax.axis_size(a) for a in axes)


def offsets(axes):
    return list(itertools.product(*[range(n) for n in sizes_of(axes)]))


def linear(index, sizes):
    total = 0
    for i, n in zip(index, sizes):
        total = total * n + i
    return total


def shift(value, axes, steps):
    if not any(steps):
        return value
    sizes = sizes_of(axes)
    pairs = []
    for index in itertools.product(*[range(n) for n in sizes]):
        target = tuple((i + s) % n for i, s, n in zip(index, steps, sizes))
        pairs.append((linear(index, sizes), linear(target, sizes)))
    return lax.ppermute(value, axes, pairs)


def swap(value):
    return lax.ppermute(value, "c", [(0, 1), (1, 0)])


def place(axes, steps, sign=1):
    sizes = sizes_of(axes)
    here = [(lax.axis_index(a) + sign * s) % n for a, s, n in zip(axes, steps, sizes)]
    return linear(here, sizes)


def pick(value, index, axis=0):
    return lax.dynamic_index_in_dim(value, index, axis, keepdims=False)


def put(buffer, value, index):
    return lax.dynamic_update_slice_in_dim(buffer, value[None], index, 0)


def together(*values):
    return lax.optimization_barrier(values)


def line_order(count):
    return np.array(
        [sorted(range(count), key=lambda j: (abs(i - j), j != i ^ 1)) for i in range(count)],
        dtype=np.int32,
    )


class Line:
    def __init__(self, axes):
        self.axes = axes
        sizes = sizes_of(axes)
        self.count = sizes[0] * sizes[1]
        self.place = linear([lax.axis_index(a) for a in axes], sizes)
        self.order = line_order(self.count)

    def served(self, k):
        return jnp.asarray(self.order[:, k])[self.place]

    def hop(self, value, step, keep=lambda i: True):
        pairs = [
            (i, i + step) for i in range(self.count) if 0 <= i + step < self.count and keep(i)
        ]
        return lax.ppermute(value, self.axes, pairs)

    def choose(self, options, wanted):
        used = sorted({w for w in wanted if w is not None})
        value = options[used[0]]
        for w in used[1:]:
            mask = np.array([v == w for v in wanted])
            value = jnp.where(jnp.asarray(mask)[self.place], options[w], value)
        return value

    def gather(self, block, work, extra=None, plan=None, swaps=None):
        last = self.count - 1
        plan = plan or [[k] for k in range(last)] + [[]]
        swaps = swaps or [[k] for k in range(last + 1)]
        options, results, tied, arrived, other = {}, [], [], [], {-1: None}
        for slot in range(self.count):
            if slot:
                wanted = []
                for i in range(self.count):
                    j = self.order[i, slot]
                    wanted.append((1, i - j) if j < i else (-1, j - i))
                arrived.append(self.choose(options, wanted))
            else:
                arrived.append(block)
            moved = ()
            if slot < last:
                moved = tuple(
                    self.hop(options[(step, slot)] if slot else block, step) for step in (1, -1)
                )
            swapped = [swap(arrived[k]) for k in swaps[slot]]
            done = [work(k, arrived[k], other[k - 1]) for k in plan[slot]]
            more = extra(slot, tied) if extra else ()
            moved, swapped, done, more = together(moved, swapped, done, more)
            if moved:
                options[(1, slot + 1)], options[(-1, slot + 1)] = moved
            other.update(zip(swaps[slot], swapped))
            tied.append(more)
            results += done
        results.append(work(last, arrived[last], other[last]))
        results.append(work(self.count, None, other[last - 1]))
        return results, tied

    def hop_values(self, made, far, last):
        wanted = {}
        for step in (1, -1):
            wanted[step] = []
            for i in range(self.count):
                j = i + step * far
                known = 0 <= j < self.count
                wanted[step].append(int(np.argmax(self.order[i] == j)) if known else None)
        values = []
        for step in (1, -1):
            value = self.choose(made, wanted[step])
            if last[step] is not None:
                value = value.astype(f32) + last[step].astype(f32)
            values.append(value.astype(bf16))
        return values

    def scatter(self, parts, fill=None, plan=None):
        count = self.count
        plan = plan or [[k] for k in range(count - 2, -1, -1)]
        made = {count - 1: parts(count - 1)}
        last = {1: None, -1: None}
        tied = self.tied = []
        for slot in range(1, count):
            far = count - slot
            values = self.hop_values(made, far, last)
            moved = []
            for step, value in zip((1, -1), values):
                keep = lambda i: 0 <= i + step * far < count
                moved.append(self.hop(value, step, keep))
            done = [parts(k) for k in plan[slot - 1]]
            more = fill(slot, tied) if fill else ()
            moved, done, more = together(moved, done, more)
            tied.append(more)
            made.update(zip(plan[slot - 1], done))
            last[1], last[-1] = moved
        total = made[0].astype(f32) + last[1].astype(f32) + last[-1].astype(f32)
        return total, tied


def scatter_sum(for_same, for_other):
    return (for_same.astype(f32) + swap(for_other.astype(bf16)).astype(f32)).astype(bf16)


def cores_start(blocks):
    core = lax.axis_index("c")
    return pick(blocks, core, 1), swap(pick(blocks, 1 - core, 1))


def exchange_cores(blocks):
    return by_core(*cores_start(blocks))


def by_core(mine, other):
    shape = (mine.shape[0], 2) + mine.shape[1:]
    here = lax.broadcasted_iota(jnp.int32, shape, 1) == lax.axis_index("c")
    return jnp.where(here, mine[:, None], other[:, None])


def assemble_kernel(*refs):
    out_ref = refs[-1]
    for i, piece in enumerate(refs[1:-1]):

        @pl.when(pl.program_id(0) == i)
        def _(piece=piece):
            out_ref[0] = piece[...]


def assemble(pieces, places):
    shape = pieces[0].shape
    block = pl.BlockSpec(shape, lambda i, places: (0,) * len(shape))
    return pl.pallas_call(
        assemble_kernel,
        grid_spec=pltpu.PrefetchScalarGridSpec(
            num_scalar_prefetch=1,
            grid=(len(pieces),),
            in_specs=[block] * len(pieces),
            out_specs=pl.BlockSpec((1,) + shape, lambda i, places: (places[i],) + (0,) * len(shape)),
        ),
        out_shape=jax.ShapeDtypeStruct((len(pieces),) + shape, pieces[0].dtype),
        compiler_params=pltpu.CompilerParams(vmem_limit_bytes=18 << 20),
        cost_estimate=cost(2),
        name="assemble",
    )(jnp.stack(places).astype(jnp.int32), *pieces)


def shifts(value_for, chips):
    return tuple(shift(value_for(steps), chips, steps) for steps in offsets(chips))


def by_source(pieces, chips):
    return assemble(pieces, [place(chips, steps, -1) for steps in offsets(chips)])


def chips_start(pairs, chips):
    return shifts(lambda steps: pick(pairs, place(chips, steps)), chips)


def exchange_chips(pairs, chips):
    return by_source(chips_start(pairs, chips), chips)


def exchange(blocks, chips):
    return exchange_chips(exchange_cores(blocks), chips)


def small_sum(value, axes):
    for axis in axes:
        if lax.axis_size(axis) == 2:
            value = value + lax.ppermute(value, axis, [(0, 1), (1, 0)])
        else:
            value = lax.psum(value, axis)
    return value


def product(left_side, right_side):
    return jnp.dot(left_side, right_side, preferred_element_type=f32)


def product_left(left_side, right_side):
    return lax.dot_general(
        left_side, right_side, (((0,), (0,)), ((), ())), preferred_element_type=f32
    )


def product_right(left_side, right_side):
    return lax.dot_general(
        left_side, right_side, (((1,), (1,)), ((), ())), preferred_element_type=f32
    )


def cost(microseconds):
    return pl.CostEstimate(
        flops=int(microseconds * 1.0e9),
        transcendentals=0,
        bytes_accessed=int(microseconds * 3.0e6),
    )


def allowed_keys(shape, key_start, query_start, starts):
    key_place = key_start + lax.broadcasted_iota(jnp.int32, shape, 0)
    query_place = query_start + lax.broadcasted_iota(jnp.int32, shape, 1)
    return (key_place >= starts) & (key_place <= query_place)


def attend_kernel(low_ref, starts_ref, q_ref, k_ref, v_ref, out_ref, log_ref):
    block = pl.program_id(1)
    bq, bk = q_ref.shape[0], BLOCK_K
    queries, starts = q_ref[...], starts_ref[...]

    def step(j, carry):
        top, total, acc = carry
        rows = pl.ds(pl.multiple_of(j * bk, bk), bk)
        scores = product_right(k_ref[rows, :], queries) * scale_factor
        ok = allowed_keys(scores.shape, j * bk, block * bq, starts)
        scores = jnp.where(ok, scores, masked_score)
        new_top = jnp.maximum(top, jnp.max(scores, axis=0, keepdims=True))
        ratio = jnp.exp(top - new_top)
        expanded = jnp.exp(scores - new_top)
        total = total * ratio + jnp.sum(expanded, axis=0, keepdims=True)
        acc = acc * ratio + product_left(v_ref[rows, :], expanded.astype(bf16))
        return (new_top, total, acc)

    init = (
        jnp.full((1, bq), masked_score, f32),
        jnp.zeros((1, bq), f32),
        jnp.zeros((HEAD_DIM, bq), f32),
    )
    top, total, acc = lax.fori_loop(low_ref[block], (block * bq + bq) // bk, step, init)
    out_ref[...] = (acc / total).T
    log_ref[0] = top + jnp.log(total)


def in_hbm(*arrays):
    return tuple(pltpu.with_memory_space_constraint(a, pltpu.HBM) for a in arrays)


def attend(lows, starts, queries, keys, values):
    length, width = queries.shape
    queries, keys, values = in_hbm(queries, keys, values)
    heads, bq = width // HEAD_DIM, BLOCK_Q
    return pl.pallas_call(
        attend_kernel,
        grid_spec=pltpu.PrefetchScalarGridSpec(
            num_scalar_prefetch=1,
            grid=(heads, length // bq),
            in_specs=[
                pl.BlockSpec((1, bq), lambda h, i, low: (0, i)),
                pl.BlockSpec((bq, HEAD_DIM), lambda h, i, low: (i, h)),
                pl.BlockSpec((length, HEAD_DIM), lambda h, i, low: (0, h)),
                pl.BlockSpec((length, HEAD_DIM), lambda h, i, low: (0, h)),
            ],
            out_specs=[
                pl.BlockSpec((bq, HEAD_DIM), lambda h, i, low: (i, h)),
                pl.BlockSpec((1, 1, bq), lambda h, i, low: (h, 0, i)),
            ],
        ),
        out_shape=[
            pltpu.HBM((length, width), f32),
            jax.ShapeDtypeStruct((heads, 1, length), f32),
        ],
        compiler_params=pltpu.CompilerParams(vmem_limit_bytes=16 << 20),
        cost_estimate=cost(16),
        name="attend",
    )(lows, starts, queries, keys, values)


def attend_back_kernel(
    low_ref, starts_ref, q_ref, k_ref, v_ref, out_ref, log_ref, grad_ref, dq_ref, dk_ref, dv_ref
):
    length = q_ref.shape[0]
    bq, bk = BLOCK_Q, BLOCK_K
    dk_ref[...] = jnp.zeros_like(dk_ref)
    dv_ref[...] = jnp.zeros_like(dv_ref)

    def query_step(i, carry):
        queries_at = pl.ds(pl.multiple_of(i * bq, bq), bq)
        queries, grads = q_ref[queries_at, :], grad_ref[queries_at, :]
        starts = starts_ref[:, queries_at]
        log_total = log_ref[0, :, queries_at]
        inner = jnp.sum((grads.astype(f32) * out_ref[queries_at, :]).T, axis=0, keepdims=True)

        def step(j, acc):
            rows = pl.ds(pl.multiple_of(j * bk, bk), bk)
            keys = k_ref[rows, :]
            scores = product_right(keys, queries) * scale_factor
            ok = allowed_keys(scores.shape, j * bk, i * bq, starts)
            probs = jnp.where(ok, jnp.exp(scores - log_total), 0.0)
            dv_ref[rows, :] += product(probs.astype(bf16), grads)
            prob_grad = product_right(v_ref[rows, :], grads)
            score_grad = (probs * (prob_grad - inner)).astype(bf16)
            dk_ref[rows, :] += product(score_grad, queries) * scale_factor
            return acc + product_left(keys, score_grad)

        acc = lax.fori_loop(
            low_ref[i], (i * bq + bq) // bk, step, jnp.zeros((HEAD_DIM, bq), f32)
        )
        dq_ref[queries_at, :] = (acc * scale_factor).T
        return carry

    lax.fori_loop(0, length // bq, query_step, 0)


def attend_back(lows, starts, queries, keys, values, out, log_total, grads):
    length, width = queries.shape
    heads = width // HEAD_DIM
    column = pl.BlockSpec((length, HEAD_DIM), lambda h, low: (0, h))
    return pl.pallas_call(
        attend_back_kernel,
        grid_spec=pltpu.PrefetchScalarGridSpec(
            num_scalar_prefetch=1,
            grid=(heads,),
            in_specs=[
                pl.BlockSpec((1, length), lambda h, low: (0, 0)),
                column,
                column,
                column,
                column,
                pl.BlockSpec((1, 1, length), lambda h, low: (h, 0, 0)),
                column,
            ],
            out_specs=[column, column, column],
        ),
        out_shape=[pltpu.HBM((length, width), f32)] * 3,
        compiler_params=pltpu.CompilerParams(vmem_limit_bytes=28 << 20),
        cost_estimate=cost(26),
        name="attend_back",
    )(lows, starts, queries, keys, values, out, log_total, grads)


def spread_kernel(in_ref, out_ref):
    unit = out_ref.shape[2]
    for k in range(out_ref.shape[0]):
        out_ref[k] = in_ref[:, k * unit : (k + 1) * unit]


def spread(weight, groups, owners):
    rows, columns = weight.shape
    unit = columns // (groups * owners)
    if unit % 128:
        shaped = weight.reshape(rows, groups, owners, unit).transpose(2, 0, 1, 3)
        return shaped.reshape(owners, rows, groups * unit)
    return pl.pallas_call(
        spread_kernel,
        grid=(groups,),
        in_specs=[pl.BlockSpec((rows, owners * unit), lambda g: (0, g))],
        out_specs=pl.BlockSpec((owners, rows, unit), lambda g: (0, 0, g)),
        out_shape=jax.ShapeDtypeStruct((owners, rows, groups * unit), weight.dtype),
        cost_estimate=cost(4),
        name="spread",
    )(weight)


def collect_kernel(in_ref, out_ref):
    unit = in_ref.shape[2]
    for k in range(in_ref.shape[0]):
        out_ref[:, k * unit : (k + 1) * unit] = in_ref[k].astype(f32)


def collect(blocks, groups):
    owners, rows, columns = blocks.shape
    unit = columns // groups
    if unit % 128:
        shaped = blocks.reshape(owners, rows, groups, unit).transpose(1, 2, 0, 3)
        return shaped.reshape(rows, groups * owners * unit).astype(f32)
    return pl.pallas_call(
        collect_kernel,
        grid=(groups,),
        in_specs=[pl.BlockSpec((owners, rows, unit), lambda g: (0, 0, g))],
        out_specs=pl.BlockSpec((rows, owners * unit), lambda g: (0, g)),
        out_shape=jax.ShapeDtypeStruct((rows, groups * owners * unit), f32),
        cost_estimate=cost(5),
        name="collect",
    )(blocks)


def columns_of(row):
    return jnp.broadcast_to(row, (HEAD_DIM, row.shape[1])).T


def halves_swapped(values):
    return pltpu.roll(values, HEAD_DIM // 2, 1)


def project_kernel(in_ref, weight_ref, out_ref, square_ref):
    width = out_ref.shape[1] // 3
    out = product(in_ref[...], weight_ref[...])
    out_ref[...] = out
    for part in range(2):
        total = None
        for h in range(0, width, HEAD_DIM):
            raw = out[:, part * width + h : part * width + h + HEAD_DIM]
            total = raw * raw if total is None else total + raw * raw
        square_ref[part : part + 1, :] = jnp.sum(total.T, axis=0, keepdims=True)


def project(inputs, weight):
    length, depth = inputs.shape
    columns = weight.shape[1]
    return pl.pallas_call(
        project_kernel,
        grid=(length // 256,),
        in_specs=[row_block(depth, 256), whole_block(depth, columns)],
        out_specs=[row_block(columns, 256), lane_block(2, 256)],
        out_shape=[
            pltpu.HBM((length, columns), f32),
            jax.ShapeDtypeStruct((2, length), f32),
        ],
        compiler_params=pltpu.CompilerParams(vmem_limit_bytes=18 << 20),
        cost_estimate=cost(10),
        name="project",
    )(inputs, weight)


def join_kernel(core_ref, full_ref, got_ref, out_ref):
    out_ref[...] = (full_ref[:, 0].astype(f32) + got_ref[...].astype(f32)).astype(bf16)


def join(full, got):
    count, _, rows, columns = full.shape
    step = 4 if count % 4 == 0 else 1
    part = pl.BlockSpec((step, rows, columns), lambda i, core: (i, 0, 0))
    return pl.pallas_call(
        join_kernel,
        grid_spec=pltpu.PrefetchScalarGridSpec(
            num_scalar_prefetch=1,
            grid=(count // step,),
            in_specs=[
                pl.BlockSpec((step, 1, rows, columns), lambda i, core: (i, core[0], 0, 0)),
                part,
            ],
            out_specs=part,
        ),
        out_shape=jax.ShapeDtypeStruct((count, rows, columns), bf16),
        cost_estimate=cost(1),
        name="join",
    )(lax.axis_index("c").astype(jnp.int32).reshape(1), full, got)


def turn_kernel(proj_ref, factor_ref, gain_ref, cos_ref, sin_ref, q_ref, k_ref, v_ref):
    width = q_ref.shape[1]
    cosine, sine_part = cos_ref[...], sin_ref[...]
    for part, out in enumerate((q_ref, k_ref)):
        factor = columns_of(factor_ref[part : part + 1, :])
        for h in range(0, width, HEAD_DIM):
            raw = proj_ref[:, part * width + h : part * width + h + HEAD_DIM]
            normed = raw * factor * gain_ref[part : part + 1, h : h + HEAD_DIM]
            turned = normed * cosine + halves_swapped(normed) * sine_part
            out[:, h : h + HEAD_DIM] = turned.astype(bf16)
    v_ref[...] = proj_ref[:, 2 * width :].astype(bf16)


def row_block(columns, rows=512):
    return pl.BlockSpec((rows, columns), lambda i: (i, 0))


def lane_block(lines, rows=512):
    return pl.BlockSpec((lines, rows), lambda i: (0, i))


def whole_block(*shape):
    return pl.BlockSpec(shape, lambda i: (0,) * len(shape))


def turn(projected, factors, gains, cosine, sine_part):
    length, columns = projected.shape
    width = columns // 3
    return pl.pallas_call(
        turn_kernel,
        grid=(length // 512,),
        in_specs=[
            row_block(columns),
            lane_block(2),
            whole_block(2, width),
            row_block(HEAD_DIM),
            row_block(HEAD_DIM),
        ],
        out_specs=[row_block(width)] * 3,
        out_shape=[pltpu.HBM((length, width), bf16)] * 3,
        cost_estimate=cost(1),
        name="turn",
    )(projected, factors, gains, cosine, sine_part)


def unturn_kernel(
    dq_ref, dk_ref, proj_ref, factor_ref, gain_ref, cos_ref, sin_ref, out_ref, mix_ref, sum_ref
):
    width = dq_ref.shape[1]
    cosine, sine_part = cos_ref[...], sin_ref[...]

    @pl.when(pl.program_id(0) == 0)
    def _():
        sum_ref[...] = jnp.zeros_like(sum_ref)

    for part, grad_ref in enumerate((dq_ref, dk_ref)):
        factor = columns_of(factor_ref[part : part + 1, :])
        mixed = None
        for h in range(0, width, HEAD_DIM):
            at = part * width + h
            grad = grad_ref[:, h : h + HEAD_DIM]
            turned = grad * cosine - halves_swapped(grad) * sine_part
            raw = proj_ref[:, at : at + HEAD_DIM]
            sums = jnp.sum(turned * raw * factor, axis=0, keepdims=True)
            sum_ref[part : part + 1, h : h + HEAD_DIM] += sums
            weighted = turned * gain_ref[part : part + 1, h : h + HEAD_DIM]
            out_ref[:, at : at + HEAD_DIM] = weighted
            mixed = weighted * raw if mixed is None else mixed + weighted * raw
        mix_ref[part : part + 1, :] = jnp.sum(mixed.T, axis=0, keepdims=True)


def unturn(query_grad, key_grad, projected, factors, gains, cosine, sine_part):
    length, width = query_grad.shape
    query_grad, key_grad, projected = in_hbm(query_grad, key_grad, projected)
    return pl.pallas_call(
        unturn_kernel,
        grid=(length // 512,),
        in_specs=[
            row_block(width),
            row_block(width),
            row_block(3 * width),
            lane_block(2),
            whole_block(2, width),
            row_block(HEAD_DIM),
            row_block(HEAD_DIM),
        ],
        out_specs=[row_block(2 * width), lane_block(2), whole_block(2, width)],
        out_shape=[
            pltpu.HBM((length, 2 * width), f32),
            jax.ShapeDtypeStruct((2, length), f32),
            jax.ShapeDtypeStruct((2, width), f32),
        ],
        cost_estimate=cost(1),
        name="unturn",
    )(query_grad, key_grad, projected, factors, gains, cosine, sine_part)


def finish_kernel(weighted_ref, proj_ref, factor_ref, mix_ref, dv_ref, out_ref):
    width = dv_ref.shape[1]
    for part in range(2):
        factor = columns_of(factor_ref[part : part + 1, :])
        mixing = columns_of(mix_ref[part : part + 1, :])
        for h in range(0, width, HEAD_DIM):
            at = pl.ds(part * width + h, HEAD_DIM)
            grad = weighted_ref[:, at] - proj_ref[:, at] * factor * factor * mixing
            out_ref[:, at] = (factor * grad).astype(bf16)
    out_ref[:, 2 * width :] = dv_ref[...].astype(bf16)


def finish(weighted, projected, factors, mixing, value_grad):
    length, width = value_grad.shape
    return pl.pallas_call(
        finish_kernel,
        grid=(length // 512,),
        in_specs=[
            row_block(2 * width),
            row_block(3 * width),
            lane_block(2),
            lane_block(2),
            row_block(width),
        ],
        out_specs=row_block(3 * width),
        out_shape=jax.ShapeDtypeStruct((length, 3 * width), bf16),
        cost_estimate=cost(1),
        name="finish",
    )(weighted, projected, factors, mixing, value_grad)


def take_rows(block_refs, rows_out):
    for i, block in enumerate(block_refs):

        @pl.when(pl.program_id(0) == i)
        def _(block=block):
            rows_out[...] = block[...]

    return rows_out[...]


def give_part(part, part_refs):
    for i, out in enumerate(part_refs):

        @pl.when(pl.program_id(0) == i)
        def _(out=out):
            out[...] = part.astype(bf16)


def feed_kernel(count, held, *refs):
    block_refs, (in_w, down_w) = refs[:count], refs[count : count + 2]
    outs = refs[count + 2 + held :]
    rows_out, gate_out, up_out, hidden_out = outs[:4]
    units = down_w.shape[0]
    both = product(take_rows(block_refs, rows_out), in_w[...])
    gate, up = both[:, :units], both[:, units:]
    hidden = (gate * jax.nn.sigmoid(gate) * up).astype(bf16)
    gate_out[...], up_out[...], hidden_out[...] = gate.astype(bf16), up.astype(bf16), hidden
    give_part(product(hidden, down_w[...]), outs[4:])


def feed_back_kernel(count, held, *refs):
    block_refs, (in_w, down_w) = refs[:count], refs[count : count + 2]
    gate_in, up_in = refs[count + 2 : count + 4]
    rows_out, grads_out = refs[count + 4 + held : count + 6 + held]
    units = down_w.shape[0]
    hidden_grad = product_right(take_rows(block_refs, rows_out), down_w[...])
    gate, up = gate_in[...].astype(f32), up_in[...].astype(f32)
    sigmoid_gate = jax.nn.sigmoid(gate)
    gate_grad = hidden_grad * up * sigmoid_gate * (1.0 + gate * (1.0 - sigmoid_gate))
    grads_out[:, :units] = gate_grad.astype(bf16)
    grads_out[:, units:] = (hidden_grad * gate * sigmoid_gate).astype(bf16)
    give_part(product_right(grads_out[...], in_w[...]), refs[count + 6 + held :])


def feed_call(kernel, name, blocks, first, length, weights, saved, widths, held):
    count, piece = len(blocks), blocks[0].shape[0]
    held = list(held or ())
    whole = pl.BlockSpec((piece, D), lambda i: (0, 0))

    def rows(columns):
        return pl.BlockSpec((piece, columns), lambda i: (first + i, 0))

    in_specs = [whole] * count + [pl.BlockSpec(memory_space=pltpu.VMEM)] * 2
    in_specs += [rows(array.shape[1]) for array in saved]
    results = pl.pallas_call(
        functools.partial(kernel, count, len(held)),
        grid=(count,),
        in_specs=in_specs + [pl.BlockSpec(memory_space=pltpu.HBM)] * len(held),
        out_specs=[rows(w) for w in widths] + [whole] * count,
        out_shape=[pltpu.HBM((length, w), bf16) for w in widths]
        + [jax.ShapeDtypeStruct((piece, D), bf16)] * count,
        input_output_aliases={len(in_specs) + i: i for i in range(len(held))},
        cost_estimate=cost(1),
        compiler_params=pltpu.CompilerParams(vmem_limit_bytes=24 << 20),
        name=name,
    )(*blocks, *weights, *saved, *held)
    return list(results[: len(widths)]), tuple(results[len(widths) :])


def norm_forward(values, gain_row):
    factor = lax.rsqrt(jnp.mean(values * values, axis=-1, keepdims=True) + norm_epsilon)
    return (values * factor * gain_row, factor)


def norm_backward(values, factor, gain_row, incoming):
    weighted = incoming * gain_row
    mixing = jnp.mean(weighted * values, axis=-1, keepdims=True)
    return (
        factor * (weighted - values * factor * factor * mixing),
        jnp.sum(incoming * values * factor, axis=0),
    )


def arrange(lengths, positions):
    finish = jnp.cumsum(lengths)
    has_ended = finish[None, :] <= positions[:, None]
    return jnp.sum(jnp.where(has_ended, lengths[None, :], 0), axis=1).astype(jnp.int32)


def scatter_over(value, axes):
    return lax.psum_scatter(value.astype(bf16), axes, scatter_dimension=0, tiled=True)


def on_device(
    hidden_in, seq_lengths, qkv_weight, out_weight, in_weight, down_weight, norm_gains, upstream
):
    piece_len, model_width = hidden_in.shape[1:]
    line_sizes = sizes_of(LINE)
    line = line_sizes[0] * line_sizes[1]
    length = piece_len * line * 2
    width = D // (line * 2)
    core = lax.axis_index("c")
    ctx_place = linear([lax.axis_index(a) for a in CTX], sizes_of(CTX))
    data_place = linear([lax.axis_index(a) for a in DATA], sizes_of(DATA))
    line_place = linear([lax.axis_index(a) for a in LINE], line_sizes)
    lengths = lax.dynamic_index_in_dim(seq_lengths, data_place, 0, keepdims=False)
    places = jnp.arange(length, dtype=jnp.int32)
    starts = arrange(lengths, places)
    offset = (places - starts).astype(f32)
    lows = starts[::BLOCK_Q] // BLOCK_K
    starts_row = starts.reshape(1, length)
    inverse = rope_base ** (-2.0 * jnp.arange(HEAD_DIM // 2, dtype=f32) / HEAD_DIM)

    def tables(offset):
        angles = offset[:, None] * inverse[None, :]
        cosine, sine_part = jnp.cos(angles), jnp.sin(angles)
        cosine = jnp.concatenate([cosine, cosine], axis=1)
        return cosine, jnp.concatenate([-sine_part, sine_part], axis=1)

    own_input = hidden_in.reshape(piece_len, model_width)

    row = Line(LINE)

    row_count = qkv_weight.shape[0]
    owners = line * 2
    data_count = sizes_of(DATA)[0] * sizes_of(DATA)[1]
    buffer = [jnp.zeros((line, 2, piece_len, model_width), bf16)]

    def keep_input(k, same, other):
        of_other = k if k == line - 1 else k - 1 if k < line else line - 2
        for at_core, block, at in ((core, same, k), (1 - core, other, of_other)):
            if block is not None:
                buffer[0] = lax.dynamic_update_slice(
                    buffer[0], block[None, None], (row.served(at), at_core, 0, 0)
                )
        return ()

    def weights_step(slot, tied):
        if slot == 0:
            blocks = spread(qkv_weight, 3, owners)
            blocks = exchange_cores(blocks.reshape(line, 2, row_count, 3 * width))
            return (blocks, in_weight, offset)
        if slot == 1:
            down = lax.all_gather(down_weight, DATA, axis=0, tiled=True)
            blocks = spread(tied[0][1], 2 * data_count, owners)
            return (chips_start(tied[0][0], LINE), down, blocks, tables(tied[0][2]))
        if slot == 2:
            return cores_start(tied[1][2].reshape((line, 2) + tied[1][2].shape[1:]))
        if slot == line - 1:
            return (out_weight, tied[2])
        return ()

    plan = [[0], [1], []] + [[slot - 1] for slot in range(3, line)]
    swaps = [[0], [], [1, 2]] + [[k] for k in range(3, line)]
    _, tied = row.gather(own_input, keep_input, weights_step, plan, swaps)
    full_input = buffer[0].reshape(length, model_width)
    qkv_rows = by_source(tied[1][0], LINE).reshape(-1, 3 * width)
    qkv_here = lax.all_gather(qkv_rows, DATA, axis=0, tiled=True)
    down_here, (cosine, sine_part) = tied[1][1], tied[1][3]
    units = down_here.shape[0]
    out_shuffled, (in_keep, in_got) = tied[line - 1]
    out_pieces = shifts(lambda steps: out_shuffled, LINE)

    projected, squares = project(full_input, qkv_here)
    squares, out_pieces, in_got = together(squares, out_pieces, in_got)
    out_line = by_source(out_pieces, LINE)
    out_half = lax.all_gather(out_line.reshape(-1, D), DATA, axis=0, tiled=True)
    in_pieces = chips_start(by_core(in_keep, in_got), LINE)
    factors = lax.rsqrt(small_sum(squares, CTX) / D + norm_epsilon)
    gains_here = lax.dynamic_slice(norm_gains, (0, ctx_place * width), (2, width))
    query_low, key_low, value_low = turn(projected, factors, gains_here, cosine, sine_part)
    head_out, log_total = attend(lows, starts_row, query_low, key_low, value_low)

    blocks = head_out.astype(bf16).reshape(line, 2, piece_len, width)
    keep, got = cores_start(blocks)
    got, in_pieces, out_half = together(got, in_pieces, out_half)
    out_half = out_half.reshape(-1, out_weight.shape[0], D)
    out_other = swap(out_half)
    in_rows = by_source(in_pieces, LINE)
    in_here = lax.all_gather(in_rows.reshape(-1, in_rows.shape[-1]), DATA, axis=0, tiled=True)
    out_full = by_core(out_half, out_other).reshape(D, D)
    pieces, out_full = together(chips_start(by_core(keep, got), LINE), out_full)
    attended = by_source(pieces, LINE)
    attended_low = attended.reshape(line * 2, piece_len, width).transpose(1, 0, 2)
    attended_low = attended_low.reshape(piece_len, D)
    branch = product(attended_low, out_full)
    branch_normed, branch_factor = norm_forward(branch, norm_gains[2])
    residual = own_input.astype(f32) + branch_normed
    residual_low = residual.astype(bf16)

    def chip_sums(results):
        def parts(k):
            if k == line - 1:
                other = results[k][1]
            else:
                other = results[line][0] if k == line - 2 else results[k + 1][1]
            return scatter_sum(results[k][0], other)

        return parts

    def window_of(k):
        return 2 * line - 2 if k == 0 else 2 * line - 1 if k == line else 2 * (k - 1)

    held = {}
    weights_here = tuple(
        pltpu.with_memory_space_constraint(w, pltpu.VMEM) for w in (in_here, down_here)
    )

    def forward_chip(k, same, other):
        blocks = [b for b in (same, other) if b is not None]
        held["forward"], parts = feed_call(
            feed_kernel, "feed", blocks, window_of(k), length, weights_here, (),
            (D, units, units, units), held.get("forward"),
        )
        return parts

    plan = [[], [0], [1, 2]] + [[k] for k in range(3, line - 1)] + [[]]
    forward, _ = row.gather(residual_low, forward_chip, plan=plan)
    residual_all, gate_all, up_all, hidden_all = held["forward"]
    second, _ = row.scatter(chip_sums(forward))
    second_normed, second_factor = norm_forward(second, norm_gains[3])
    result = residual + second_normed
    live_places = ctx_place * piece_len + jnp.arange(piece_len, dtype=jnp.int32)
    live_rows = (live_places < jnp.sum(lengths)).astype(f32)[:, None]
    sums = jnp.stack(
        [
            jnp.sum(result * result * live_rows),
            jnp.sum(branch * branch * live_rows),
            jnp.sum(second * second * live_rows),
        ]
    )

    incoming = upstream.reshape(piece_len, model_width).astype(f32)
    second_grad, second_gain_grad = norm_backward(second, second_factor, norm_gains[3], incoming)

    def backward_chip(k, same, other):
        blocks = [b for b in (same, other) if b is not None]
        held["backward"], parts = feed_call(
            feed_back_kernel, "feed_back", blocks, window_of(k), length, weights_here,
            (gate_all, up_all), (D, 2 * units), held.get("backward"),
        )
        return parts

    backward, _ = row.gather(second_grad.astype(bf16), backward_chip)
    second_grad_all, gate_up_grads = held["backward"]

    def weight_grads(slot, tied):
        if slot == 1:
            return (product_left(residual_all, gate_up_grads).astype(bf16),)
        if slot == 2:
            return (product_left(hidden_all, second_grad_all).astype(bf16),)
        return ()

    residual_part, tied = row.scatter(chip_sums(backward), weight_grads)
    grad_in, grad_down = tied[0][0], tied[1][0]
    residual_grad = incoming + residual_part
    grad_in = scatter_over(grad_in, DATA).reshape(in_rows.shape)

    branch_grad, branch_gain_grad = norm_backward(
        branch, branch_factor, norm_gains[2], residual_grad
    )
    branch_grad_low = branch_grad.astype(bf16)
    attended_grad = product_right(branch_grad_low, out_full).astype(bf16)
    attended_grad = attended_grad.reshape(piece_len, line, 2, width).transpose(1, 2, 0, 3)
    keep, give = pick(attended_grad, core, 1), pick(attended_grad, 1 - core, 1)
    give, branch_grad_low = together(give, branch_grad_low)
    out_grad = product_left(attended_low, branch_grad_low).astype(bf16)
    out_grad = out_grad.reshape(-1, 2, out_weight.shape[0], D)
    got, out_grad, grad_in = together(swap(give), out_grad, grad_in)
    pieces = chips_start(by_core(keep, got), LINE)
    in_keep, in_got = cores_start(grad_in.reshape((line, 2) + in_rows.shape[2:]))
    out_got = swap(pick(out_grad, 1 - core, 1))
    pieces, in_got, out_got = together(pieces, in_got, out_got)
    head_grad = by_source(pieces, LINE).reshape(length, width)
    in_pieces = chips_start(by_core(in_keep, in_got), LINE)
    out_grad = join(out_grad, out_got)
    head_grad, out_grad = together(head_grad, out_grad)
    out_grad = scatter_over(out_grad.reshape(D // 2, D), DATA)
    out_grad = out_grad.reshape((line,) + out_weight.shape)

    query_grad, key_grad, value_grad = attend_back(
        lows, starts_row, query_low, key_low, value_low, head_out, log_total, head_grad
    )
    weighted, mixing, gain_grads = unturn(
        query_grad, key_grad, projected, factors, gains_here, cosine, sine_part
    )
    mixing, in_pieces, grad_down = together(mixing, in_pieces, grad_down)
    grad_down = scatter_over(grad_down, DATA)
    mixing = small_sum(mixing, CTX) / D
    projected_grad = finish(weighted, projected, factors, mixing, value_grad)
    out_steps = offsets(LINE)

    def out_pieces(turn):
        return [shift(pick(out_grad, place(LINE, steps)), LINE, steps) for steps in turn]

    projected_grad, near = together(projected_grad, out_pieces(out_steps[:-1]))
    grad_blocks = projected_grad.reshape(line, 2, piece_len, 3 * width)

    later = []

    def input_product(k):
        rows = pick(grad_blocks, row.served(k))
        rows = jnp.concatenate([pick(rows, core), pick(rows, 1 - core)], axis=0)
        return product_right(rows, qkv_here).astype(bf16)

    def input_chip(k):
        part = row.tied[0][2] if k == line - 4 else input_product(k)
        part = scatter_sum(part[:piece_len], part[piece_len:])
        if not later:
            later.extend(together(part, projected_grad))
            part = later[0]
        return part

    def step(rows, axis):
        if lax.axis_size(axis) == 2:
            return (rows, lax.ppermute(rows, axis, [(0, 1), (1, 0)]))
        return (lax.psum(rows, axis),)

    def last_grads(slot, tied):
        if slot == 1:
            grads = product_left(full_input, later[1]).astype(bf16)
            return (grads, gain_grads, input_product(line - 4), out_pieces(out_steps[-1:]))
        if slot == 2:
            rows = jnp.zeros((5, D), f32)
            rows = lax.dynamic_update_slice(rows, tied[0][1], (0, ctx_place * width))
            rows = rows.at[2].set(branch_gain_grad).at[3].set(second_gain_grad)
            rows = rows.at[4, :3].set(sums)
            return (scatter_over(tied[0][0], DATA), step(rows, "c"), grad_down)
        if slot == line - 1:
            blocks = tied[1][0].reshape(line, 2, row_count, 3 * width)
            return (cores_start(blocks), step(sum(tied[1][1]), "zl"), in_pieces, tied[1][2])
        return ()

    plan = [[line - 2, line - 3]] + [[k] for k in range(line - 4, -1, -1)] + [[]]
    input_part, tied = row.scatter(input_chip, last_grads, plan)
    qkv_cores, gain_rows, in_pieces, grad_down = tied[line - 2]
    qkv_pieces = chips_start(by_core(*qkv_cores), LINE)
    gain_rows, qkv_pieces = together(step(sum(gain_rows), "zh"), qkv_pieces)
    gain_rows = sum(gain_rows)
    if sizes_of(DATA) == (2, 2):
        sides = [shift(gain_rows, DATA, steps) for steps in offsets(DATA)]
        gain_rows = (sides[0] + sides[1]) + (sides[2] + sides[3])
    else:
        gain_rows = small_sum(gain_rows, ("dl", "dh"))
    input_grad = residual_grad + input_part
    grad_in = by_source(in_pieces, LINE)
    grad_in = collect(grad_in.reshape((owners,) + grad_in.shape[2:]), 2 * data_count)
    grad_down = grad_down.astype(f32)
    grad_out = sum(piece.astype(f32) for piece in near + tied[0][3])
    grad_qkv = by_source(qkv_pieces, LINE)
    grad_qkv = collect(grad_qkv.reshape(owners, row_count, 3 * width), 3)
    live_count = jnp.sum(seq_lengths).astype(f32)
    rms_values = jnp.sqrt(gain_rows[4, :3] / (live_count * model_width))
    return (
        result.astype(bf16)[None],
        input_grad[None],
        grad_qkv,
        grad_out,
        grad_in,
        grad_down,
        gain_rows[:4],
        rms_values,
    )


def solution(mesh):
    dp, ctx = mesh.shape["dp"], mesh.shape["ctx"]
    fine = Mesh(mesh.devices.reshape(2, dp // 2, 2, ctx // 4, 2), AXES)
    return jax.shard_map(
        on_device,
        mesh=fine,
        in_specs=(
            P(DATA, CTX, None),
            P(),
            P(AXES, None),
            P(AXES, None),
            P(AXES, None),
            P(AXES, None),
            P(),
            P(DATA, CTX, None),
        ),
        out_specs=(
            P(DATA, CTX, None),
            P(DATA, CTX, None),
            P(AXES, None),
            P(AXES, None),
            P(AXES, None),
            P(AXES, None),
            P(),
            P(),
        ),
        check_vma=False,
    )
```

```python
import functools
import itertools

import jax
import jax.numpy as jnp
import numpy as np
from jax import lax
from jax.experimental import pallas as pl
from jax.experimental.pallas import tpu as pltpu
from jax.sharding import Mesh
from jax.sharding import PartitionSpec as P

D = 2048
HEADS = 16
HEAD_DIM = 128
FF = 8192

norm_epsilon = 1e-06
rope_base = 500000.0
masked_score = -1e30
scale_factor = HEAD_DIM ** (-0.5)

AXES = ("dh", "dl", "zh", "zl", "c")
DATA = ("dh", "dl")
LINE = ("zh", "zl")
CTX = ("zh", "zl", "c")

BLOCK_Q = 512
BLOCK_K = 512

bf16 = jnp.bfloat16
f32 = jnp.float32


def sizes_of(axes):
    return tuple(lax.axis_size(a) for a in axes)


def offsets(axes):
    return list(itertools.product(*[range(n) for n in sizes_of(axes)]))


def linear(index, sizes):
    total = 0
    for i, n in zip(index, sizes):
        total = total * n + i
    return total


def shift(value, axes, steps):
    if not any(steps):
        return value
    sizes = sizes_of(axes)
    pairs = []
    for index in itertools.product(*[range(n) for n in sizes]):
        target = tuple((i + s) % n for i, s, n in zip(index, steps, sizes))
        pairs.append((linear(index, sizes), linear(target, sizes)))
    return lax.ppermute(value, axes, pairs)


def swap(value):
    return lax.ppermute(value, "c", [(0, 1), (1, 0)])


def place(axes, steps, sign=1):
    sizes = sizes_of(axes)
    here = [(lax.axis_index(a) + sign * s) % n for a, s, n in zip(axes, steps, sizes)]
    return linear(here, sizes)


def pick(value, index, axis=0):
    return lax.dynamic_index_in_dim(value, index, axis, keepdims=False)


def put(buffer, value, index):
    return lax.dynamic_update_slice_in_dim(buffer, value[None], index, 0)


def together(*values):
    return lax.optimization_barrier(values)


def line_order(count):
    return np.array(
        [sorted(range(count), key=lambda j: (abs(i - j), j != i ^ 1)) for i in range(count)],
        dtype=np.int32,
    )


class Line:
    def __init__(self, axes):
        self.axes = axes
        sizes = sizes_of(axes)
        self.count = sizes[0] * sizes[1]
        self.place = linear([lax.axis_index(a) for a in axes], sizes)
        self.order = line_order(self.count)

    def served(self, k):
        return jnp.asarray(self.order[:, k])[self.place]

    def hop(self, value, step, keep=lambda i: True):
        pairs = [
            (i, i + step) for i in range(self.count) if 0 <= i + step < self.count and keep(i)
        ]
        return lax.ppermute(value, self.axes, pairs)

    def choose(self, options, wanted):
        used = sorted({w for w in wanted if w is not None})
        value = options[used[0]]
        for w in used[1:]:
            mask = np.array([v == w for v in wanted])
            value = jnp.where(jnp.asarray(mask)[self.place], options[w], value)
        return value

    def gather(self, block, work, extra=None, plan=None, swaps=None):
        last = self.count - 1
        plan = plan or [[k] for k in range(last)] + [[]]
        swaps = swaps or [[k] for k in range(last + 1)]
        options, results, tied, arrived, other = {}, [], [], [], {-1: None}
        for slot in range(self.count):
            if slot:
                wanted = []
                for i in range(self.count):
                    j = self.order[i, slot]
                    wanted.append((1, i - j) if j < i else (-1, j - i))
                arrived.append(self.choose(options, wanted))
            else:
                arrived.append(block)
            moved = ()
            if slot < last:
                moved = tuple(
                    self.hop(options[(step, slot)] if slot else block, step) for step in (1, -1)
                )
            swapped = [swap(arrived[k]) for k in swaps[slot]]
            done = [work(k, arrived[k], other[k - 1]) for k in plan[slot]]
            more = extra(slot, tied) if extra else ()
            moved, swapped, done, more = together(moved, swapped, done, more)
            if moved:
                options[(1, slot + 1)], options[(-1, slot + 1)] = moved
            other.update(zip(swaps[slot], swapped))
            tied.append(more)
            results += done
        results.append(work(last, arrived[last], other[last]))
        results.append(work(self.count, None, other[last - 1]))
        return results, tied

    def hop_values(self, made, far, last):
        wanted = {}
        for step in (1, -1):
            wanted[step] = []
            for i in range(self.count):
                j = i + step * far
                known = 0 <= j < self.count
                wanted[step].append(int(np.argmax(self.order[i] == j)) if known else None)
        used = sorted({w for side in wanted.values() for w in side if w is not None})
        if last[1] is not None and len(used) == 2:
            flags = [[int(w == used[1]) for w in wanted[step]] for step in (1, -1)]
            flags = jnp.asarray(np.array(flags, dtype=np.int32))[:, self.place]
            return combine(flags, made[used[0]], made[used[1]], last[1], last[-1])
        values = []
        for step in (1, -1):
            value = self.choose(made, wanted[step])
            if last[step] is not None:
                value = value.astype(f32) + last[step].astype(f32)
            values.append(value.astype(bf16))
        return values

    def scatter(self, parts, fill=None, plan=None):
        count = self.count
        plan = plan or [[k] for k in range(count - 2, -1, -1)]
        made = {count - 1: parts(count - 1)}
        last = {1: None, -1: None}
        tied = self.tied = []
        for slot in range(1, count):
            far = count - slot
            values = self.hop_values(made, far, last)
            moved = []
            for step, value in zip((1, -1), values):
                keep = lambda i: 0 <= i + step * far < count
                moved.append(self.hop(value, step, keep))
            done = [parts(k) for k in plan[slot - 1]]
            more = fill(slot, tied) if fill else ()
            moved, done, more = together(moved, done, more)
            tied.append(more)
            made.update(zip(plan[slot - 1], done))
            last[1], last[-1] = moved
        total = made[0].astype(f32) + last[1].astype(f32) + last[-1].astype(f32)
        return total, tied


def combine_kernel(flag_ref, one_ref, two_ref, right_ref, left_ref, right_out, left_out):
    for i, (last, out) in enumerate(((right_ref, right_out), (left_ref, left_out))):
        chosen = jnp.where(flag_ref[i] == 0, one_ref[...], two_ref[...])
        out[...] = (chosen.astype(f32) + last[...].astype(f32)).astype(bf16)


def combine(flags, one, two, right, left):
    rows, columns = one.shape
    block = pl.BlockSpec((rows, columns), lambda i, flags: (0, 0))
    return pl.pallas_call(
        combine_kernel,
        grid_spec=pltpu.PrefetchScalarGridSpec(
            num_scalar_prefetch=1, grid=(1,), in_specs=[block] * 4, out_specs=[block] * 2
        ),
        out_shape=[jax.ShapeDtypeStruct((rows, columns), bf16)] * 2,
        cost_estimate=cost(1),
        compiler_params=pltpu.CompilerParams(vmem_limit_bytes=16 << 20),
        name="combine",
    )(flags, one, two, right, left)


def scatter_sum(for_same, for_other):
    return (for_same.astype(f32) + swap(for_other.astype(bf16)).astype(f32)).astype(bf16)


def cores_start(blocks):
    core = lax.axis_index("c")
    return pick(blocks, core, 1), swap(pick(blocks, 1 - core, 1))


def exchange_cores(blocks):
    return by_core(*cores_start(blocks))


def by_core(mine, other):
    shape = (mine.shape[0], 2) + mine.shape[1:]
    here = lax.broadcasted_iota(jnp.int32, shape, 1) == lax.axis_index("c")
    return jnp.where(here, mine[:, None], other[:, None])


def assemble_kernel(*refs):
    out_ref = refs[-1]
    for i, piece in enumerate(refs[1:-1]):

        @pl.when(pl.program_id(0) == i)
        def _(piece=piece):
            out_ref[0] = piece[...]


def assemble(pieces, places):
    shape = pieces[0].shape
    block = pl.BlockSpec(shape, lambda i, places: (0,) * len(shape))
    return pl.pallas_call(
        assemble_kernel,
        grid_spec=pltpu.PrefetchScalarGridSpec(
            num_scalar_prefetch=1,
            grid=(len(pieces),),
            in_specs=[block] * len(pieces),
            out_specs=pl.BlockSpec((1,) + shape, lambda i, places: (places[i],) + (0,) * len(shape)),
        ),
        out_shape=jax.ShapeDtypeStruct((len(pieces),) + shape, pieces[0].dtype),
        compiler_params=pltpu.CompilerParams(vmem_limit_bytes=18 << 20),
        cost_estimate=cost(2),
        name="assemble",
    )(jnp.stack(places).astype(jnp.int32), *pieces)


def shifts(value_for, chips):
    return tuple(shift(value_for(steps), chips, steps) for steps in offsets(chips))


def by_source(pieces, chips):
    return assemble(pieces, [place(chips, steps, -1) for steps in offsets(chips)])


def chips_start(pairs, chips):
    return shifts(lambda steps: pick(pairs, place(chips, steps)), chips)


def exchange_chips(pairs, chips):
    return by_source(chips_start(pairs, chips), chips)


def exchange(blocks, chips):
    return exchange_chips(exchange_cores(blocks), chips)


def small_sum(value, axes):
    for axis in axes:
        if lax.axis_size(axis) == 2:
            value = value + lax.ppermute(value, axis, [(0, 1), (1, 0)])
        else:
            value = lax.psum(value, axis)
    return value


def product(left_side, right_side):
    return jnp.dot(left_side, right_side, preferred_element_type=f32)


def product_left(left_side, right_side):
    return lax.dot_general(
        left_side, right_side, (((0,), (0,)), ((), ())), preferred_element_type=f32
    )


def product_right(left_side, right_side):
    return lax.dot_general(
        left_side, right_side, (((1,), (1,)), ((), ())), preferred_element_type=f32
    )


def cost(microseconds):
    return pl.CostEstimate(
        flops=int(microseconds * 1.0e9),
        transcendentals=0,
        bytes_accessed=int(microseconds * 3.0e6),
    )


def allowed_keys(shape, key_start, query_start, starts):
    key_place = key_start + lax.broadcasted_iota(jnp.int32, shape, 0)
    query_place = query_start + lax.broadcasted_iota(jnp.int32, shape, 1)
    return (key_place >= starts) & (key_place <= query_place)


def heads_of(width):
    return [slice(h, h + HEAD_DIM) for h in range(0, width, HEAD_DIM)]


def attend_kernel(low_ref, starts_ref, q_ref, k_ref, v_ref, out_ref, log_ref):
    block = pl.program_id(0)
    bq, bk = q_ref.shape[0], BLOCK_K
    starts, heads = starts_ref[...], heads_of(q_ref.shape[1])

    def step(j, carry):
        rows = pl.ds(pl.multiple_of(j * bk, bk), bk)
        ok = allowed_keys((bk, bq), j * bk, block * bq, starts)
        results = []
        for head, (top, total, acc) in zip(heads, carry):
            scores = product_right(k_ref[rows, head], q_ref[:, head]) * scale_factor
            scores = jnp.where(ok, scores, masked_score)
            new_top = jnp.maximum(top, jnp.max(scores, axis=0, keepdims=True))
            ratio = jnp.exp(top - new_top)
            expanded = jnp.exp(scores - new_top)
            total = total * ratio + jnp.sum(expanded, axis=0, keepdims=True)
            acc = acc * ratio + product_left(v_ref[rows, head], expanded.astype(bf16))
            results.append((new_top, total, acc))
        return tuple(results)

    init = (
        jnp.full((1, bq), masked_score, f32),
        jnp.zeros((1, bq), f32),
        jnp.zeros((HEAD_DIM, bq), f32),
    )
    final = lax.fori_loop(
        low_ref[block], (block * bq + bq) // bk, step, tuple(init for _ in heads)
    )
    for h, (head, (top, total, acc)) in enumerate(zip(heads, final)):
        out_ref[:, head] = (acc / total).T
        log_ref[h] = top + jnp.log(total)


def in_hbm(*arrays):
    return tuple(pltpu.with_memory_space_constraint(a, pltpu.HBM) for a in arrays)


def attend(lows, starts, queries, keys, values):
    length, width = queries.shape
    queries, keys, values = in_hbm(queries, keys, values)
    heads, bq = width // HEAD_DIM, BLOCK_Q
    whole = pl.BlockSpec((length, width), lambda i, low: (0, 0))
    part = pl.BlockSpec((bq, width), lambda i, low: (i, 0))
    return pl.pallas_call(
        attend_kernel,
        grid_spec=pltpu.PrefetchScalarGridSpec(
            num_scalar_prefetch=1,
            grid=(length // bq,),
            in_specs=[pl.BlockSpec((1, bq), lambda i, low: (0, i)), part, whole, whole],
            out_specs=[part, pl.BlockSpec((heads, 1, bq), lambda i, low: (0, 0, i))],
        ),
        out_shape=[
            pltpu.HBM((length, width), f32),
            jax.ShapeDtypeStruct((heads, 1, length), f32),
        ],
        compiler_params=pltpu.CompilerParams(vmem_limit_bytes=24 << 20),
        cost_estimate=cost(16),
        name="attend",
    )(lows, starts, queries, keys, values)


def attend_back_kernel(
    low_ref, starts_ref, q_ref, k_ref, v_ref, out_ref, log_ref, grad_ref, dq_ref, dk_ref, dv_ref
):
    block = pl.program_id(0)
    bq, bk = q_ref.shape[0], BLOCK_K
    starts, heads = starts_ref[...], heads_of(q_ref.shape[1])

    @pl.when(block == 0)
    def _():
        dk_ref[...] = jnp.zeros_like(dk_ref)
        dv_ref[...] = jnp.zeros_like(dv_ref)

    inner = [
        jnp.sum((grad_ref[:, head].astype(f32) * out_ref[:, head]).T, axis=0, keepdims=True)
        for head in heads
    ]

    def step(j, carry):
        rows = pl.ds(pl.multiple_of(j * bk, bk), bk)
        ok = allowed_keys((bk, bq), j * bk, block * bq, starts)
        results = []
        for h, (head, acc) in enumerate(zip(heads, carry)):
            keys, queries, grads = k_ref[rows, head], q_ref[:, head], grad_ref[:, head]
            scores = product_right(keys, queries) * scale_factor
            probs = jnp.where(ok, jnp.exp(scores - log_ref[h]), 0.0)
            dv_ref[rows, head] += product(probs.astype(bf16), grads)
            prob_grad = product_right(v_ref[rows, head], grads)
            score_grad = (probs * (prob_grad - inner[h])).astype(bf16)
            dk_ref[rows, head] += product(score_grad, queries) * scale_factor
            results.append(acc + product_left(keys, score_grad))
        return tuple(results)

    final = lax.fori_loop(
        low_ref[block],
        (block * bq + bq) // bk,
        step,
        tuple(jnp.zeros((HEAD_DIM, bq), f32) for _ in heads),
    )
    for head, acc in zip(heads, final):
        dq_ref[:, head] = (acc * scale_factor).T


def attend_back(lows, starts, queries, keys, values, out, log_total, grads):
    length, width = queries.shape
    heads, bq = width // HEAD_DIM, BLOCK_Q
    whole = pl.BlockSpec((length, width), lambda i, low: (0, 0))
    part = pl.BlockSpec((bq, width), lambda i, low: (i, 0))
    return pl.pallas_call(
        attend_back_kernel,
        grid_spec=pltpu.PrefetchScalarGridSpec(
            num_scalar_prefetch=1,
            grid=(length // bq,),
            in_specs=[
                pl.BlockSpec((1, bq), lambda i, low: (0, i)),
                part,
                whole,
                whole,
                part,
                pl.BlockSpec((heads, 1, bq), lambda i, low: (0, 0, i)),
                part,
            ],
            out_specs=[part, whole, whole],
        ),
        out_shape=[pltpu.HBM((length, width), f32)] * 3,
        compiler_params=pltpu.CompilerParams(vmem_limit_bytes=32 << 20),
        cost_estimate=cost(26),
        name="attend_back",
    )(lows, starts, queries, keys, values, out, log_total, grads)


def spread_kernel(in_ref, out_ref):
    unit = out_ref.shape[2]
    for k in range(out_ref.shape[0]):
        out_ref[k] = in_ref[:, k * unit : (k + 1) * unit]


def spread(weight, groups, owners):
    rows, columns = weight.shape
    unit = columns // (groups * owners)
    if unit % 128:
        shaped = weight.reshape(rows, groups, owners, unit).transpose(2, 0, 1, 3)
        return shaped.reshape(owners, rows, groups * unit)
    return pl.pallas_call(
        spread_kernel,
        grid=(groups,),
        in_specs=[pl.BlockSpec((rows, owners * unit), lambda g: (0, g))],
        out_specs=pl.BlockSpec((owners, rows, unit), lambda g: (0, 0, g)),
        out_shape=jax.ShapeDtypeStruct((owners, rows, groups * unit), weight.dtype),
        cost_estimate=cost(4),
        name="spread",
    )(weight)


def collect_kernel(in_ref, out_ref):
    unit = in_ref.shape[2]
    for k in range(in_ref.shape[0]):
        out_ref[:, k * unit : (k + 1) * unit] = in_ref[k].astype(f32)


def collect(blocks, groups):
    owners, rows, columns = blocks.shape
    unit = columns // groups
    if unit % 128:
        shaped = blocks.reshape(owners, rows, groups, unit).transpose(1, 2, 0, 3)
        return shaped.reshape(rows, groups * owners * unit).astype(f32)
    return pl.pallas_call(
        collect_kernel,
        grid=(groups,),
        in_specs=[pl.BlockSpec((owners, rows, unit), lambda g: (0, 0, g))],
        out_specs=pl.BlockSpec((rows, owners * unit), lambda g: (0, g)),
        out_shape=jax.ShapeDtypeStruct((rows, groups * owners * unit), f32),
        cost_estimate=cost(5),
        name="collect",
    )(blocks)


def columns_of(row):
    return jnp.broadcast_to(row, (HEAD_DIM, row.shape[1])).T


def halves_swapped(values):
    return pltpu.roll(values, HEAD_DIM // 2, 1)


def project_kernel(in_ref, weight_ref, out_ref, square_ref):
    width = out_ref.shape[1] // 3
    out = product(in_ref[...], weight_ref[...])
    out_ref[...] = out
    for part in range(2):
        total = None
        for h in range(0, width, HEAD_DIM):
            raw = out[:, part * width + h : part * width + h + HEAD_DIM]
            total = raw * raw if total is None else total + raw * raw
        square_ref[part : part + 1, :] = jnp.sum(total.T, axis=0, keepdims=True)


def project(inputs, weight):
    length, depth = inputs.shape
    columns = weight.shape[1]
    return pl.pallas_call(
        project_kernel,
        grid=(length // 256,),
        in_specs=[row_block(depth, 256), whole_block(depth, columns)],
        out_specs=[row_block(columns, 256), lane_block(2, 256)],
        out_shape=[
            pltpu.HBM((length, columns), f32),
            jax.ShapeDtypeStruct((2, length), f32),
        ],
        compiler_params=pltpu.CompilerParams(vmem_limit_bytes=18 << 20),
        cost_estimate=cost(10),
        name="project",
    )(inputs, weight)


def join_kernel(core_ref, full_ref, got_ref, out_ref):
    out_ref[...] = (full_ref[:, 0].astype(f32) + got_ref[...].astype(f32)).astype(bf16)


def join(full, got):
    count, _, rows, columns = full.shape
    step = 4 if count % 4 == 0 else 1
    part = pl.BlockSpec((step, rows, columns), lambda i, core: (i, 0, 0))
    return pl.pallas_call(
        join_kernel,
        grid_spec=pltpu.PrefetchScalarGridSpec(
            num_scalar_prefetch=1,
            grid=(count // step,),
            in_specs=[
                pl.BlockSpec((step, 1, rows, columns), lambda i, core: (i, core[0], 0, 0)),
                part,
            ],
            out_specs=part,
        ),
        out_shape=jax.ShapeDtypeStruct((count, rows, columns), bf16),
        cost_estimate=cost(1),
        name="join",
    )(lax.axis_index("c").astype(jnp.int32).reshape(1), full, got)


def turn_kernel(proj_ref, factor_ref, gain_ref, cos_ref, sin_ref, q_ref, k_ref, v_ref):
    width = q_ref.shape[1]
    cosine, sine_part = cos_ref[...], sin_ref[...]
    for part, out in enumerate((q_ref, k_ref)):
        factor = columns_of(factor_ref[part : part + 1, :])
        for h in range(0, width, HEAD_DIM):
            raw = proj_ref[:, part * width + h : part * width + h + HEAD_DIM]
            normed = raw * factor * gain_ref[part : part + 1, h : h + HEAD_DIM]
            turned = normed * cosine + halves_swapped(normed) * sine_part
            out[:, h : h + HEAD_DIM] = turned.astype(bf16)
    v_ref[...] = proj_ref[:, 2 * width :].astype(bf16)


def row_block(columns, rows=512):
    return pl.BlockSpec((rows, columns), lambda i: (i, 0))


def lane_block(lines, rows=512):
    return pl.BlockSpec((lines, rows), lambda i: (0, i))


def whole_block(*shape):
    return pl.BlockSpec(shape, lambda i: (0,) * len(shape))


def turn(projected, factors, gains, cosine, sine_part):
    length, columns = projected.shape
    width = columns // 3
    return pl.pallas_call(
        turn_kernel,
        grid=(length // 512,),
        in_specs=[
            row_block(columns),
            lane_block(2),
            whole_block(2, width),
            row_block(HEAD_DIM),
            row_block(HEAD_DIM),
        ],
        out_specs=[row_block(width)] * 3,
        out_shape=[pltpu.HBM((length, width), bf16)] * 3,
        cost_estimate=cost(1),
        name="turn",
    )(projected, factors, gains, cosine, sine_part)


def unturn_kernel(
    dq_ref, dk_ref, proj_ref, factor_ref, gain_ref, cos_ref, sin_ref, out_ref, mix_ref, sum_ref
):
    width = dq_ref.shape[1]
    cosine, sine_part = cos_ref[...], sin_ref[...]

    @pl.when(pl.program_id(0) == 0)
    def _():
        sum_ref[...] = jnp.zeros_like(sum_ref)

    for part, grad_ref in enumerate((dq_ref, dk_ref)):
        factor = columns_of(factor_ref[part : part + 1, :])
        mixed = None
        for h in range(0, width, HEAD_DIM):
            at = part * width + h
            grad = grad_ref[:, h : h + HEAD_DIM]
            turned = grad * cosine - halves_swapped(grad) * sine_part
            raw = proj_ref[:, at : at + HEAD_DIM]
            sums = jnp.sum(turned * raw * factor, axis=0, keepdims=True)
            sum_ref[part : part + 1, h : h + HEAD_DIM] += sums
            weighted = turned * gain_ref[part : part + 1, h : h + HEAD_DIM]
            out_ref[:, at : at + HEAD_DIM] = weighted
            mixed = weighted * raw if mixed is None else mixed + weighted * raw
        mix_ref[part : part + 1, :] = jnp.sum(mixed.T, axis=0, keepdims=True)


def unturn(query_grad, key_grad, projected, factors, gains, cosine, sine_part):
    length, width = query_grad.shape
    query_grad, key_grad, projected = in_hbm(query_grad, key_grad, projected)
    return pl.pallas_call(
        unturn_kernel,
        grid=(length // 512,),
        in_specs=[
            row_block(width),
            row_block(width),
            row_block(3 * width),
            lane_block(2),
            whole_block(2, width),
            row_block(HEAD_DIM),
            row_block(HEAD_DIM),
        ],
        out_specs=[row_block(2 * width), lane_block(2), whole_block(2, width)],
        out_shape=[
            pltpu.HBM((length, 2 * width), f32),
            jax.ShapeDtypeStruct((2, length), f32),
            jax.ShapeDtypeStruct((2, width), f32),
        ],
        cost_estimate=cost(1),
        name="unturn",
    )(query_grad, key_grad, projected, factors, gains, cosine, sine_part)


def finish_kernel(weighted_ref, proj_ref, factor_ref, mix_ref, dv_ref, out_ref):
    width = dv_ref.shape[1]
    for part in range(2):
        factor = columns_of(factor_ref[part : part + 1, :])
        mixing = columns_of(mix_ref[part : part + 1, :])
        for h in range(0, width, HEAD_DIM):
            at = pl.ds(part * width + h, HEAD_DIM)
            grad = weighted_ref[:, at] - proj_ref[:, at] * factor * factor * mixing
            out_ref[:, at] = (factor * grad).astype(bf16)
    out_ref[:, 2 * width :] = dv_ref[...].astype(bf16)


def finish(weighted, projected, factors, mixing, value_grad):
    length, width = value_grad.shape
    return pl.pallas_call(
        finish_kernel,
        grid=(length // 512,),
        in_specs=[
            row_block(2 * width),
            row_block(3 * width),
            lane_block(2),
            lane_block(2),
            row_block(width),
        ],
        out_specs=row_block(3 * width),
        out_shape=jax.ShapeDtypeStruct((length, 3 * width), bf16),
        cost_estimate=cost(1),
        name="finish",
    )(weighted, projected, factors, mixing, value_grad)


def take_rows(block_refs, rows_out):
    for i, block in enumerate(block_refs):

        @pl.when(pl.program_id(0) == i)
        def _(block=block):
            rows_out[...] = block[...]

    return rows_out[...]


def give_part(part, part_refs):
    for i, out in enumerate(part_refs):

        @pl.when(pl.program_id(0) == i)
        def _(out=out):
            out[...] = part.astype(bf16)


def feed_kernel(count, held, *refs):
    block_refs, (in_w, down_w) = refs[:count], refs[count : count + 2]
    outs = refs[count + 2 + held :]
    rows_out, gate_out, up_out, hidden_out = outs[:4]
    units = down_w.shape[0]
    both = product(take_rows(block_refs, rows_out), in_w[...])
    gate, up = both[:, :units], both[:, units:]
    hidden = (gate * jax.nn.sigmoid(gate) * up).astype(bf16)
    gate_out[...], up_out[...], hidden_out[...] = gate.astype(bf16), up.astype(bf16), hidden
    give_part(product(hidden, down_w[...]), outs[4:])


def feed_back_kernel(count, held, *refs):
    block_refs, (in_w, down_w) = refs[:count], refs[count : count + 2]
    gate_in, up_in = refs[count + 2 : count + 4]
    rows_out, grads_out = refs[count + 4 + held : count + 6 + held]
    units = down_w.shape[0]
    hidden_grad = product_right(take_rows(block_refs, rows_out), down_w[...])
    gate, up = gate_in[...].astype(f32), up_in[...].astype(f32)
    sigmoid_gate = jax.nn.sigmoid(gate)
    gate_grad = hidden_grad * up * sigmoid_gate * (1.0 + gate * (1.0 - sigmoid_gate))
    grads_out[:, :units] = gate_grad.astype(bf16)
    grads_out[:, units:] = (hidden_grad * gate * sigmoid_gate).astype(bf16)
    give_part(product_right(grads_out[...], in_w[...]), refs[count + 6 + held :])


def feed_call(kernel, name, blocks, first, length, weights, saved, widths, held):
    count, piece = len(blocks), blocks[0].shape[0]
    held = list(held or ())
    whole = pl.BlockSpec((piece, D), lambda i: (0, 0))

    def rows(columns):
        return pl.BlockSpec((piece, columns), lambda i: (first + i, 0))

    in_specs = [whole] * count + [pl.BlockSpec(memory_space=pltpu.VMEM)] * 2
    in_specs += [rows(array.shape[1]) for array in saved]
    results = pl.pallas_call(
        functools.partial(kernel, count, len(held)),
        grid=(count,),
        in_specs=in_specs + [pl.BlockSpec(memory_space=pltpu.HBM)] * len(held),
        out_specs=[rows(w) for w in widths] + [whole] * count,
        out_shape=[pltpu.HBM((length, w), bf16) for w in widths]
        + [jax.ShapeDtypeStruct((piece, D), bf16)] * count,
        input_output_aliases={len(in_specs) + i: i for i in range(len(held))},
        cost_estimate=cost(1),
        compiler_params=pltpu.CompilerParams(vmem_limit_bytes=24 << 20),
        name=name,
    )(*blocks, *weights, *saved, *held)
    return list(results[: len(widths)]), tuple(results[len(widths) :])


def norm_forward(values, gain_row):
    factor = lax.rsqrt(jnp.mean(values * values, axis=-1, keepdims=True) + norm_epsilon)
    return (values * factor * gain_row, factor)


def norm_backward(values, factor, gain_row, incoming):
    weighted = incoming * gain_row
    mixing = jnp.mean(weighted * values, axis=-1, keepdims=True)
    return (
        factor * (weighted - values * factor * factor * mixing),
        jnp.sum(incoming * values * factor, axis=0),
    )


def arrange(lengths, positions):
    finish = jnp.cumsum(lengths)
    has_ended = finish[None, :] <= positions[:, None]
    return jnp.sum(jnp.where(has_ended, lengths[None, :], 0), axis=1).astype(jnp.int32)


def scatter_over(value, axes):
    return lax.psum_scatter(value.astype(bf16), axes, scatter_dimension=0, tiled=True)


def on_device(
    hidden_in, seq_lengths, qkv_weight, out_weight, in_weight, down_weight, norm_gains, upstream
):
    piece_len, model_width = hidden_in.shape[1:]
    line_sizes = sizes_of(LINE)
    line = line_sizes[0] * line_sizes[1]
    length = piece_len * line * 2
    width = D // (line * 2)
    core = lax.axis_index("c")
    ctx_place = linear([lax.axis_index(a) for a in CTX], sizes_of(CTX))
    data_place = linear([lax.axis_index(a) for a in DATA], sizes_of(DATA))
    line_place = linear([lax.axis_index(a) for a in LINE], line_sizes)
    lengths = lax.dynamic_index_in_dim(seq_lengths, data_place, 0, keepdims=False)
    places = jnp.arange(length, dtype=jnp.int32)
    starts = arrange(lengths, places)
    offset = (places - starts).astype(f32)
    lows = starts[::BLOCK_Q] // BLOCK_K
    starts_row = starts.reshape(1, length)
    inverse = rope_base ** (-2.0 * jnp.arange(HEAD_DIM // 2, dtype=f32) / HEAD_DIM)

    def tables(offset):
        angles = offset[:, None] * inverse[None, :]
        cosine, sine_part = jnp.cos(angles), jnp.sin(angles)
        cosine = jnp.concatenate([cosine, cosine], axis=1)
        return cosine, jnp.concatenate([-sine_part, sine_part], axis=1)

    own_input = hidden_in.reshape(piece_len, model_width)

    row = Line(LINE)

    row_count = qkv_weight.shape[0]
    owners = line * 2
    data_count = sizes_of(DATA)[0] * sizes_of(DATA)[1]
    buffer = [jnp.zeros((line, 2, piece_len, model_width), bf16)]

    def keep_input(k, same, other):
        of_other = k if k == line - 1 else k - 1 if k < line else line - 2
        for at_core, block, at in ((core, same, k), (1 - core, other, of_other)):
            if block is not None:
                buffer[0] = lax.dynamic_update_slice(
                    buffer[0], block[None, None], (row.served(at), at_core, 0, 0)
                )
        return ()

    def weights_step(slot, tied):
        if slot == 0:
            blocks = spread(qkv_weight, 3, owners)
            blocks = exchange_cores(blocks.reshape(line, 2, row_count, 3 * width))
            return (blocks, in_weight, offset)
        if slot == 1:
            down = lax.all_gather(down_weight, DATA, axis=0, tiled=True)
            blocks = spread(tied[0][1], 2 * data_count, owners)
            return (chips_start(tied[0][0], LINE), down, blocks, tables(tied[0][2]))
        if slot == 2:
            return cores_start(tied[1][2].reshape((line, 2) + tied[1][2].shape[1:]))
        if slot == line - 1:
            return (out_weight, tied[2])
        return ()

    plan = [[0], [1], []] + [[slot - 1] for slot in range(3, line)]
    swaps = [[0], [], [1, 2]] + [[k] for k in range(3, line)]
    _, tied = row.gather(own_input, keep_input, weights_step, plan, swaps)
    full_input = buffer[0].reshape(length, model_width)
    qkv_rows = by_source(tied[1][0], LINE).reshape(-1, 3 * width)
    qkv_here = lax.all_gather(qkv_rows, DATA, axis=0, tiled=True)
    down_here, (cosine, sine_part) = tied[1][1], tied[1][3]
    units = down_here.shape[0]
    out_shuffled, (in_keep, in_got) = tied[line - 1]
    out_pieces = shifts(lambda steps: out_shuffled, LINE)

    projected, squares = project(full_input, qkv_here)
    squares, out_pieces, in_got = together(squares, out_pieces, in_got)
    out_line = by_source(out_pieces, LINE)
    out_half = lax.all_gather(out_line.reshape(-1, D), DATA, axis=0, tiled=True)
    in_pieces = chips_start(by_core(in_keep, in_got), LINE)
    factors = lax.rsqrt(small_sum(squares, CTX) / D + norm_epsilon)
    gains_here = lax.dynamic_slice(norm_gains, (0, ctx_place * width), (2, width))
    query_low, key_low, value_low = turn(projected, factors, gains_here, cosine, sine_part)
    head_out, log_total = attend(lows, starts_row, query_low, key_low, value_low)

    blocks = head_out.astype(bf16).reshape(line, 2, piece_len, width)
    keep, got = cores_start(blocks)
    got, in_pieces, out_half = together(got, in_pieces, out_half)
    out_half = out_half.reshape(-1, out_weight.shape[0], D)
    out_other = swap(out_half)
    in_rows = by_source(in_pieces, LINE)
    in_here = lax.all_gather(in_rows.reshape(-1, in_rows.shape[-1]), DATA, axis=0, tiled=True)
    out_full = by_core(out_half, out_other).reshape(D, D)
    pieces, out_full = together(chips_start(by_core(keep, got), LINE), out_full)
    attended = by_source(pieces, LINE)
    attended_low = attended.reshape(line * 2, piece_len, width).transpose(1, 0, 2)
    attended_low = attended_low.reshape(piece_len, D)
    branch = product(attended_low, out_full)
    branch_normed, branch_factor = norm_forward(branch, norm_gains[2])
    residual = own_input.astype(f32) + branch_normed
    residual_low = residual.astype(bf16)

    def chip_sums(results):
        def parts(k):
            if k == line - 1:
                other = results[k][1]
            else:
                other = results[line][0] if k == line - 2 else results[k + 1][1]
            return scatter_sum(results[k][0], other)

        return parts

    def window_of(k):
        return 2 * line - 2 if k == 0 else 2 * line - 1 if k == line else 2 * (k - 1)

    held = {}
    weights_here = tuple(
        pltpu.with_memory_space_constraint(w, pltpu.VMEM) for w in (in_here, down_here)
    )

    def forward_chip(k, same, other):
        blocks = [b for b in (same, other) if b is not None]
        held["forward"], parts = feed_call(
            feed_kernel, "feed", blocks, window_of(k), length, weights_here, (),
            (D, units, units, units), held.get("forward"),
        )
        return parts

    plan = [[], [0], [1, 2]] + [[k] for k in range(3, line - 1)] + [[]]
    forward, _ = row.gather(residual_low, forward_chip, plan=plan)
    residual_all, gate_all, up_all, hidden_all = held["forward"]
    second, _ = row.scatter(chip_sums(forward))
    second_normed, second_factor = norm_forward(second, norm_gains[3])
    result = residual + second_normed
    live_places = ctx_place * piece_len + jnp.arange(piece_len, dtype=jnp.int32)
    live_rows = (live_places < jnp.sum(lengths)).astype(f32)[:, None]
    sums = jnp.stack(
        [
            jnp.sum(result * result * live_rows),
            jnp.sum(branch * branch * live_rows),
            jnp.sum(second * second * live_rows),
        ]
    )

    incoming = upstream.reshape(piece_len, model_width).astype(f32)
    second_grad, second_gain_grad = norm_backward(second, second_factor, norm_gains[3], incoming)

    def backward_chip(k, same, other):
        blocks = [b for b in (same, other) if b is not None]
        held["backward"], parts = feed_call(
            feed_back_kernel, "feed_back", blocks, window_of(k), length, weights_here,
            (gate_all, up_all), (D, 2 * units), held.get("backward"),
        )
        return parts

    backward, _ = row.gather(second_grad.astype(bf16), backward_chip)
    second_grad_all, gate_up_grads = held["backward"]

    def weight_grads(slot, tied):
        if slot == 1:
            return (product_left(residual_all, gate_up_grads).astype(bf16),)
        if slot == 2:
            return (product_left(hidden_all, second_grad_all).astype(bf16),)
        return ()

    residual_part, tied = row.scatter(chip_sums(backward), weight_grads)
    grad_in, grad_down = tied[0][0], tied[1][0]
    residual_grad = incoming + residual_part
    grad_in = scatter_over(grad_in, DATA).reshape(in_rows.shape)

    branch_grad, branch_gain_grad = norm_backward(
        branch, branch_factor, norm_gains[2], residual_grad
    )
    branch_grad_low = branch_grad.astype(bf16)
    attended_grad = product_right(branch_grad_low, out_full).astype(bf16)
    attended_grad = attended_grad.reshape(piece_len, line, 2, width).transpose(1, 2, 0, 3)
    keep, give = pick(attended_grad, core, 1), pick(attended_grad, 1 - core, 1)
    give, branch_grad_low = together(give, branch_grad_low)
    out_grad = product_left(attended_low, branch_grad_low).astype(bf16)
    out_grad = out_grad.reshape(-1, 2, out_weight.shape[0], D)
    got, out_grad, grad_in = together(swap(give), out_grad, grad_in)
    pieces = chips_start(by_core(keep, got), LINE)
    in_keep, in_got = cores_start(grad_in.reshape((line, 2) + in_rows.shape[2:]))
    out_got = swap(pick(out_grad, 1 - core, 1))
    pieces, in_got, out_got = together(pieces, in_got, out_got)
    head_grad = by_source(pieces, LINE).reshape(length, width)
    in_pieces = chips_start(by_core(in_keep, in_got), LINE)
    out_grad = join(out_grad, out_got)
    head_grad, out_grad = together(head_grad, out_grad)
    out_grad = scatter_over(out_grad.reshape(D // 2, D), DATA)
    out_grad = out_grad.reshape((line,) + out_weight.shape)

    query_grad, key_grad, value_grad = attend_back(
        lows, starts_row, query_low, key_low, value_low, head_out, log_total, head_grad
    )
    weighted, mixing, gain_grads = unturn(
        query_grad, key_grad, projected, factors, gains_here, cosine, sine_part
    )
    mixing, in_pieces, grad_down = together(mixing, in_pieces, grad_down)
    grad_down = scatter_over(grad_down, DATA)
    mixing = small_sum(mixing, CTX) / D
    projected_grad = finish(weighted, projected, factors, mixing, value_grad)
    out_steps = offsets(LINE)

    def out_pieces(turn):
        return [shift(pick(out_grad, place(LINE, steps)), LINE, steps) for steps in turn]

    projected_grad, near = together(projected_grad, out_pieces(out_steps[:-1]))
    grad_blocks = projected_grad.reshape(line, 2, piece_len, 3 * width)

    later = []

    def input_product(k):
        rows = pick(grad_blocks, row.served(k))
        rows = jnp.concatenate([pick(rows, core), pick(rows, 1 - core)], axis=0)
        return product_right(rows, qkv_here).astype(bf16)

    def input_chip(k):
        part = row.tied[0][2] if k == line - 4 else input_product(k)
        part = scatter_sum(part[:piece_len], part[piece_len:])
        if not later:
            later.extend(together(part, projected_grad))
            part = later[0]
        return part

    def step(rows, axis):
        if lax.axis_size(axis) == 2:
            return (rows, lax.ppermute(rows, axis, [(0, 1), (1, 0)]))
        return (lax.psum(rows, axis),)

    def last_grads(slot, tied):
        if slot == 1:
            grads = product_left(full_input, later[1]).astype(bf16)
            return (grads, gain_grads, input_product(line - 4), out_pieces(out_steps[-1:]))
        if slot == 2:
            rows = jnp.zeros((5, D), f32)
            rows = lax.dynamic_update_slice(rows, tied[0][1], (0, ctx_place * width))
            rows = rows.at[2].set(branch_gain_grad).at[3].set(second_gain_grad)
            rows = rows.at[4, :3].set(sums)
            return (scatter_over(tied[0][0], DATA), step(rows, "c"), grad_down)
        if slot == line - 1:
            blocks = tied[1][0].reshape(line, 2, row_count, 3 * width)
            return (cores_start(blocks), step(sum(tied[1][1]), "zl"), in_pieces, tied[1][2])
        return ()

    plan = [[line - 2, line - 3]] + [[k] for k in range(line - 4, -1, -1)] + [[]]
    input_part, tied = row.scatter(input_chip, last_grads, plan)
    qkv_cores, gain_rows, in_pieces, grad_down = tied[line - 2]
    qkv_pieces = chips_start(by_core(*qkv_cores), LINE)
    gain_rows, qkv_pieces = together(step(sum(gain_rows), "zh"), qkv_pieces)
    gain_rows = sum(gain_rows)
    if sizes_of(DATA) == (2, 2):
        sides = [shift(gain_rows, DATA, steps) for steps in offsets(DATA)]
        gain_rows = (sides[0] + sides[1]) + (sides[2] + sides[3])
    else:
        gain_rows = small_sum(gain_rows, ("dl", "dh"))
    input_grad = residual_grad + input_part
    grad_in = by_source(in_pieces, LINE)
    grad_in = collect(grad_in.reshape((owners,) + grad_in.shape[2:]), 2 * data_count)
    grad_down = grad_down.astype(f32)
    grad_out = sum(piece.astype(f32) for piece in near + tied[0][3])
    grad_qkv = by_source(qkv_pieces, LINE)
    grad_qkv = collect(grad_qkv.reshape(owners, row_count, 3 * width), 3)
    live_count = jnp.sum(seq_lengths).astype(f32)
    rms_values = jnp.sqrt(gain_rows[4, :3] / (live_count * model_width))
    return (
        result.astype(bf16)[None],
        input_grad[None],
        grad_qkv,
        grad_out,
        grad_in,
        grad_down,
        gain_rows[:4],
        rms_values,
    )


def solution(mesh):
    dp, ctx = mesh.shape["dp"], mesh.shape["ctx"]
    fine = Mesh(mesh.devices.reshape(2, dp // 2, 2, ctx // 4, 2), AXES)
    return jax.shard_map(
        on_device,
        mesh=fine,
        in_specs=(
            P(DATA, CTX, None),
            P(),
            P(AXES, None),
            P(AXES, None),
            P(AXES, None),
            P(AXES, None),
            P(),
            P(DATA, CTX, None),
        ),
        out_specs=(
            P(DATA, CTX, None),
            P(DATA, CTX, None),
            P(AXES, None),
            P(AXES, None),
            P(AXES, None),
            P(AXES, None),
            P(),
            P(),
        ),
        check_vma=False,
    )
```

```python
import functools
import itertools

import jax
import jax.numpy as jnp
import numpy as np
from jax import lax
from jax.experimental import pallas as pl
from jax.experimental.pallas import tpu as pltpu
from jax.sharding import Mesh
from jax.sharding import PartitionSpec as P

D = 2048
HEADS = 16
HEAD_DIM = 128
FF = 8192

norm_epsilon = 1e-06
rope_base = 500000.0
masked_score = -1e30
scale_factor = HEAD_DIM ** (-0.5)

AXES = ("dh", "dl", "zh", "zl", "c")
DATA = ("dh", "dl")
LINE = ("zh", "zl")
CTX = ("zh", "zl", "c")

BLOCK_Q = 512
BLOCK_K = 512

bf16 = jnp.bfloat16
f32 = jnp.float32


def sizes_of(axes):
    return tuple(lax.axis_size(a) for a in axes)


def offsets(axes):
    return list(itertools.product(*[range(n) for n in sizes_of(axes)]))


def linear(index, sizes):
    total = 0
    for i, n in zip(index, sizes):
        total = total * n + i
    return total


def shift(value, axes, steps):
    if not any(steps):
        return value
    sizes = sizes_of(axes)
    pairs = []
    for index in itertools.product(*[range(n) for n in sizes]):
        target = tuple((i + s) % n for i, s, n in zip(index, steps, sizes))
        pairs.append((linear(index, sizes), linear(target, sizes)))
    return lax.ppermute(value, axes, pairs)


def swap(value):
    return lax.ppermute(value, "c", [(0, 1), (1, 0)])


def place(axes, steps, sign=1):
    sizes = sizes_of(axes)
    here = [(lax.axis_index(a) + sign * s) % n for a, s, n in zip(axes, steps, sizes)]
    return linear(here, sizes)


def pick(value, index, axis=0):
    return lax.dynamic_index_in_dim(value, index, axis, keepdims=False)


def put(buffer, value, index):
    return lax.dynamic_update_slice_in_dim(buffer, value[None], index, 0)


def together(*values):
    return lax.optimization_barrier(values)


def line_order(count):
    return np.array(
        [sorted(range(count), key=lambda j: (abs(i - j), j != i ^ 1)) for i in range(count)],
        dtype=np.int32,
    )


class Line:
    def __init__(self, axes):
        self.axes = axes
        sizes = sizes_of(axes)
        self.count = sizes[0] * sizes[1]
        self.place = linear([lax.axis_index(a) for a in axes], sizes)
        self.order = line_order(self.count)

    def served(self, k):
        return jnp.asarray(self.order[:, k])[self.place]

    def hop(self, value, step, keep=lambda i: True):
        pairs = [
            (i, i + step) for i in range(self.count) if 0 <= i + step < self.count and keep(i)
        ]
        return lax.ppermute(value, self.axes, pairs)

    def choose(self, options, wanted):
        used = sorted({w for w in wanted if w is not None})
        value = options[used[0]]
        for w in used[1:]:
            mask = np.array([v == w for v in wanted])
            value = jnp.where(jnp.asarray(mask)[self.place], options[w], value)
        return value

    def gather(self, block, work, extra=None, plan=None, swaps=None):
        last = self.count - 1
        plan = plan or [[k] for k in range(last)] + [[]]
        swaps = swaps or [[k] for k in range(last + 1)]
        options, results, tied, arrived, other = {}, [], [], [], {-1: None}
        for slot in range(self.count):
            if slot:
                wanted = []
                for i in range(self.count):
                    j = self.order[i, slot]
                    wanted.append((1, i - j) if j < i else (-1, j - i))
                arrived.append(self.choose(options, wanted))
            else:
                arrived.append(block)
            moved = ()
            if slot < last:
                moved = tuple(
                    self.hop(options[(step, slot)] if slot else block, step) for step in (1, -1)
                )
            swapped = [swap(arrived[k]) for k in swaps[slot]]
            done = [work(k, arrived[k], other[k - 1]) for k in plan[slot]]
            more = extra(slot, tied) if extra else ()
            moved, swapped, done, more = together(moved, swapped, done, more)
            if moved:
                options[(1, slot + 1)], options[(-1, slot + 1)] = moved
            other.update(zip(swaps[slot], swapped))
            tied.append(more)
            results += done
        results.append(work(last, arrived[last], other[last]))
        results.append(work(self.count, None, other[last - 1]))
        return results, tied

    def hop_values(self, made, far, last):
        wanted = {}
        for step in (1, -1):
            wanted[step] = []
            for i in range(self.count):
                j = i + step * far
                known = 0 <= j < self.count
                wanted[step].append(int(np.argmax(self.order[i] == j)) if known else None)
        used = sorted({w for side in wanted.values() for w in side if w is not None})
        if last[1] is not None and len(used) == 2:
            flags = [[int(w == used[1]) for w in wanted[step]] for step in (1, -1)]
            flags = jnp.asarray(np.array(flags, dtype=np.int32))[:, self.place]
            return combine(flags, made[used[0]], made[used[1]], last[1], last[-1])
        values = []
        for step in (1, -1):
            value = self.choose(made, wanted[step])
            if last[step] is not None:
                value = value.astype(f32) + last[step].astype(f32)
            values.append(value.astype(bf16))
        return values

    def scatter(self, parts, fill=None, plan=None):
        count = self.count
        plan = plan or [[k] for k in range(count - 2, -1, -1)]
        made = {count - 1: parts(count - 1)}
        last = {1: None, -1: None}
        tied = self.tied = []
        for slot in range(1, count):
            far = count - slot
            values = self.hop_values(made, far, last)
            moved = []
            for step, value in zip((1, -1), values):
                keep = lambda i: 0 <= i + step * far < count
                moved.append(self.hop(value, step, keep))
            done = [parts(k) for k in plan[slot - 1]]
            more = fill(slot, tied) if fill else ()
            moved, done, more = together(moved, done, more)
            tied.append(more)
            made.update(zip(plan[slot - 1], done))
            last[1], last[-1] = moved
        total = made[0].astype(f32) + last[1].astype(f32) + last[-1].astype(f32)
        return total, tied


def combine_kernel(flag_ref, one_ref, two_ref, right_ref, left_ref, right_out, left_out):
    for i, (last, out) in enumerate(((right_ref, right_out), (left_ref, left_out))):
        chosen = jnp.where(flag_ref[i] == 0, one_ref[...], two_ref[...])
        out[...] = (chosen.astype(f32) + last[...].astype(f32)).astype(bf16)


def combine(flags, one, two, right, left):
    rows, columns = one.shape
    block = pl.BlockSpec((rows, columns), lambda i, flags: (0, 0))
    return pl.pallas_call(
        combine_kernel,
        grid_spec=pltpu.PrefetchScalarGridSpec(
            num_scalar_prefetch=1, grid=(1,), in_specs=[block] * 4, out_specs=[block] * 2
        ),
        out_shape=[jax.ShapeDtypeStruct((rows, columns), bf16)] * 2,
        cost_estimate=cost(1),
        compiler_params=pltpu.CompilerParams(vmem_limit_bytes=16 << 20),
        name="combine",
    )(flags, one, two, right, left)


def scatter_sum(for_same, for_other):
    return (for_same.astype(f32) + swap(for_other.astype(bf16)).astype(f32)).astype(bf16)


def cores_start(blocks):
    core = lax.axis_index("c")
    return pick(blocks, core, 1), swap(pick(blocks, 1 - core, 1))


def exchange_cores(blocks):
    return by_core(*cores_start(blocks))


def by_core(mine, other):
    shape = (mine.shape[0], 2) + mine.shape[1:]
    here = lax.broadcasted_iota(jnp.int32, shape, 1) == lax.axis_index("c")
    return jnp.where(here, mine[:, None], other[:, None])


def assemble_kernel(*refs):
    out_ref = refs[-1]
    for i, piece in enumerate(refs[1:-1]):

        @pl.when(pl.program_id(0) == i)
        def _(piece=piece):
            out_ref[0] = piece[...]


def assemble(pieces, places):
    shape = pieces[0].shape
    block = pl.BlockSpec(shape, lambda i, places: (0,) * len(shape))
    return pl.pallas_call(
        assemble_kernel,
        grid_spec=pltpu.PrefetchScalarGridSpec(
            num_scalar_prefetch=1,
            grid=(len(pieces),),
            in_specs=[block] * len(pieces),
            out_specs=pl.BlockSpec((1,) + shape, lambda i, places: (places[i],) + (0,) * len(shape)),
        ),
        out_shape=jax.ShapeDtypeStruct((len(pieces),) + shape, pieces[0].dtype),
        compiler_params=pltpu.CompilerParams(vmem_limit_bytes=18 << 20),
        cost_estimate=cost(2),
        name="assemble",
    )(jnp.stack(places).astype(jnp.int32), *pieces)


def shifts(value_for, chips):
    return tuple(shift(value_for(steps), chips, steps) for steps in offsets(chips))


def by_source(pieces, chips):
    return assemble(pieces, [place(chips, steps, -1) for steps in offsets(chips)])


def chips_start(pairs, chips):
    return shifts(lambda steps: pick(pairs, place(chips, steps)), chips)


def exchange_chips(pairs, chips):
    return by_source(chips_start(pairs, chips), chips)


def exchange(blocks, chips):
    return exchange_chips(exchange_cores(blocks), chips)


def small_sum(value, axes):
    for axis in axes:
        if lax.axis_size(axis) == 2:
            value = value + lax.ppermute(value, axis, [(0, 1), (1, 0)])
        else:
            value = lax.psum(value, axis)
    return value


def product(left_side, right_side):
    return jnp.dot(left_side, right_side, preferred_element_type=f32)


def product_left(left_side, right_side):
    return lax.dot_general(
        left_side, right_side, (((0,), (0,)), ((), ())), preferred_element_type=f32
    )


def product_right(left_side, right_side):
    return lax.dot_general(
        left_side, right_side, (((1,), (1,)), ((), ())), preferred_element_type=f32
    )


def cost(microseconds):
    return pl.CostEstimate(
        flops=int(microseconds * 1.0e9),
        transcendentals=0,
        bytes_accessed=int(microseconds * 3.0e6),
    )


def allowed_keys(shape, key_start, query_start, starts):
    key_place = key_start + lax.broadcasted_iota(jnp.int32, shape, 0)
    query_place = query_start + lax.broadcasted_iota(jnp.int32, shape, 1)
    return (key_place >= starts) & (key_place <= query_place)


def heads_of(width):
    return [slice(h, h + HEAD_DIM) for h in range(0, width, HEAD_DIM)]


def attend_kernel(low_ref, starts_ref, q_ref, k_ref, v_ref, out_ref, log_ref):
    block = pl.program_id(0)
    bq, bk = q_ref.shape[0], BLOCK_K
    starts, heads = starts_ref[...], heads_of(q_ref.shape[1])

    def step(j, carry):
        rows = pl.ds(pl.multiple_of(j * bk, bk), bk)
        ok = allowed_keys((bk, bq), j * bk, block * bq, starts)
        results = []
        for head, (top, total, acc) in zip(heads, carry):
            scores = product_right(k_ref[rows, head], q_ref[:, head]) * scale_factor
            scores = jnp.where(ok, scores, masked_score)
            new_top = jnp.maximum(top, jnp.max(scores, axis=0, keepdims=True))
            ratio = jnp.exp(top - new_top)
            expanded = jnp.exp(scores - new_top)
            total = total * ratio + jnp.sum(expanded, axis=0, keepdims=True)
            acc = acc * ratio + product_left(v_ref[rows, head], expanded.astype(bf16))
            results.append((new_top, total, acc))
        return tuple(results)

    init = (
        jnp.full((1, bq), masked_score, f32),
        jnp.zeros((1, bq), f32),
        jnp.zeros((HEAD_DIM, bq), f32),
    )
    final = lax.fori_loop(
        low_ref[block], (block * bq + bq) // bk, step, tuple(init for _ in heads)
    )
    for h, (head, (top, total, acc)) in enumerate(zip(heads, final)):
        out_ref[:, head] = (acc / total).T
        log_ref[h] = top + jnp.log(total)


def in_hbm(*arrays):
    return tuple(pltpu.with_memory_space_constraint(a, pltpu.HBM) for a in arrays)


def attend(lows, starts, queries, keys, values):
    length, width = queries.shape
    queries, keys, values = in_hbm(queries, keys, values)
    heads, bq = width // HEAD_DIM, BLOCK_Q
    whole = pl.BlockSpec((length, width), lambda i, low: (0, 0))
    part = pl.BlockSpec((bq, width), lambda i, low: (i, 0))
    return pl.pallas_call(
        attend_kernel,
        grid_spec=pltpu.PrefetchScalarGridSpec(
            num_scalar_prefetch=1,
            grid=(length // bq,),
            in_specs=[pl.BlockSpec((1, bq), lambda i, low: (0, i)), part, whole, whole],
            out_specs=[part, pl.BlockSpec((heads, 1, bq), lambda i, low: (0, 0, i))],
        ),
        out_shape=[
            pltpu.HBM((length, width), f32),
            jax.ShapeDtypeStruct((heads, 1, length), f32),
        ],
        compiler_params=pltpu.CompilerParams(vmem_limit_bytes=24 << 20),
        cost_estimate=cost(16),
        name="attend",
    )(lows, starts, queries, keys, values)


def attend_back_kernel(
    low_ref, starts_ref, q_ref, k_ref, v_ref, out_ref, log_ref, grad_ref, dq_ref, dk_ref, dv_ref
):
    block = pl.program_id(0)
    bq, bk = q_ref.shape[0], BLOCK_K
    starts, heads = starts_ref[...], heads_of(q_ref.shape[1])

    @pl.when(block == 0)
    def _():
        dk_ref[...] = jnp.zeros_like(dk_ref)
        dv_ref[...] = jnp.zeros_like(dv_ref)

    inner = [
        jnp.sum((grad_ref[:, head].astype(f32) * out_ref[:, head]).T, axis=0, keepdims=True)
        for head in heads
    ]

    def step(j, carry):
        rows = pl.ds(pl.multiple_of(j * bk, bk), bk)
        ok = allowed_keys((bk, bq), j * bk, block * bq, starts)
        results = []
        for h, (head, acc) in enumerate(zip(heads, carry)):
            keys, queries, grads = k_ref[rows, head], q_ref[:, head], grad_ref[:, head]
            scores = product_right(keys, queries) * scale_factor
            probs = jnp.where(ok, jnp.exp(scores - log_ref[h]), 0.0)
            dv_ref[rows, head] += product(probs.astype(bf16), grads)
            prob_grad = product_right(v_ref[rows, head], grads)
            score_grad = (probs * (prob_grad - inner[h])).astype(bf16)
            dk_ref[rows, head] += product(score_grad, queries) * scale_factor
            results.append(acc + product_left(keys, score_grad))
        return tuple(results)

    final = lax.fori_loop(
        low_ref[block],
        (block * bq + bq) // bk,
        step,
        tuple(jnp.zeros((HEAD_DIM, bq), f32) for _ in heads),
    )
    for head, acc in zip(heads, final):
        dq_ref[:, head] = (acc * scale_factor).T


def attend_back(lows, starts, queries, keys, values, out, log_total, grads):
    length, width = queries.shape
    heads, bq = width // HEAD_DIM, BLOCK_Q
    whole = pl.BlockSpec((length, width), lambda i, low: (0, 0))
    part = pl.BlockSpec((bq, width), lambda i, low: (i, 0))
    return pl.pallas_call(
        attend_back_kernel,
        grid_spec=pltpu.PrefetchScalarGridSpec(
            num_scalar_prefetch=1,
            grid=(length // bq,),
            in_specs=[
                pl.BlockSpec((1, bq), lambda i, low: (0, i)),
                part,
                whole,
                whole,
                part,
                pl.BlockSpec((heads, 1, bq), lambda i, low: (0, 0, i)),
                part,
            ],
            out_specs=[part, whole, whole],
        ),
        out_shape=[pltpu.HBM((length, width), f32)] * 3,
        compiler_params=pltpu.CompilerParams(vmem_limit_bytes=32 << 20),
        cost_estimate=cost(26),
        name="attend_back",
    )(lows, starts, queries, keys, values, out, log_total, grads)


def spread_kernel(in_ref, out_ref):
    unit = out_ref.shape[2]
    for k in range(out_ref.shape[0]):
        out_ref[k] = in_ref[:, k * unit : (k + 1) * unit]


def spread(weight, groups, owners):
    rows, columns = weight.shape
    unit = columns // (groups * owners)
    if unit % 128:
        shaped = weight.reshape(rows, groups, owners, unit).transpose(2, 0, 1, 3)
        return shaped.reshape(owners, rows, groups * unit)
    return pl.pallas_call(
        spread_kernel,
        grid=(groups,),
        in_specs=[pl.BlockSpec((rows, owners * unit), lambda g: (0, g))],
        out_specs=pl.BlockSpec((owners, rows, unit), lambda g: (0, 0, g)),
        out_shape=jax.ShapeDtypeStruct((owners, rows, groups * unit), weight.dtype),
        cost_estimate=cost(4),
        name="spread",
    )(weight)


def collect_kernel(in_ref, out_ref):
    unit = in_ref.shape[2]
    for k in range(in_ref.shape[0]):
        out_ref[:, k * unit : (k + 1) * unit] = in_ref[k].astype(f32)


def collect(blocks, groups):
    owners, rows, columns = blocks.shape
    unit = columns // groups
    if unit % 128:
        shaped = blocks.reshape(owners, rows, groups, unit).transpose(1, 2, 0, 3)
        return shaped.reshape(rows, groups * owners * unit).astype(f32)
    return pl.pallas_call(
        collect_kernel,
        grid=(groups,),
        in_specs=[pl.BlockSpec((owners, rows, unit), lambda g: (0, 0, g))],
        out_specs=pl.BlockSpec((rows, owners * unit), lambda g: (0, g)),
        out_shape=jax.ShapeDtypeStruct((rows, groups * owners * unit), f32),
        cost_estimate=cost(5),
        name="collect",
    )(blocks)


def columns_of(row):
    return jnp.broadcast_to(row, (HEAD_DIM, row.shape[1])).T


def halves_swapped(values):
    return pltpu.roll(values, HEAD_DIM // 2, 1)


def project_kernel(in_ref, weight_ref, out_ref, square_ref):
    width = out_ref.shape[1] // 3
    out = product(in_ref[...], weight_ref[...])
    out_ref[...] = out
    for part in range(2):
        total = None
        for h in range(0, width, HEAD_DIM):
            raw = out[:, part * width + h : part * width + h + HEAD_DIM]
            total = raw * raw if total is None else total + raw * raw
        square_ref[part : part + 1, :] = jnp.sum(total.T, axis=0, keepdims=True)


def project(inputs, weight):
    length, depth = inputs.shape
    columns = weight.shape[1]
    return pl.pallas_call(
        project_kernel,
        grid=(length // 256,),
        in_specs=[row_block(depth, 256), whole_block(depth, columns)],
        out_specs=[row_block(columns, 256), lane_block(2, 256)],
        out_shape=[
            pltpu.HBM((length, columns), f32),
            jax.ShapeDtypeStruct((2, length), f32),
        ],
        compiler_params=pltpu.CompilerParams(vmem_limit_bytes=18 << 20),
        cost_estimate=cost(10),
        name="project",
    )(inputs, weight)


def join_kernel(core_ref, full_ref, got_ref, out_ref):
    out_ref[...] = (full_ref[:, 0].astype(f32) + got_ref[...].astype(f32)).astype(bf16)


def join(full, got):
    count, _, rows, columns = full.shape
    step = 4 if count % 4 == 0 else 1
    part = pl.BlockSpec((step, rows, columns), lambda i, core: (i, 0, 0))
    return pl.pallas_call(
        join_kernel,
        grid_spec=pltpu.PrefetchScalarGridSpec(
            num_scalar_prefetch=1,
            grid=(count // step,),
            in_specs=[
                pl.BlockSpec((step, 1, rows, columns), lambda i, core: (i, core[0], 0, 0)),
                part,
            ],
            out_specs=part,
        ),
        out_shape=jax.ShapeDtypeStruct((count, rows, columns), bf16),
        cost_estimate=cost(1),
        name="join",
    )(lax.axis_index("c").astype(jnp.int32).reshape(1), full, got)


def turn_kernel(proj_ref, factor_ref, gain_ref, cos_ref, sin_ref, q_ref, k_ref, v_ref):
    width = q_ref.shape[1]
    cosine, sine_part = cos_ref[...], sin_ref[...]
    for part, out in enumerate((q_ref, k_ref)):
        factor = columns_of(factor_ref[part : part + 1, :])
        for h in range(0, width, HEAD_DIM):
            raw = proj_ref[:, part * width + h : part * width + h + HEAD_DIM]
            normed = raw * factor * gain_ref[part : part + 1, h : h + HEAD_DIM]
            turned = normed * cosine + halves_swapped(normed) * sine_part
            out[:, h : h + HEAD_DIM] = turned.astype(bf16)
    v_ref[...] = proj_ref[:, 2 * width :].astype(bf16)


def row_block(columns, rows=512):
    return pl.BlockSpec((rows, columns), lambda i: (i, 0))


def lane_block(lines, rows=512):
    return pl.BlockSpec((lines, rows), lambda i: (0, i))


def whole_block(*shape):
    return pl.BlockSpec(shape, lambda i: (0,) * len(shape))


def turn(projected, factors, gains, cosine, sine_part):
    length, columns = projected.shape
    width = columns // 3
    return pl.pallas_call(
        turn_kernel,
        grid=(length // 512,),
        in_specs=[
            row_block(columns),
            lane_block(2),
            whole_block(2, width),
            row_block(HEAD_DIM),
            row_block(HEAD_DIM),
        ],
        out_specs=[row_block(width)] * 3,
        out_shape=[pltpu.HBM((length, width), bf16)] * 3,
        cost_estimate=cost(1),
        name="turn",
    )(projected, factors, gains, cosine, sine_part)


def unturn_kernel(
    dq_ref, dk_ref, proj_ref, factor_ref, gain_ref, cos_ref, sin_ref, out_ref, mix_ref, sum_ref
):
    width = dq_ref.shape[1]
    cosine, sine_part = cos_ref[...], sin_ref[...]

    @pl.when(pl.program_id(0) == 0)
    def _():
        sum_ref[...] = jnp.zeros_like(sum_ref)

    for part, grad_ref in enumerate((dq_ref, dk_ref)):
        factor = columns_of(factor_ref[part : part + 1, :])
        mixed = None
        for h in range(0, width, HEAD_DIM):
            at = part * width + h
            grad = grad_ref[:, h : h + HEAD_DIM]
            turned = grad * cosine - halves_swapped(grad) * sine_part
            raw = proj_ref[:, at : at + HEAD_DIM]
            sums = jnp.sum(turned * raw * factor, axis=0, keepdims=True)
            sum_ref[part : part + 1, h : h + HEAD_DIM] += sums
            weighted = turned * gain_ref[part : part + 1, h : h + HEAD_DIM]
            out_ref[:, at : at + HEAD_DIM] = weighted
            mixed = weighted * raw if mixed is None else mixed + weighted * raw
        mix_ref[part : part + 1, :] = jnp.sum(mixed.T, axis=0, keepdims=True)


def unturn(query_grad, key_grad, projected, factors, gains, cosine, sine_part):
    length, width = query_grad.shape
    query_grad, key_grad, projected = in_hbm(query_grad, key_grad, projected)
    return pl.pallas_call(
        unturn_kernel,
        grid=(length // 512,),
        in_specs=[
            row_block(width),
            row_block(width),
            row_block(2 * width),
            lane_block(2),
            whole_block(2, width),
            row_block(HEAD_DIM),
            row_block(HEAD_DIM),
        ],
        out_specs=[row_block(2 * width), lane_block(2), whole_block(2, width)],
        out_shape=[
            pltpu.HBM((length, 2 * width), f32),
            jax.ShapeDtypeStruct((2, length), f32),
            jax.ShapeDtypeStruct((2, width), f32),
        ],
        cost_estimate=cost(1),
        name="unturn",
    )(query_grad, key_grad, projected, factors, gains, cosine, sine_part)


def finish_kernel(weighted_ref, proj_ref, factor_ref, mix_ref, dv_ref, out_ref):
    width = dv_ref.shape[1]
    for part in range(2):
        factor = columns_of(factor_ref[part : part + 1, :])
        mixing = columns_of(mix_ref[part : part + 1, :])
        for h in range(0, width, HEAD_DIM):
            at = pl.ds(part * width + h, HEAD_DIM)
            grad = weighted_ref[:, at] - proj_ref[:, at] * factor * factor * mixing
            out_ref[:, at] = (factor * grad).astype(bf16)
    out_ref[:, 2 * width :] = dv_ref[...].astype(bf16)


def finish(weighted, projected, factors, mixing, value_grad):
    length, width = value_grad.shape
    return pl.pallas_call(
        finish_kernel,
        grid=(length // 512,),
        in_specs=[
            row_block(2 * width),
            row_block(2 * width),
            lane_block(2),
            lane_block(2),
            row_block(width),
        ],
        out_specs=row_block(3 * width),
        out_shape=jax.ShapeDtypeStruct((length, 3 * width), bf16),
        cost_estimate=cost(1),
        name="finish",
    )(weighted, projected, factors, mixing, value_grad)


def take_rows(block_refs, rows_out):
    for i, block in enumerate(block_refs):

        @pl.when(pl.program_id(0) == i)
        def _(block=block):
            rows_out[...] = block[...]

    return rows_out[...]


def give_part(part, part_refs):
    for i, out in enumerate(part_refs):

        @pl.when(pl.program_id(0) == i)
        def _(out=out):
            out[...] = part.astype(bf16)


def feed_kernel(count, held, *refs):
    block_refs, (in_w, down_w) = refs[:count], refs[count : count + 2]
    outs = refs[count + 2 + held :]
    rows_out, gate_out, up_out, hidden_out = outs[:4]
    units = down_w.shape[0]
    both = product(take_rows(block_refs, rows_out), in_w[...])
    gate, up = both[:, :units], both[:, units:]
    hidden = (gate * jax.nn.sigmoid(gate) * up).astype(bf16)
    gate_out[...], up_out[...], hidden_out[...] = gate.astype(bf16), up.astype(bf16), hidden
    give_part(product(hidden, down_w[...]), outs[4:])


def feed_back_kernel(count, held, *refs):
    block_refs, (in_w, down_w) = refs[:count], refs[count : count + 2]
    gate_in, up_in = refs[count + 2 : count + 4]
    rows_out, grads_out = refs[count + 4 + held : count + 6 + held]
    units = down_w.shape[0]
    hidden_grad = product_right(take_rows(block_refs, rows_out), down_w[...])
    gate, up = gate_in[...].astype(f32), up_in[...].astype(f32)
    sigmoid_gate = jax.nn.sigmoid(gate)
    gate_grad = hidden_grad * up * sigmoid_gate * (1.0 + gate * (1.0 - sigmoid_gate))
    grads_out[:, :units] = gate_grad.astype(bf16)
    grads_out[:, units:] = (hidden_grad * gate * sigmoid_gate).astype(bf16)
    give_part(product_right(grads_out[...], in_w[...]), refs[count + 6 + held :])


def feed_call(kernel, name, blocks, first, length, weights, saved, widths, held):
    count, piece = len(blocks), blocks[0].shape[0]
    held = list(held or ())
    whole = pl.BlockSpec((piece, D), lambda i: (0, 0))

    def rows(columns):
        return pl.BlockSpec((piece, columns), lambda i: (first + i, 0))

    in_specs = [whole] * count + [pl.BlockSpec(memory_space=pltpu.VMEM)] * 2
    in_specs += [rows(array.shape[1]) for array in saved]
    results = pl.pallas_call(
        functools.partial(kernel, count, len(held)),
        grid=(count,),
        in_specs=in_specs + [pl.BlockSpec(memory_space=pltpu.HBM)] * len(held),
        out_specs=[rows(w) for w in widths] + [whole] * count,
        out_shape=[pltpu.HBM((length, w), bf16) for w in widths]
        + [jax.ShapeDtypeStruct((piece, D), bf16)] * count,
        input_output_aliases={len(in_specs) + i: i for i in range(len(held))},
        cost_estimate=cost(1),
        compiler_params=pltpu.CompilerParams(vmem_limit_bytes=24 << 20),
        name=name,
    )(*blocks, *weights, *saved, *held)
    return list(results[: len(widths)]), tuple(results[len(widths) :])


def norm_forward(values, gain_row):
    factor = lax.rsqrt(jnp.mean(values * values, axis=-1, keepdims=True) + norm_epsilon)
    return (values * factor * gain_row, factor)


def norm_backward(values, factor, gain_row, incoming):
    weighted = incoming * gain_row
    mixing = jnp.mean(weighted * values, axis=-1, keepdims=True)
    return (
        factor * (weighted - values * factor * factor * mixing),
        jnp.sum(incoming * values * factor, axis=0),
    )


def arrange(lengths, positions):
    finish = jnp.cumsum(lengths)
    has_ended = finish[None, :] <= positions[:, None]
    return jnp.sum(jnp.where(has_ended, lengths[None, :], 0), axis=1).astype(jnp.int32)


def scatter_over(value, axes):
    return lax.psum_scatter(value.astype(bf16), axes, scatter_dimension=0, tiled=True)


def on_device(
    hidden_in, seq_lengths, qkv_weight, out_weight, in_weight, down_weight, norm_gains, upstream
):
    piece_len, model_width = hidden_in.shape[1:]
    line_sizes = sizes_of(LINE)
    line = line_sizes[0] * line_sizes[1]
    length = piece_len * line * 2
    width = D // (line * 2)
    core = lax.axis_index("c")
    ctx_place = linear([lax.axis_index(a) for a in CTX], sizes_of(CTX))
    data_place = linear([lax.axis_index(a) for a in DATA], sizes_of(DATA))
    line_place = linear([lax.axis_index(a) for a in LINE], line_sizes)
    lengths = lax.dynamic_index_in_dim(seq_lengths, data_place, 0, keepdims=False)
    places = jnp.arange(length, dtype=jnp.int32)
    starts = arrange(lengths, places)
    offset = (places - starts).astype(f32)
    lows = starts[::BLOCK_Q] // BLOCK_K
    starts_row = starts.reshape(1, length)
    inverse = rope_base ** (-2.0 * jnp.arange(HEAD_DIM // 2, dtype=f32) / HEAD_DIM)

    def tables(offset):
        angles = offset[:, None] * inverse[None, :]
        cosine, sine_part = jnp.cos(angles), jnp.sin(angles)
        cosine = jnp.concatenate([cosine, cosine], axis=1)
        return cosine, jnp.concatenate([-sine_part, sine_part], axis=1)

    own_input = hidden_in.reshape(piece_len, model_width)

    row = Line(LINE)

    row_count = qkv_weight.shape[0]
    owners = line * 2
    data_count = sizes_of(DATA)[0] * sizes_of(DATA)[1]
    buffer = [jnp.zeros((line, 2, piece_len, model_width), bf16)]

    def keep_input(k, same, other):
        of_other = k if k == line - 1 else k - 1 if k < line else line - 2
        for at_core, block, at in ((core, same, k), (1 - core, other, of_other)):
            if block is not None:
                buffer[0] = lax.dynamic_update_slice(
                    buffer[0], block[None, None], (row.served(at), at_core, 0, 0)
                )
        return ()

    def weights_step(slot, tied):
        if slot == 0:
            blocks = spread(qkv_weight, 3, owners)
            blocks = exchange_cores(blocks.reshape(line, 2, row_count, 3 * width))
            return (blocks, in_weight, offset)
        if slot == 1:
            down = lax.all_gather(down_weight, DATA, axis=0, tiled=True)
            blocks = spread(tied[0][1], 2 * data_count, owners)
            return (chips_start(tied[0][0], LINE), down, blocks, tables(tied[0][2]))
        if slot == 2:
            return cores_start(tied[1][2].reshape((line, 2) + tied[1][2].shape[1:]))
        if slot == line - 1:
            return (out_weight, tied[2])
        return ()

    plan = [[0], [1], []] + [[slot - 1] for slot in range(3, line)]
    swaps = [[0], [], [1, 2]] + [[k] for k in range(3, line)]
    _, tied = row.gather(own_input, keep_input, weights_step, plan, swaps)
    full_input = buffer[0].reshape(length, model_width)
    qkv_rows = by_source(tied[1][0], LINE).reshape(-1, 3 * width)
    qkv_here = lax.all_gather(qkv_rows, DATA, axis=0, tiled=True)
    down_here, (cosine, sine_part) = tied[1][1], tied[1][3]
    units = down_here.shape[0]
    out_shuffled, (in_keep, in_got) = tied[line - 1]
    out_pieces = shifts(lambda steps: out_shuffled, LINE)

    projected, squares = project(full_input, qkv_here)
    squares, out_pieces, in_got = together(squares, out_pieces, in_got)
    out_line = by_source(out_pieces, LINE)
    out_half = lax.all_gather(out_line.reshape(-1, D), DATA, axis=0, tiled=True)
    in_pieces = chips_start(by_core(in_keep, in_got), LINE)
    factors = lax.rsqrt(small_sum(squares, CTX) / D + norm_epsilon)
    gains_here = lax.dynamic_slice(norm_gains, (0, ctx_place * width), (2, width))
    query_low, key_low, value_low = turn(projected, factors, gains_here, cosine, sine_part)
    head_out, log_total = attend(lows, starts_row, query_low, key_low, value_low)

    blocks = head_out.astype(bf16).reshape(line, 2, piece_len, width)
    keep, got = cores_start(blocks)
    got, in_pieces, out_half = together(got, in_pieces, out_half)
    out_half = out_half.reshape(-1, out_weight.shape[0], D)
    out_other = swap(out_half)
    in_rows = by_source(in_pieces, LINE)
    in_here = lax.all_gather(in_rows.reshape(-1, in_rows.shape[-1]), DATA, axis=0, tiled=True)
    out_full = by_core(out_half, out_other).reshape(D, D)
    pieces, out_full = together(chips_start(by_core(keep, got), LINE), out_full)
    attended = by_source(pieces, LINE)
    attended_low = attended.reshape(line * 2, piece_len, width).transpose(1, 0, 2)
    attended_low = attended_low.reshape(piece_len, D)
    branch = product(attended_low, out_full)
    branch_normed, branch_factor = norm_forward(branch, norm_gains[2])
    residual = own_input.astype(f32) + branch_normed
    residual_low = residual.astype(bf16)

    def chip_sums(results):
        def parts(k):
            if k == line - 1:
                other = results[k][1]
            else:
                other = results[line][0] if k == line - 2 else results[k + 1][1]
            return scatter_sum(results[k][0], other)

        return parts

    def window_of(k):
        return 2 * line - 2 if k == 0 else 2 * line - 1 if k == line else 2 * (k - 1)

    held = {}
    weights_here = tuple(
        pltpu.with_memory_space_constraint(w, pltpu.VMEM) for w in (in_here, down_here)
    )

    def forward_chip(k, same, other):
        blocks = [b for b in (same, other) if b is not None]
        held["forward"], parts = feed_call(
            feed_kernel, "feed", blocks, window_of(k), length, weights_here, (),
            (D, units, units, units), held.get("forward"),
        )
        return parts

    plan = [[], [0], [1, 2]] + [[k] for k in range(3, line - 1)] + [[]]
    forward, _ = row.gather(residual_low, forward_chip, plan=plan)
    residual_all, gate_all, up_all, hidden_all = held["forward"]
    second, _ = row.scatter(chip_sums(forward))
    second_normed, second_factor = norm_forward(second, norm_gains[3])
    result = residual + second_normed
    live_places = ctx_place * piece_len + jnp.arange(piece_len, dtype=jnp.int32)
    live_rows = (live_places < jnp.sum(lengths)).astype(f32)[:, None]
    sums = jnp.stack(
        [
            jnp.sum(result * result * live_rows),
            jnp.sum(branch * branch * live_rows),
            jnp.sum(second * second * live_rows),
        ]
    )

    incoming = upstream.reshape(piece_len, model_width).astype(f32)
    second_grad, second_gain_grad = norm_backward(second, second_factor, norm_gains[3], incoming)

    def backward_chip(k, same, other):
        blocks = [b for b in (same, other) if b is not None]
        held["backward"], parts = feed_call(
            feed_back_kernel, "feed_back", blocks, window_of(k), length, weights_here,
            (gate_all, up_all), (D, 2 * units), held.get("backward"),
        )
        return parts

    backward, _ = row.gather(second_grad.astype(bf16), backward_chip)
    second_grad_all, gate_up_grads = held["backward"]

    def weight_grads(slot, tied):
        if slot == 1:
            return (product_left(residual_all, gate_up_grads).astype(bf16),)
        if slot == 2:
            return (product_left(hidden_all, second_grad_all).astype(bf16),)
        return ()

    residual_part, tied = row.scatter(chip_sums(backward), weight_grads)
    grad_in, grad_down = tied[0][0], tied[1][0]
    residual_grad = incoming + residual_part
    grad_in = scatter_over(grad_in, DATA).reshape(in_rows.shape)

    branch_grad, branch_gain_grad = norm_backward(
        branch, branch_factor, norm_gains[2], residual_grad
    )
    branch_grad_low = branch_grad.astype(bf16)
    attended_grad = product_right(branch_grad_low, out_full).astype(bf16)
    attended_grad = attended_grad.reshape(piece_len, line, 2, width).transpose(1, 2, 0, 3)
    keep, give = pick(attended_grad, core, 1), pick(attended_grad, 1 - core, 1)
    give, branch_grad_low = together(give, branch_grad_low)
    out_grad = product_left(attended_low, branch_grad_low).astype(bf16)
    out_grad = out_grad.reshape(-1, 2, out_weight.shape[0], D)
    got, out_grad, grad_in = together(swap(give), out_grad, grad_in)
    pieces = chips_start(by_core(keep, got), LINE)
    in_keep, in_got = cores_start(grad_in.reshape((line, 2) + in_rows.shape[2:]))
    out_got = swap(pick(out_grad, 1 - core, 1))
    pieces, in_got, out_got = together(pieces, in_got, out_got)
    head_grad = by_source(pieces, LINE).reshape(length, width)
    in_pieces = chips_start(by_core(in_keep, in_got), LINE)
    out_grad = join(out_grad, out_got)
    head_grad, out_grad = together(head_grad, out_grad)
    out_grad = scatter_over(out_grad.reshape(D // 2, D), DATA)
    out_grad = out_grad.reshape((line,) + out_weight.shape)

    query_grad, key_grad, value_grad = attend_back(
        lows, starts_row, query_low, key_low, value_low, head_out, log_total, head_grad
    )
    weighted, mixing, gain_grads = unturn(
        query_grad, key_grad, projected, factors, gains_here, cosine, sine_part
    )
    mixing, in_pieces, grad_down = together(mixing, in_pieces, grad_down)
    grad_down = scatter_over(grad_down, DATA)
    mixing = small_sum(mixing, CTX) / D
    projected_grad = finish(weighted, projected, factors, mixing, value_grad)
    out_steps = offsets(LINE)

    def out_pieces(turn):
        return [shift(pick(out_grad, place(LINE, steps)), LINE, steps) for steps in turn]

    projected_grad, near = together(projected_grad, out_pieces(out_steps[:-1]))
    grad_blocks = projected_grad.reshape(line, 2, piece_len, 3 * width)

    later = []

    def input_product(k):
        rows = pick(grad_blocks, row.served(k))
        rows = jnp.concatenate([pick(rows, core), pick(rows, 1 - core)], axis=0)
        return product_right(rows, qkv_here).astype(bf16)

    def input_chip(k):
        part = row.tied[0][2] if k == line - 4 else input_product(k)
        part = scatter_sum(part[:piece_len], part[piece_len:])
        if not later:
            later.extend(together(part, projected_grad))
            part = later[0]
        return part

    def step(rows, axis):
        if lax.axis_size(axis) == 2:
            return (rows, lax.ppermute(rows, axis, [(0, 1), (1, 0)]))
        return (lax.psum(rows, axis),)

    def last_grads(slot, tied):
        if slot == 1:
            grads = product_left(full_input, later[1]).astype(bf16)
            return (grads, gain_grads, input_product(line - 4), out_pieces(out_steps[-1:]))
        if slot == 2:
            rows = jnp.zeros((5, D), f32)
            rows = lax.dynamic_update_slice(rows, tied[0][1], (0, ctx_place * width))
            rows = rows.at[2].set(branch_gain_grad).at[3].set(second_gain_grad)
            rows = rows.at[4, :3].set(sums)
            return (scatter_over(tied[0][0], DATA), step(rows, "c"), grad_down)
        if slot == line - 1:
            blocks = tied[1][0].reshape(line, 2, row_count, 3 * width)
            return (cores_start(blocks), step(sum(tied[1][1]), "zl"), in_pieces, tied[1][2])
        return ()

    plan = [[line - 2, line - 3]] + [[k] for k in range(line - 4, -1, -1)] + [[]]
    input_part, tied = row.scatter(input_chip, last_grads, plan)
    qkv_cores, gain_rows, in_pieces, grad_down = tied[line - 2]
    qkv_pieces = chips_start(by_core(*qkv_cores), LINE)
    gain_rows, qkv_pieces = together(step(sum(gain_rows), "zh"), qkv_pieces)
    gain_rows = sum(gain_rows)
    if sizes_of(DATA) == (2, 2):
        sides = [shift(gain_rows, DATA, steps) for steps in offsets(DATA)]
        gain_rows = (sides[0] + sides[1]) + (sides[2] + sides[3])
    else:
        gain_rows = small_sum(gain_rows, ("dl", "dh"))
    input_grad = residual_grad + input_part
    grad_in = by_source(in_pieces, LINE)
    grad_in = collect(grad_in.reshape((owners,) + grad_in.shape[2:]), 2 * data_count)
    grad_down = grad_down.astype(f32)
    grad_out = sum(piece.astype(f32) for piece in near + tied[0][3])
    grad_qkv = by_source(qkv_pieces, LINE)
    grad_qkv = collect(grad_qkv.reshape(owners, row_count, 3 * width), 3)
    live_count = jnp.sum(seq_lengths).astype(f32)
    rms_values = jnp.sqrt(gain_rows[4, :3] / (live_count * model_width))
    return (
        result.astype(bf16)[None],
        input_grad[None],
        grad_qkv,
        grad_out,
        grad_in,
        grad_down,
        gain_rows[:4],
        rms_values,
    )


def solution(mesh):
    dp, ctx = mesh.shape["dp"], mesh.shape["ctx"]
    fine = Mesh(mesh.devices.reshape(2, dp // 2, 2, ctx // 4, 2), AXES)
    return jax.shard_map(
        on_device,
        mesh=fine,
        in_specs=(
            P(DATA, CTX, None),
            P(),
            P(AXES, None),
            P(AXES, None),
            P(AXES, None),
            P(AXES, None),
            P(),
            P(DATA, CTX, None),
        ),
        out_specs=(
            P(DATA, CTX, None),
            P(DATA, CTX, None),
            P(AXES, None),
            P(AXES, None),
            P(AXES, None),
            P(AXES, None),
            P(),
            P(),
        ),
        check_vma=False,
    )
```
